32 devices in a mesh: dp: 8 (over z, x), grp: 4 (over y, core).
Axes of the slice: x: 2, y: 2, z: 4, core: 2. Of those that a mesh axis runs over, the one named last changes fastest.
Arguments:
- down_in: bfloat16 [96, 32, 32, 160], P(('dp', 'grp')), may hold values from -6 to 6
- right_in: bfloat16 [96, 32, 32, 160], P(('dp', 'grp')), may hold values from -6 to 6
- pixel_mask: int32 [96, 32, 32], P(('dp', 'grp')), may hold values 0 or 1
- down_cot: bfloat16 [96, 32, 32, 160], P(('dp', 'grp')), may hold values from -6 to 6
- right_cot: bfloat16 [96, 32, 32, 160], P(('dp', 'grp')), may hold values from -6 to 6
- v_down1: bfloat16 [2, 1920, 160], P(None, 'dp'), may hold values from -0.125 to 0.125
- v_down2: bfloat16 [2, 1920, 320], P(None, 'dp'), may hold values from -0.125 to 0.125
- v_right1: bfloat16 [2, 1280, 160], P(None, 'dp'), may hold values from -0.15625 to 0.15625
- v_skip: bfloat16 [2, 320, 160], P(None, 'dp'), may hold values from -0.3125 to 0.3125
- v_right2: bfloat16 [2, 1280, 320], P(None, 'dp'), may hold values from -0.15625 to 0.15625
- gains: float32 [2, 1120], replicated, may hold values from 0.1 to 1.9
- biases: float32 [2, 1120], replicated, may hold values from -0.5 to 0.5
Outputs:
- down_out: bfloat16 [96, 32, 32, 160], P(('dp', 'grp'))
- right_out: bfloat16 [96, 32, 32, 160], P(('dp', 'grp'))
- down_grad: float32 [96, 32, 32, 160], P(('dp', 'grp'))
- right_grad: float32 [96, 32, 32, 160], P(('dp', 'grp'))
- grad_down1: float32 [2, 1920, 160], P(None, 'dp')
- grad_down2: float32 [2, 1920, 320], P(None, 'dp')
- grad_right1: float32 [2, 1280, 160], P(None, 'dp')
- grad_skip: float32 [2, 320, 160], P(None, 'dp')
- grad_right2: float32 [2, 1280, 320], P(None, 'dp')
- grad_gains: float32 [2, 1120], replicated
- grad_biases: float32 [2, 1120], replicated
The draws below stay inside these ranges and needn't reach their ends.
Inputs may be any that keep to these rules, and one draw needn't show every extreme that they name: `pixel_mask`: 1 marks a counted pixel, 0 one that is not.
All inputs are finite; a program needn't handle non-finite values. No bound on the sum of `pixel_mask` on one device may be relied on, other than what follows from the above.
Results may differ from the reference program's by a relative error of at most 0.015.
Values may be sent and summed in bfloat16 or wider, within the bound.
A program may use at most 256 MiB of HBM per device.

```python
import jax
import jax.numpy as jnp
from jax import lax

F = 160
SIDE = 32
LAYERS = 2
IMG_DEV = 3
IMAGES = 96


def place_ends(result, stream_key, low, high):
    place = [jax.random.randint(jax.random.fold_in(stream_key, axis), (), 0, length) for axis, length in enumerate(result.shape)]
    widest = result.shape.index(max(result.shape))
    neighbour = place[:widest] + [(place[widest] + 1) % result.shape[widest]] + place[widest + 1:]
    return result.at[tuple(place)].set(low).at[tuple(neighbour)].set(high)


def block_levels(own_key, dims, pieces, least, high):
    loudness, own = 1.0, jax.random.fold_in(own_key, 6)
    for axis_at, parts in pieces:
        steps = jnp.exp(jax.random.uniform(jax.random.fold_in(own, axis_at), (parts,), jnp.float32, least / len(pieces), high / len(pieces)))
        loudness = loudness * jnp.repeat(steps, dims[axis_at] // parts).reshape([-1 if axis == axis_at else 1 for axis in range(len(dims))])
    return loudness


def normal_values(key, shape, scale, most, cuts=(), dtype=jnp.bfloat16):
    array = scale * jax.random.normal(key, shape, jnp.float32)
    if cuts:
        array = array * block_levels(key, shape, cuts, -0.22, 0.18)
    return jnp.clip(array, -most, most).astype(dtype)


def setup_inputs(seed: int = 0) -> dict:
    keys = jax.random.split(jax.random.key(seed), 13)
    return {
        "down_in": normal_values(keys[0], (IMAGES, SIDE, SIDE, F), 1.0, 6.0, ((0, 32),)),
        "right_in": normal_values(keys[1], (IMAGES, SIDE, SIDE, F), 1.0, 6.0, ((0, 32),)),
        "pixel_mask": place_ends((jax.random.randint(keys[2], (IMAGES, SIDE, SIDE), 0, 4) < 3).astype(jnp.int32), jax.random.fold_in(keys[2], 1), 0, 1),
        "down_cot": normal_values(keys[3], (IMAGES, SIDE, SIDE, F), 1.0, 6.0, ((0, 32),)),
        "right_cot": normal_values(keys[4], (IMAGES, SIDE, SIDE, F), 1.0, 6.0, ((0, 32),)),
        "v_down1": normal_values(keys[5], (LAYERS, 12 * F, F), (12 * F) ** -0.5, 0.125, ((1, 8),)),
        "v_down2": normal_values(keys[6], (LAYERS, 12 * F, 2 * F), (12 * F) ** -0.5, 0.125, ((1, 8),)),
        "v_right1": normal_values(keys[7], (LAYERS, 8 * F, F), (8 * F) ** -0.5, 0.15625, ((1, 8),)),
        "v_skip": normal_values(keys[8], (LAYERS, 2 * F, F), (2 * F) ** -0.5, 0.3125, ((1, 8),)),
        "v_right2": normal_values(keys[9], (LAYERS, 8 * F, 2 * F), (8 * F) ** -0.5, 0.15625, ((1, 8),)),
        "gains": jnp.clip(1.0 + 0.18 * jax.random.normal(keys[10], (LAYERS, 7 * F), jnp.float32), 0.1, 1.9),
        "biases": jnp.clip(jax.random.uniform(keys[11], (LAYERS, 7 * F), jnp.float32, -0.5, 0.5), -0.5, 0.5),
    }


@jax.custom_vjp
def low(v):
    return lax.optimization_barrier(v.astype(jnp.bfloat16)).astype(jnp.float32)

@jax.custom_vjp
def low_back(v):
    return v

def low_keep(v):
    return (low(v), None)

def low_pass(kept, grad):
    return (grad,)

def back_keep(v):
    return (v, None)

def back_low(kept, grad):
    return (low(grad),)
low.defvjp(low_keep, low_pass)
low_back.defvjp(back_keep, back_low)
precise = lax.Precision.HIGHEST

def span_list(filters):
    return [(0, filters), (filters, 3 * filters), (3 * filters, 4 * filters), (4 * filters, 5 * filters), (5 * filters, 7 * filters)]

def taps_of(cells, stencil):
    height, breadth = (cells.shape[1], cells.shape[2])
    if stencil == 'down':
        padded = jnp.pad(cells, ((0, 0), (1, 0), (1, 1), (0, 0)))
        offsets = [(row_off, col_off) for row_off in range(2) for col_off in range(3)]
    else:
        padded = jnp.pad(cells, ((0, 0), (1, 0), (1, 0), (0, 0)))
        offsets = [(row_off, col_off) for row_off in range(2) for col_off in range(2)]
    return jnp.concatenate([padded[:, row_off:row_off + height, col_off:col_off + breadth, :] for row_off, col_off in offsets], axis=-1)

def conv(cells, weight, stencil):
    return jnp.einsum('bhwk,ko->bhwo', taps_of(cells, stencil), weight, precision=precise)

def pair_elu(values):
    return jax.nn.elu(jnp.concatenate([values, -values], axis=-1))

def normed(values, gain_row):
    return low(values * (gain_row * lax.rsqrt(lax.optimization_barrier(jnp.sum(values * values, axis=0))))[None, :])

def gate_apply(flow, gate):
    filters = flow.shape[-1]
    return flow + gate[..., :filters] * jax.nn.sigmoid(gate[..., filters:])

def forward(down_flow, right_flow, v_down1, v_down2, v_right1, v_skip, v_right2, gains, biases):
    filters = down_flow.shape[-1]
    spans = span_list(filters)
    directions = (v_down1, v_down2, v_right1, v_skip, v_right2)
    activated = low(pair_elu(down_flow))
    for layer_num in range(LAYERS):
        weights = [normed(full[layer_num], gains[layer_num, start_col:stop_col]) for full, (start_col, stop_col) in zip(directions, spans)]
        bias_parts = [biases[layer_num, start_col:stop_col] for start_col, stop_col in spans]
        hidden_down = low_back(conv(activated, weights[0], 'down') + bias_parts[0])
        gate_down = low_back(conv(low(pair_elu(hidden_down)), weights[1], 'down') + bias_parts[1])
        down_flow = gate_apply(down_flow, gate_down)
        activated = low(pair_elu(down_flow))
        skip_term = jnp.einsum('bhwk,ko->bhwo', activated, weights[3], precision=precise)
        hidden_right = low_back(conv(low(pair_elu(right_flow)), weights[2], 'right') + skip_term + bias_parts[2] + bias_parts[3])
        gate_right = low_back(conv(low(pair_elu(hidden_right)), weights[4], 'right') + bias_parts[4])
        right_flow = gate_apply(right_flow, gate_right)
    return (down_flow, right_flow)

def reference(down_in, right_in, pixel_mask, down_cot, right_cot, v_down1, v_down2, v_right1, v_skip, v_right2, gains, biases):
    weight_args = tuple((full.astype(jnp.float32) for full in (v_down1, v_down2, v_right1, v_skip, v_right2))) + (gains, biases)
    blocks = down_in.shape[0] // IMG_DEV
    mask_float = pixel_mask.astype(jnp.float32)[..., None]

    def to_blocks(values):
        return values.reshape((blocks, IMG_DEV) + values.shape[1:])
    items = (to_blocks(down_in.astype(jnp.float32)), to_blocks(right_in.astype(jnp.float32)), to_blocks(down_cot.astype(jnp.float32) * mask_float), to_blocks(right_cot.astype(jnp.float32) * mask_float))

    def one_block(totals, item):
        down_part, right_part, down_seed, right_seed = item
        outputs, pullback = jax.vjp(forward, down_part, right_part, *weight_args)
        grads = pullback((down_seed, right_seed))
        totals = tuple((total_now + grad_now for total_now, grad_now in zip(totals, grads[2:])))
        return (totals, (outputs[0].astype(jnp.bfloat16), outputs[1].astype(jnp.bfloat16), grads[0], grads[1]))
    init = tuple((jnp.zeros_like(weight_now) for weight_now in weight_args))
    totals, results = lax.scan(one_block, init, items)

    def from_blocks(values):
        return values.reshape((blocks * IMG_DEV,) + values.shape[2:])
    down_out, right_out, down_grad, right_grad = (from_blocks(values) for values in results)
    return (down_out, right_out, down_grad, right_grad, totals[0], totals[1], totals[2], totals[3], totals[4], totals[5], totals[6])
```

```python
import functools
import jax
import jax.numpy as jnp
from jax import lax
from jax.experimental import pallas as pl
from jax.experimental.pallas import tpu as pltpu
from jax.sharding import PartitionSpec as P

BF = jnp.bfloat16
F32 = jnp.float32
LAYERS = 2
C = 160
C2 = 320
SPANS = ((0, 160), (160, 480), (480, 640), (640, 800), (800, 1120))


def nt(a, b):
    return lax.dot_general(a, b, (((1,), (1,)), ((), ())), preferred_element_type=F32)


def nn(a, b):
    return lax.dot_general(a, b, (((1,), (0,)), ((), ())), preferred_element_type=F32)


def eye(n):
    same = lax.broadcasted_iota(jnp.int32, (n, n), 0) == lax.broadcasted_iota(jnp.int32, (n, n), 1)
    return jnp.where(same, 1.0, 0.0).astype(BF)


def lane():
    return lax.broadcasted_iota(jnp.int32, (1, 128), 1)


def keep(cond, tile):
    return jnp.where(cond, tile, jnp.zeros((), tile.dtype))


def col_shift(tile, off):
    if off == 0:
        return tile
    col = lane() & 31
    if off == 1:
        return keep(col != 31, pltpu.roll(tile, 127, 1))
    return keep(col != 0, pltpu.roll(tile, 1, 1))


def row_before(tile):
    return keep(lane() >= 32, pltpu.roll(tile, 32, 1))


def row_after(tile):
    return keep(lane() < 96, pltpu.roll(tile, 96, 1))


def at(v):
    return slice(v * 128, (v + 1) * 128)


def put_down(ext, v, tile):
    n = tile.shape[0]
    for c in range(3):
        moved = col_shift(tile, c - 1)
        ext[c * n : (c + 1) * n, at(v + 1)] = moved
        if v == 7:
            ext[c * n : (c + 1) * n, at(0)] = row_before(moved)


def put_right(ext, v, tile):
    n = tile.shape[0]
    for c in range(2):
        moved = col_shift(tile, c - 1)
        ext[(2 + c) * n : (3 + c) * n, at(v)] = moved
        if v == 7:
            ext[c * n : (c + 1) * n, at(0)] = row_before(moved)
        else:
            ext[c * n : (c + 1) * n, at(v + 1)] = moved


def put_down_back(ext, v, tile):
    n = tile.shape[0]
    for c in range(3):
        moved = col_shift(tile, 1 - c)
        ext[c * n : (c + 1) * n, at(v)] = moved
        if v == 0:
            ext[c * n : (c + 1) * n, at(8)] = row_after(moved)


def put_right_back(ext, v, tile):
    n = tile.shape[0]
    for c in range(2):
        moved = col_shift(tile, 1 - c)
        ext[(2 + c) * n : (3 + c) * n, at(v)] = moved
        if v == 0:
            ext[c * n : (c + 1) * n, at(7)] = row_after(moved)
        else:
            ext[c * n : (c + 1) * n, at(v - 1)] = moved


def pair_elu(x):
    e = jnp.exp(-jnp.abs(x)) - 1.0
    up = x > 0
    return jnp.concatenate([jnp.where(up, x, e), jnp.where(up, e, -x)], axis=0).astype(BF)


def elu_back(grad, act):
    slope = jnp.minimum(act.astype(F32), 0.0) + 1.0
    both = grad * slope
    return both[:C] - both[C:]


def sigmoid(x):
    return 1.0 / (1.0 + jnp.exp(-x))


def load_cells(ref, v):
    rows = jnp.concatenate([ref[g * 8 + v] for g in range(4)], axis=0)
    return nt(eye(C), rows)


def store_bf16(ref, v, tile):
    out = nt(eye(128), tile.astype(BF)).astype(BF)
    for g in range(4):
        ref[g * 8 + v] = out[g * 32 : (g + 1) * 32]


def store_f32(ref, v, tile):
    out = tile.T
    for g in range(4):
        ref[g * 8 + v] = out[g * 32 : (g + 1) * 32]


def scale_of(total, gain):
    return gain * lax.rsqrt(total)


def transpose_weight(v_ref, first, rows, width, dest):
    unit = eye(width)
    part = 320
    for k in range(rows // part):
        block = v_ref[first + k * part : first + (k + 1) * part, :]
        dest[:, k * part : (k + 1) * part] = nt(unit, block).astype(BF)


def square_sum(ref):
    vals = ref[...].astype(F32)
    return jnp.sum(vals * vals, axis=1, keepdims=True)


def fwd_kernel(
    down_in, right_in, v1, v2, r1, vs, r2, cols,
    down_out, right_out, cells, actd, actr, acth, gated, gater, kappa,
    w1, w2, wr1, ws, wr2, ext, ext4, dflow, rflow,
):
    @pl.when(pl.program_id(0) == 0)
    def _():
        for l in range(LAYERS):
            for a in range(2):
                transpose_weight(v1.at[l], a * 960, 960, 160, w1.at[l, a])
                transpose_weight(v2.at[l], a * 960, 960, 320, w2.at[l, a])
            transpose_weight(r1.at[l], 0, 1280, 160, wr1.at[l])
            transpose_weight(vs.at[l], 0, 320, 160, ws.at[l])
            transpose_weight(r2.at[l], 0, 1280, 320, wr2.at[l])
            totals = (
                square_sum(w1.at[l, 0]) + square_sum(w1.at[l, 1]),
                square_sum(w2.at[l, 0]) + square_sum(w2.at[l, 1]),
                square_sum(wr1.at[l]),
                square_sum(ws.at[l]),
                square_sum(wr2.at[l]),
            )
            for total, (lo, hi) in zip(totals, SPANS):
                kappa[lo:hi, l : l + 1] = scale_of(total, cols[lo:hi, l : l + 1])

    for v in range(8):
        x = load_cells(down_in.at[0], v)
        dflow[:, at(v)] = x
        act = pair_elu(x)
        cells[0, 0, :, at(v)] = act
        put_down(ext, v, act)
        rflow[:, at(v)] = load_cells(right_in.at[0], v)
    for l in range(LAYERS):
        def scale(m):
            lo, hi = SPANS[m]
            return kappa[lo:hi, l : l + 1]

        def bias(m):
            lo, hi = SPANS[m]
            return cols[lo:hi, 2 + l : 3 + l]

        for j in range(4):
            acc = nn(w1[l, 0], ext[:, j * 256 : j * 256 + 256])
            acc = acc + nn(w1[l, 1], ext[:, j * 256 + 128 : j * 256 + 384])
            for h in range(2):
                v = 2 * j + h
                actd[0, l, :, at(v)] = pair_elu(acc[:, at(h)] * scale(0) + bias(0))
        for v in range(8):
            put_down(ext, v, actd[0, l, :, at(v)])
            act = pair_elu(rflow[:, at(v)])
            actr[0, l, :, at(v)] = act
            put_right(ext4, v, act)
        for j in range(4):
            acc = nn(w2[l, 0], ext[:, j * 256 : j * 256 + 256])
            acc = acc + nn(w2[l, 1], ext[:, j * 256 + 128 : j * 256 + 384])
            for h in range(2):
                v = 2 * j + h
                gate = acc[:, at(h)] * scale(1) + bias(1)
                t = gate[:C]
                s = sigmoid(gate[C:])
                gated[0, l, :C, at(v)] = t.astype(BF)
                gated[0, l, C:, at(v)] = s.astype(BF)
                new = dflow[:, at(v)] + t * s
                dflow[:, at(v)] = new
                cells[0, l + 1, :, at(v)] = pair_elu(new)
        skip_bias = bias(2) + bias(3)
        for j in range(4):
            acc = nn(wr1[l], ext4[:, j * 256 : j * 256 + 256]) * scale(2)
            acc = acc + nn(ws[l], cells[0, l + 1, :, j * 256 : j * 256 + 256]) * scale(3)
            for h in range(2):
                v = 2 * j + h
                acth[0, l, :, at(v)] = pair_elu(acc[:, at(h)] + skip_bias)
        for v in range(8):
            put_right(ext4, v, acth[0, l, :, at(v)])
            if l + 1 < LAYERS:
                put_down(ext, v, cells[0, l + 1, :, at(v)])
        for j in range(4):
            acc = nn(wr2[l], ext4[:, j * 256 : j * 256 + 256])
            for h in range(2):
                v = 2 * j + h
                gate = acc[:, at(h)] * scale(4) + bias(4)
                t = gate[:C]
                s = sigmoid(gate[C:])
                gater[0, l, :C, at(v)] = t.astype(BF)
                gater[0, l, C:, at(v)] = s.astype(BF)
                rflow[:, at(v)] = rflow[:, at(v)] + t * s
    for v in range(8):
        store_bf16(down_out.at[0], v, dflow[:, at(v)])
        store_bf16(right_out.at[0], v, rflow[:, at(v)])


def taps_beside(v_ref, first, count, dest):
    n = v_ref.shape[1]
    for k in range(count):
        dest[:, k * n : (k + 1) * n] = v_ref[first + k * C2 : first + (k + 1) * C2, :]


def gate_back(g, t, s):
    p = g * s
    q = p * t * (1.0 - s)
    return jnp.concatenate([p, q], axis=0)


def bwd_kernel(
    top, down_g, right_g, mask, *refs,
):
    refs = list(refs)
    cells_g = None if top else refs.pop(0)
    (
        low_cells, high_cells, actd, actr, acth, gated, gater, kappa, v1, v2, r1, vs, r2,
    ) = refs[:13]
    refs = refs[13:]
    if top:
        down_out, right_out, cells_out = refs[:3]
        refs = refs[3:]
    else:
        down_out, right_out = refs[:2]
        refs = refs[2:]
    (
        o1, o2, or1, os, or2, obias,
        b1, b2, br1, br2, g1, g2, gr1, gs, gr2, bsum, ext, ext1, ext4, ext41, dskip, gdown, gright,
    ) = refs
    layer = 1 if top else 0
    step = pl.program_id(0)

    @pl.when(step == 0)
    def _():
        for a in range(2):
            taps_beside(v1.at[0], a * 960, 3, b1.at[a])
            taps_beside(v2.at[0], a * 960, 3, b2.at[a])
        taps_beside(r1.at[0], 0, 4, br1)
        taps_beside(r2.at[0], 0, 4, br2)
        for acc in (g1, g2, gr1, gs, gr2, bsum):
            acc[...] = jnp.zeros(acc.shape, F32)

    def scale(m):
        lo, hi = SPANS[m]
        return kappa[lo:hi, layer : layer + 1]

    def add_bias(m, total):
        lo, hi = SPANS[m]
        bsum[lo:hi, :] += total

    total = None
    for v in range(8):
        if top:
            m = mask[0, :, at(v)]
            gdown[:, at(v)] = load_cells(down_g.at[0], v) * m
            g = load_cells(right_g.at[0], v) * m
            gright[:, at(v)] = g
        else:
            g = right_g[0, :, at(v)]
        d = gate_back(g, gater[0, 0, :C, at(v)].astype(F32), gater[0, 0, C:, at(v)].astype(F32))
        total = d if total is None else total + d
        put_right_back(ext4, v, (d * scale(4)).astype(BF))
    add_bias(4, total)
    gr2[...] += nt(acth[0, 0], ext4[...])
    total = None
    for j in range(4):
        e = nn(br2[...], ext4[:, j * 256 : j * 256 + 256])
        for h in range(2):
            v = 2 * j + h
            d = elu_back(e[:, at(h)], acth[0, 0, :, at(v)])
            total = d if total is None else total + d
            put_right_back(ext41, v, (d * scale(2)).astype(BF))
            dskip[:, at(v)] = (d * scale(3)).astype(BF)
    add_bias(2, total)
    add_bias(3, total)
    gr1[...] += nt(actr[0, 0], ext41[...])
    gs[...] += nt(high_cells[0, 0], dskip[...])
    for j in range(4):
        e = nn(br1[...], ext41[:, j * 256 : j * 256 + 256])
        k = nn(vs[0], dskip[:, j * 256 : j * 256 + 256])
        for h in range(2):
            v = 2 * j + h
            old = gright[:, at(v)] if top else right_g[0, :, at(v)]
            new = old + elu_back(e[:, at(h)], actr[0, 0, :, at(v)])
            if top:
                right_out[0, :, at(v)] = new
            else:
                store_f32(right_out.at[0], v, new)
            gc = k[:, at(h)]
            if not top:
                gc = gc + cells_g[0, :, at(v)]
            old = gdown[:, at(v)] if top else down_g[0, :, at(v)]
            gdown[:, at(v)] = old + elu_back(gc, high_cells[0, 0, :, at(v)])
    total = None
    for v in range(8):
        g = gdown[:, at(v)]
        if top:
            down_out[0, :, at(v)] = g
        d = gate_back(g, gated[0, 0, :C, at(v)].astype(F32), gated[0, 0, C:, at(v)].astype(F32))
        total = d if total is None else total + d
        put_down_back(ext, v, (d * scale(1)).astype(BF))
    add_bias(1, total)
    for a in range(2):
        lo = 128 * (1 - a)
        g2[a] += nt(actd[0, 0], ext[:, lo : lo + 1024])
    total = None
    for j in range(4):
        e = nn(b2[1], ext[:, j * 256 : j * 256 + 256])
        e = e + nn(b2[0], ext[:, j * 256 + 128 : j * 256 + 384])
        for h in range(2):
            v = 2 * j + h
            d = elu_back(e[:, at(h)], actd[0, 0, :, at(v)])
            total = d if total is None else total + d
            put_down_back(ext1, v, (d * scale(0)).astype(BF))
    add_bias(0, total)
    for a in range(2):
        lo = 128 * (1 - a)
        g1[a] += nt(low_cells[0, 0], ext1[:, lo : lo + 1024])
    for j in range(4):
        e = nn(b1[1], ext1[:, j * 256 : j * 256 + 256])
        e = e + nn(b1[0], ext1[:, j * 256 + 128 : j * 256 + 384])
        if top:
            cells_out[0, :, j * 256 : j * 256 + 256] = e
        else:
            for h in range(2):
                v = 2 * j + h
                last = gdown[:, at(v)] + elu_back(e[:, at(h)], low_cells[0, 0, :, at(v)])
                store_f32(down_out.at[0], v, last)

    @pl.when(step == pl.num_programs(0) - 1)
    def _():
        for a in range(2):
            for c in range(3):
                row = (a * 3 + c) * C2
                o1[row : row + C2, :] = g1[a, :, c * C : (c + 1) * C].astype(BF)
                o2[row : row + C2, :] = g2[a, :, c * C2 : (c + 1) * C2].astype(BF)
        for t in range(4):
            or1[t * C2 : (t + 1) * C2, :] = gr1[:, t * C : (t + 1) * C].astype(BF)
            or2[t * C2 : (t + 1) * C2, :] = gr2[:, t * C2 : (t + 1) * C2].astype(BF)
        os[...] = gs[...].astype(BF)
        obias[...] = jnp.sum(bsum[...], axis=1, keepdims=True)


def whole(shape, dtype=None):
    zeros = (0,) * len(shape)
    return pl.BlockSpec(shape, lambda i: zeros)


def once(shape):
    zeros = (0,) * len(shape)
    return pl.BlockSpec(shape, lambda i: zeros, pipeline_mode=pl.Buffered(1))


def image(shape):
    rest = (0,) * (len(shape) - 1)
    return pl.BlockSpec(shape, lambda i: (i,) + rest)


def run_forward(down_in, right_in, whole_v, cols):
    n = down_in.shape[0]
    sds = jax.ShapeDtypeStruct
    px = 1024
    kept = [(3, C2, px)] + [(LAYERS, C2, px)] * 5
    return pl.pallas_call(
        fwd_kernel,
        grid=(n,),
        in_specs=[image((1, 32, 32, C))] * 2 + [once(v.shape) for v in whole_v] + [once((1120, 4))],
        out_specs=[image((1, 32, 32, C))] * 2 + [image((1,) + s) for s in kept] + [whole((1120, 2))],
        out_shape=[sds((n, 32, 32, C), BF)] * 2 + [sds((n,) + s, BF) for s in kept] + [sds((1120, 2), F32)],
        scratch_shapes=[
            pltpu.VMEM((LAYERS, 2, 160, 960), BF),
            pltpu.VMEM((LAYERS, 2, 320, 960), BF),
            pltpu.VMEM((LAYERS, 160, 1280), BF),
            pltpu.VMEM((LAYERS, 160, 320), BF),
            pltpu.VMEM((LAYERS, 320, 1280), BF),
            pltpu.VMEM((960, 1152), BF),
            pltpu.VMEM((1280, 1024), BF),
            pltpu.VMEM((C, px), F32),
            pltpu.VMEM((C, px), F32),
        ],
        compiler_params=pltpu.CompilerParams(vmem_limit_bytes=60 << 20),
        name="forward",
    )(down_in, right_in, *whole_v, cols)


def run_backward(layer, down_g, right_g, cells_g, mask, kept, kappa, whole_v):
    n = down_g.shape[0]
    top = layer == 1
    sds = jax.ShapeDtypeStruct
    px = 1024
    shapes = [(1920, 160), (1920, 320), (1280, 160), (320, 160), (1280, 320)]
    flow = image((1, C, px))
    wide = image((1, C2, px))

    def pick(which):
        return pl.BlockSpec((1, 1, C2, px), lambda i: (i, which, 0, 0))

    def one_layer(shape):
        return pl.BlockSpec((1,) + shape, lambda i: (layer, 0, 0), pipeline_mode=pl.Buffered(1))

    cells = kept[0]
    ins = [down_g, right_g, mask] + ([] if top else [cells_g]) + [cells, cells] + list(kept[1:]) + [kappa] + list(whole_v)
    photo = image((1, 32, 32, C))
    in_specs = (
        ([photo] * 2 if top else [flow] * 2)
        + [image((1, 1, px))]
        + ([] if top else [wide])
        + [pick(layer), pick(layer + 1)]
        + [pick(layer)] * 5
        + [once((1120, 2))]
        + [one_layer(s) for s in shapes]
    )
    if top:
        out_specs = [flow, flow, wide]
        out_shape = [sds((n, C, px), F32)] * 2 + [sds((n, C2, px), F32)]
    else:
        out_specs = [photo] * 2
        out_shape = [sds((n, 32, 32, C), F32)] * 2
    return pl.pallas_call(
        functools.partial(bwd_kernel, top),
        grid=(n,),
        in_specs=in_specs,
        out_specs=out_specs + [once(s) for s in shapes] + [once((1120, 1))],
        out_shape=out_shape + [sds(s, BF) for s in shapes] + [sds((1120, 1), F32)],
        scratch_shapes=[
            pltpu.VMEM((2, 320, 480), BF),
            pltpu.VMEM((2, 320, 960), BF),
            pltpu.VMEM((320, 640), BF),
            pltpu.VMEM((320, 1280), BF),
            pltpu.VMEM((2, 320, 480), F32),
            pltpu.VMEM((2, 320, 960), F32),
            pltpu.VMEM((320, 640), F32),
            pltpu.VMEM((320, 160), F32),
            pltpu.VMEM((320, 1280), F32),
            pltpu.VMEM((1120, 128), F32),
            pltpu.VMEM((960, 1152), BF),
            pltpu.VMEM((480, 1152), BF),
            pltpu.VMEM((1280, 1024), BF),
            pltpu.VMEM((640, 1024), BF),
            pltpu.VMEM((160, 1024), BF),
            pltpu.VMEM((C, px), F32),
            pltpu.VMEM((C, px), F32),
        ],
        compiler_params=pltpu.CompilerParams(vmem_limit_bytes=60 << 20),
        name="backward%d" % layer,
    )(*ins)


def on_device(
    down_in,
    right_in,
    pixel_mask,
    down_cot,
    right_cot,
    v_down1,
    v_down2,
    v_right1,
    v_skip,
    v_right2,
    gains,
    biases,
):
    shards = (v_down1, v_down2, v_right1, v_skip, v_right2)
    whole_v = tuple(lax.all_gather(v, "dp", axis=1, tiled=True) for v in shards)
    cols = jnp.concatenate([gains, biases], axis=0).T
    n = down_in.shape[0]
    down_out, right_out, *kept, kappa = run_forward(down_in, right_in, whole_v, cols)
    mask = pixel_mask.reshape(n, 4, 8, 32).transpose(0, 2, 1, 3).reshape(n, 1, 1024).astype(F32)
    down_g, right_g, cells_g, *upper = run_backward(1, down_cot, right_cot, None, mask, kept, kappa, whole_v)
    down_grad, right_grad, *lower = run_backward(0, down_g, right_g, cells_g, mask, kept, kappa, whole_v)
    bias_sum = lax.psum(jnp.stack([lower[5][:, 0], upper[5][:, 0]]), ("dp", "grp"))
    sums = []
    for m in range(5):
        both = jnp.stack([lower[m], upper[m]])
        part = lax.psum_scatter(both, "dp", scatter_dimension=1, tiled=True)
        sums.append(lax.psum(part, "grp").astype(F32))
    units = []
    inverse = []
    for m in range(5):
        vals = whole_v[m].astype(F32)
        inv = lax.rsqrt(jnp.sum(vals * vals, axis=1))
        inverse.append(inv)
        units.append(shards[m].astype(F32) * inv[:, None, :])
    dots = jnp.concatenate([jnp.sum(units[m] * sums[m], axis=1) for m in range(5)], axis=1)
    dots = lax.psum(dots, "dp")
    grads = [
        sums[m] - units[m] * dots[:, None, lo:hi] for m, (lo, hi) in enumerate(SPANS)
    ]
    grad_gains = dots / (gains * jnp.concatenate(inverse, axis=1))
    return (down_out, right_out, down_grad, right_grad, *grads, grad_gains, bias_sum)


def solution(mesh):
    photo = P(("dp", "grp"), None, None, None)
    rows = P(None, "dp", None)
    return jax.shard_map(
        on_device,
        mesh=mesh,
        in_specs=(photo, photo, P(("dp", "grp"), None, None), photo, photo) + (rows,) * 5 + (P(), P()),
        out_specs=(photo,) * 4 + (rows,) * 5 + (P(), P()),
        check_vma=False,
    )
```

```python
import functools
import jax
import jax.numpy as jnp
from jax import lax
from jax.experimental import pallas as pl
from jax.experimental.pallas import tpu as pltpu
from jax.sharding import PartitionSpec as P

BF = jnp.bfloat16
F32 = jnp.float32
LAYERS = 2
HI = 4
MESH = pl.DeviceIdType.MESH
C = 160
C2 = 320
SPANS = ((0, 160), (160, 480), (480, 640), (640, 800), (800, 1120))


def nt(a, b):
    return lax.dot_general(a, b, (((1,), (1,)), ((), ())), preferred_element_type=F32)


def nn(a, b):
    return lax.dot_general(a, b, (((1,), (0,)), ((), ())), preferred_element_type=F32)


def eye(n):
    same = lax.broadcasted_iota(jnp.int32, (n, n), 0) == lax.broadcasted_iota(jnp.int32, (n, n), 1)
    return jnp.where(same, 1.0, 0.0).astype(BF)


def lane():
    return lax.broadcasted_iota(jnp.int32, (1, 128), 1)


def keep(cond, tile):
    return jnp.where(cond, tile, jnp.zeros((), tile.dtype))


def col_shift(tile, off):
    if off == 0:
        return tile
    col = lane() & 31
    if off == 1:
        return keep(col != 31, pltpu.roll(tile, 127, 1))
    return keep(col != 0, pltpu.roll(tile, 1, 1))


def row_before(tile):
    return keep(lane() >= 32, pltpu.roll(tile, 32, 1))


def row_after(tile):
    return keep(lane() < 96, pltpu.roll(tile, 96, 1))


def at(v):
    return slice(v * 128, (v + 1) * 128)


def put_down(ext, v, tile):
    n = tile.shape[0]
    for c in range(3):
        moved = col_shift(tile, c - 1)
        ext[c * n : (c + 1) * n, at(v + 1)] = moved
        if v == 7:
            ext[c * n : (c + 1) * n, at(0)] = row_before(moved)


def put_right(ext, v, tile):
    n = tile.shape[0]
    for c in range(2):
        moved = col_shift(tile, c - 1)
        ext[(2 + c) * n : (3 + c) * n, at(v)] = moved
        if v == 7:
            ext[c * n : (c + 1) * n, at(0)] = row_before(moved)
        else:
            ext[c * n : (c + 1) * n, at(v + 1)] = moved


def put_down_back(ext, v, tile):
    n = tile.shape[0]
    for c in range(3):
        moved = col_shift(tile, 1 - c)
        ext[c * n : (c + 1) * n, at(v)] = moved
        if v == 0:
            ext[c * n : (c + 1) * n, at(8)] = row_after(moved)


def put_right_back(ext, v, tile):
    n = tile.shape[0]
    for c in range(2):
        moved = col_shift(tile, 1 - c)
        ext[(2 + c) * n : (3 + c) * n, at(v)] = moved
        if v == 0:
            ext[c * n : (c + 1) * n, at(7)] = row_after(moved)
        else:
            ext[c * n : (c + 1) * n, at(v - 1)] = moved


def pair_elu(x):
    e = jnp.exp(-jnp.abs(x)) - 1.0
    up = x > 0
    return jnp.concatenate([jnp.where(up, x, e), jnp.where(up, e, -x)], axis=0).astype(BF)


def elu_back(grad, act):
    slope = jnp.minimum(act.astype(F32), 0.0) + 1.0
    both = grad * slope
    return both[:C] - both[C:]


def sigmoid(x):
    return 1.0 / (1.0 + jnp.exp(-x))


def load_cells(ref, v):
    rows = jnp.concatenate([ref[g * 8 + v] for g in range(4)], axis=0)
    return nt(eye(C), rows)


def store_bf16(ref, v, tile):
    out = nt(eye(128), tile.astype(BF)).astype(BF)
    for g in range(4):
        ref[g * 8 + v] = out[g * 32 : (g + 1) * 32]


def store_f32(ref, v, tile):
    out = tile.T
    for g in range(4):
        ref[g * 8 + v] = out[g * 32 : (g + 1) * 32]


def scale_of(total, gain):
    return gain * lax.rsqrt(total)


def square_sum(vals):
    vals = vals.astype(F32)
    return jnp.sum(vals * vals, axis=1, keepdims=True)


def down_product(weight, first, count, ext, j):
    acc = None
    for k in range(8):
        lo = j * 256 + 128 * (k // 4)
        part = nn(weight[k, first : first + count, :240], ext[240 * (k % 4) : 240 * (k % 4) + 240, lo : lo + 256])
        acc = part if acc is None else acc + part
    return acc


def fwd_kernel(
    down_in, right_in, wd, wr, wk, cols,
    down_out, right_out, cells, actd, actr, acth, gated, gater, kappa,
    right_t, skip_t, ext, ext4, dflow, rflow,
):
    @pl.when(pl.program_id(0) == 0)
    def _():
        for l in range(LAYERS):
            for k in range(4):
                rows = wr[l, k * C2 : (k + 1) * C2, :480]
                right_t[l, :, k * C2 : (k + 1) * C2] = nt(eye(480), rows).astype(BF)
            skip_t[l] = nt(eye(C), wk[l]).astype(BF)
            down_total = sum(square_sum(wd[l, k, :, :240]) for k in range(8))
            right_total = square_sum(right_t[l])
            totals = (down_total[C2:], down_total[:C2], right_total[C2:], square_sum(skip_t[l]), right_total[:C2])
            for total, (lo, hi) in zip(totals, SPANS):
                kappa[lo:hi, l : l + 1] = scale_of(total, cols[lo:hi, l : l + 1])

    for v in range(8):
        x = load_cells(down_in.at[0], v)
        dflow[:, at(v)] = x
        act = pair_elu(x)
        cells[0, 0, :, at(v)] = act
        put_down(ext, v, act)
        rflow[:, at(v)] = load_cells(right_in.at[0], v)
    for l in range(LAYERS):
        def scale(m):
            lo, hi = SPANS[m]
            return kappa[lo:hi, l : l + 1]

        def bias(m):
            lo, hi = SPANS[m]
            return cols[lo:hi, 2 + l : 3 + l]

        for j in range(4):
            acc = down_product(wd.at[l], C2, C, ext, j)
            for h in range(2):
                v = 2 * j + h
                actd[0, l, :, at(v)] = pair_elu(acc[:, at(h)] * scale(0) + bias(0))
        for v in range(8):
            put_down(ext, v, actd[0, l, :, at(v)])
            act = pair_elu(rflow[:, at(v)])
            actr[0, l, :, at(v)] = act
            put_right(ext4, v, act)
        for j in range(4):
            acc = down_product(wd.at[l], 0, C2, ext, j)
            for h in range(2):
                v = 2 * j + h
                gate = acc[:, at(h)] * scale(1) + bias(1)
                t = gate[:C]
                s = sigmoid(gate[C:])
                gated[0, l, :C, at(v)] = t.astype(BF)
                gated[0, l, C:, at(v)] = s.astype(BF)
                new = dflow[:, at(v)] + t * s
                dflow[:, at(v)] = new
                cells[0, l + 1, :, at(v)] = pair_elu(new)
        skip_bias = bias(2) + bias(3)
        for j in range(4):
            acc = nn(right_t[l, C2:], ext4[:, j * 256 : j * 256 + 256]) * scale(2)
            acc = acc + nn(skip_t[l], cells[0, l + 1, :, j * 256 : j * 256 + 256]) * scale(3)
            for h in range(2):
                v = 2 * j + h
                acth[0, l, :, at(v)] = pair_elu(acc[:, at(h)] + skip_bias)
        for v in range(8):
            put_right(ext4, v, acth[0, l, :, at(v)])
            if l + 1 < LAYERS:
                put_down(ext, v, cells[0, l + 1, :, at(v)])
        for j in range(4):
            acc = nn(right_t[l, :C2], ext4[:, j * 256 : j * 256 + 256])
            for h in range(2):
                v = 2 * j + h
                gate = acc[:, at(h)] * scale(4) + bias(4)
                t = gate[:C]
                s = sigmoid(gate[C:])
                gater[0, l, :C, at(v)] = t.astype(BF)
                gater[0, l, C:, at(v)] = s.astype(BF)
                rflow[:, at(v)] = rflow[:, at(v)] + t * s
    for v in range(8):
        store_bf16(down_out.at[0], v, dflow[:, at(v)])
        store_bf16(right_out.at[0], v, rflow[:, at(v)])


def gate_back(g, t, s):
    p = g * s
    q = p * t * (1.0 - s)
    return jnp.concatenate([p, q], axis=0)


def bwd_kernel(
    top, down_g, right_g, mask, *refs,
):
    refs = list(refs)
    cells_g = None if top else refs.pop(0)
    (
        low_cells, high_cells, actd, actr, acth, gated, gater, kappa, wd, wr, wk,
    ) = refs[:11]
    refs = refs[11:]
    if top:
        down_out, right_out, cells_out = refs[:3]
        refs = refs[3:]
    else:
        down_out, right_out = refs[:2]
        refs = refs[2:]
    (
        od, orr, obias,
        b1, b2, br1, br2, g1, g2, gr1, gs, gr2, bsum, ext, ext1, ext4, ext41, dskip, gdown, gright,
    ) = refs
    layer = 1 if top else 0
    step = pl.program_id(0)

    @pl.when(step == 0)
    def _():
        for k in range(8):
            rows = nt(eye(240), wd[0, k, :, :240]).astype(BF)
            for p in range(3):
                tap, chan = divmod(240 * k + 80 * p, C2)
                a, c = divmod(tap, 3)
                b2[a, chan : chan + 80, c * C2 : (c + 1) * C2] = rows[80 * p : 80 * p + 80, :C2]
                b1[a, chan : chan + 80, c * C : (c + 1) * C] = rows[80 * p : 80 * p + 80, C2:]
        for t in range(4):
            rows = wr[0, t * C2 : (t + 1) * C2, :480]
            br2[:, t * C2 : (t + 1) * C2] = rows[:, :C2]
            br1[:, t * C : (t + 1) * C] = rows[:, C2:]
        for acc in (g1, g2, gr1, gs, gr2, bsum):
            acc[...] = jnp.zeros(acc.shape, F32)

    def scale(m):
        lo, hi = SPANS[m]
        return kappa[lo:hi, layer : layer + 1]

    def add_bias(m, total):
        lo, hi = SPANS[m]
        bsum[lo:hi, :] += total

    total = None
    for v in range(8):
        if top:
            m = mask[0, :, at(v)]
            gdown[:, at(v)] = load_cells(down_g.at[0], v) * m
            g = load_cells(right_g.at[0], v) * m
            gright[:, at(v)] = g
        else:
            g = right_g[0, :, at(v)]
        d = gate_back(g, gater[0, 0, :C, at(v)].astype(F32), gater[0, 0, C:, at(v)].astype(F32))
        total = d if total is None else total + d
        put_right_back(ext4, v, (d * scale(4)).astype(BF))
    add_bias(4, total)
    gr2[...] += nt(acth[0, 0], ext4[...])
    total = None
    for j in range(4):
        e = nn(br2[...], ext4[:, j * 256 : j * 256 + 256])
        for h in range(2):
            v = 2 * j + h
            d = elu_back(e[:, at(h)], acth[0, 0, :, at(v)])
            total = d if total is None else total + d
            put_right_back(ext41, v, (d * scale(2)).astype(BF))
            dskip[:, at(v)] = (d * scale(3)).astype(BF)
    add_bias(2, total)
    add_bias(3, total)
    gr1[...] += nt(actr[0, 0], ext41[...])
    gs[...] += nt(high_cells[0, 0], dskip[...])
    for j in range(4):
        e = nn(br1[...], ext41[:, j * 256 : j * 256 + 256])
        k = nn(wk[0], dskip[:, j * 256 : j * 256 + 256])
        for h in range(2):
            v = 2 * j + h
            old = gright[:, at(v)] if top else right_g[0, :, at(v)]
            new = old + elu_back(e[:, at(h)], actr[0, 0, :, at(v)])
            if top:
                right_out[0, :, at(v)] = new
            else:
                store_f32(right_out.at[0], v, new)
            gc = k[:, at(h)]
            if not top:
                gc = gc + cells_g[0, :, at(v)]
            old = gdown[:, at(v)] if top else down_g[0, :, at(v)]
            gdown[:, at(v)] = old + elu_back(gc, high_cells[0, 0, :, at(v)])
    total = None
    for v in range(8):
        g = gdown[:, at(v)]
        if top:
            down_out[0, :, at(v)] = g
        d = gate_back(g, gated[0, 0, :C, at(v)].astype(F32), gated[0, 0, C:, at(v)].astype(F32))
        total = d if total is None else total + d
        put_down_back(ext, v, (d * scale(1)).astype(BF))
    add_bias(1, total)
    for a in range(2):
        lo = 128 * (1 - a)
        g2[a] += nt(actd[0, 0], ext[:, lo : lo + 1024])
    total = None
    for j in range(4):
        e = nn(b2[1], ext[:, j * 256 : j * 256 + 256])
        e = e + nn(b2[0], ext[:, j * 256 + 128 : j * 256 + 384])
        for h in range(2):
            v = 2 * j + h
            d = elu_back(e[:, at(h)], actd[0, 0, :, at(v)])
            total = d if total is None else total + d
            put_down_back(ext1, v, (d * scale(0)).astype(BF))
    add_bias(0, total)
    for a in range(2):
        lo = 128 * (1 - a)
        g1[a] += nt(low_cells[0, 0], ext1[:, lo : lo + 1024])
    for j in range(4):
        e = nn(b1[1], ext1[:, j * 256 : j * 256 + 256])
        e = e + nn(b1[0], ext1[:, j * 256 + 128 : j * 256 + 384])
        if top:
            cells_out[0, :, j * 256 : j * 256 + 256] = e
        else:
            for h in range(2):
                v = 2 * j + h
                last = gdown[:, at(v)] + elu_back(e[:, at(h)], low_cells[0, 0, :, at(v)])
                store_f32(down_out.at[0], v, last)

    @pl.when(step == pl.num_programs(0) - 1)
    def _():
        def put(out, block, row, lanes, tile):
            high = out.shape[4]
            done = 0
            while done < tile.shape[0]:
                q, r = divmod(row + done, high)
                size = min(high - r, tile.shape[0] - done)
                out[q // 2, q % 2, block % 2, block // 2, r : r + size, lanes] = tile[done : done + size]
                done += size

        for k in range(8):
            for p in range(3):
                tap, chan = divmod(240 * k + 80 * p, C2)
                a, c = divmod(tap, 3)
                part = jnp.concatenate(
                    [g2[a, chan : chan + 80, c * C2 : (c + 1) * C2], g1[a, chan : chan + 80, c * C : (c + 1) * C]], axis=1
                )
                put(od, k, 80 * p, slice(0, 480), part.astype(BF))
        for k in range(8):
            t, half = divmod(k, 2)
            row = slice(half * C, (half + 1) * C)
            part = jnp.concatenate([gr2[row, t * C2 : (t + 1) * C2], gr1[row, t * C : (t + 1) * C]], axis=1)
            put(orr, k, 0, slice(0, 480), part.astype(BF))
            put(orr, k, C, slice(0, C), gs[40 * k : 40 * k + 40].astype(BF))
        obias[...] = jnp.sum(bsum[...].T, axis=0, keepdims=True)


def whole(shape, dtype=None):
    zeros = (0,) * len(shape)
    return pl.BlockSpec(shape, lambda i: zeros)


def once(shape):
    zeros = (0,) * len(shape)
    return pl.BlockSpec(shape, lambda i: zeros, pipeline_mode=pl.Buffered(1))


def image(shape):
    rest = (0,) * (len(shape) - 1)
    return pl.BlockSpec(shape, lambda i: (i,) + rest)


GD_SHAPE = (2, 2, 2, 4, 64, 512)
GR_SHAPE = (2, 2, 2, 4, 56, 512)
PX = 1024


def run_forward(down_in, right_in, wd, wr, wk, cols):
    n = down_in.shape[0]
    sds = jax.ShapeDtypeStruct
    kept = [(3, C2, PX)] + [(LAYERS, C2, PX)] * 5
    return pl.pallas_call(
        fwd_kernel,
        grid=(n,),
        in_specs=[image((1, 32, 32, C))] * 2 + [once(w.shape) for w in (wd, wr, wk)] + [once((1120, 4))],
        out_specs=[image((1, 32, 32, C))] * 2 + [image((1,) + s) for s in kept] + [once((1120, 2))],
        out_shape=[sds((n, 32, 32, C), BF)] * 2 + [sds((n,) + s, BF) for s in kept] + [sds((1120, 2), F32)],
        scratch_shapes=[
            pltpu.VMEM((LAYERS, 480, 1280), BF),
            pltpu.VMEM((LAYERS, C, C2), BF),
            pltpu.VMEM((960, 1152), BF),
            pltpu.VMEM((1280, PX), BF),
            pltpu.VMEM((C, PX), F32),
            pltpu.VMEM((C, PX), F32),
        ],
        compiler_params=pltpu.CompilerParams(vmem_limit_bytes=60 << 20),
        name="forward",
    )(down_in, right_in, wd, wr, wk, cols)


def run_backward(layer, down_g, right_g, cells_g, mask, kept, kappa, wd, wr, wk):
    n = down_g.shape[0]
    top = layer == 1
    sds = jax.ShapeDtypeStruct
    flow = image((1, C, PX))
    wide = image((1, C2, PX))

    def pick(which):
        return pl.BlockSpec((1, 1, C2, PX), lambda i: (i, which, 0, 0))

    def one_layer(shape):
        rest = (0,) * (len(shape) - 1)
        return pl.BlockSpec((1,) + shape[1:], lambda i: (layer,) + rest, pipeline_mode=pl.Buffered(1))

    cells = kept[0]
    ins = [down_g, right_g, mask] + ([] if top else [cells_g]) + [cells, cells] + list(kept[1:]) + [kappa, wd, wr, wk]
    photo = image((1, 32, 32, C))
    in_specs = (
        ([photo] * 2 if top else [flow] * 2)
        + [image((1, 1, PX))]
        + ([] if top else [wide])
        + [pick(layer), pick(layer + 1)]
        + [pick(layer)] * 5
        + [once((1120, 2))]
        + [one_layer(w.shape) for w in (wd, wr, wk)]
    )
    if top:
        out_specs = [flow, flow, wide]
        out_shape = [sds((n, C, PX), F32)] * 2 + [sds((n, C2, PX), F32)]
    else:
        out_specs = [photo] * 2
        out_shape = [sds((n, 32, 32, C), F32)] * 2
    return pl.pallas_call(
        functools.partial(bwd_kernel, top),
        grid=(n,),
        in_specs=in_specs,
        out_specs=out_specs + [once(GD_SHAPE), once(GR_SHAPE), once((1, 1120))],
        out_shape=out_shape + [sds(GD_SHAPE, BF), sds(GR_SHAPE, BF), sds((1, 1120), F32)],
        scratch_shapes=[
            pltpu.VMEM((2, 320, 480), BF),
            pltpu.VMEM((2, 320, 960), BF),
            pltpu.VMEM((320, 640), BF),
            pltpu.VMEM((320, 1280), BF),
            pltpu.VMEM((2, 320, 480), F32),
            pltpu.VMEM((2, 320, 960), F32),
            pltpu.VMEM((320, 640), F32),
            pltpu.VMEM((320, 160), F32),
            pltpu.VMEM((320, 1280), F32),
            pltpu.VMEM((1120, 128), F32),
            pltpu.VMEM((960, 1152), BF),
            pltpu.VMEM((480, 1152), BF),
            pltpu.VMEM((1280, 1024), BF),
            pltpu.VMEM((640, 1024), BF),
            pltpu.VMEM((160, 1024), BF),
            pltpu.VMEM((C, PX), F32),
            pltpu.VMEM((C, PX), F32),
        ],
        compiler_params=pltpu.CompilerParams(vmem_limit_bytes=60 << 20),
        name="backward%d" % layer,
    )(*ins)


def assemble(v1, v2, r1, vs, r2):
    rows = jnp.concatenate([v2, v1], axis=2).reshape(LAYERS, 8, 240, 480)
    wd = jnp.pad(rows.swapaxes(2, 3), ((0, 0), (0, 0), (0, 0), (0, 16)))
    wr = jnp.pad(jnp.concatenate([r2, r1], axis=2), ((0, 0), (0, 0), (0, 32)))
    return wd, wr, vs


def unpack(gd, gr):
    d = gd.transpose(3, 2, 0, 1, 4, 5).reshape(8, 256, 512)[:, :240].reshape(1920, 512)
    r = gr.transpose(3, 2, 0, 1, 4, 5).reshape(8, 224, 512)
    right = r[:, :160].reshape(1280, 512)
    skip = r[:, 160:200, :C].reshape(320, C)
    return d[:, C2:480], d[:, :C2], right[:, C2:480], skip, right[:, :C2]


def peers(hi_count):
    me = lax.axis_index("dp")
    grp = lax.axis_index("grp")
    hi, lo = me // 2, lax.rem(me, 2)
    y, core = grp // 2, lax.rem(grp, 2)
    return me, grp, hi, lo, y, core


def meet(me, grp, hi, lo, y, core, everyone):
    barrier = pltpu.get_barrier_semaphore()
    near = [((hi + k) % HI * 2 + lo, grp) for k in range(1, HI)]
    near += [(hi * 2 + 1 - lo, grp)]
    if everyone:
        near += [((hi + k) % HI * 2 + 1 - lo, grp) for k in range(1, HI)]
    near += [(me, (grp + k) % 4) for k in range(1, 4)]
    for device in near:
        pl.semaphore_signal(barrier, inc=1, device_id=device, device_id_type=MESH)
    pl.semaphore_wait(barrier, len(near))


def send(src, dst, sems, at_, device):
    return pltpu.make_async_remote_copy(
        src_ref=src,
        dst_ref=dst,
        send_sem=sems[0].at[at_],
        recv_sem=sems[1].at[at_],
        device_id=device,
        device_id_type=MESH,
    )


def gather_stage(stage, sems, first, buf, ids):
    me, grp, hi, lo, y, core = ids
    if stage == 0:
        mine = buf.at[core, y, lo, hi]
        return [
            send(mine, mine, sems, first + k - 1, (lax.rem(hi + k, HI) * 2 + lo, grp)) for k in range(1, HI)
        ]
    if stage == 1:
        part = buf.at[core, y, lo]
        return [send(part, part, sems, first + HI - 1, (hi * 2 + 1 - lo, grp))]
    if stage == 2:
        part = buf.at[core, y]
        return [send(part, part, sems, first + HI, (me, (1 - y) * 2 + core))]
    part = buf.at[core]
    return [send(part, part, sems, first + HI + 1, (me, y * 2 + 1 - core))]


def start_all(copies):
    for copy in copies:
        copy.start()


def wait_all(copies):
    for copy in copies:
        copy.wait()


def pack_own(l, v1, v2, r1, vs, r2, bufd, bufr, owned, ownrt, ids):
    me, grp, hi, lo, y, core = ids
    down = jnp.concatenate([v2[l], v1[l]], axis=0).astype(F32)
    down = jnp.concatenate([down, jnp.zeros((480, 16), F32)], axis=1)
    right = jnp.concatenate([r2[l], r1[l]], axis=1).astype(F32)
    right = jnp.concatenate([right, jnp.zeros((160, 32), F32)], axis=1)
    skip = jnp.concatenate([vs[l].astype(F32), jnp.zeros((40, 352), F32)], axis=1)
    right = jnp.concatenate([right, skip, jnp.zeros((24, 512), F32)], axis=0)
    for q in range(4):
        owned[l, q] = down[q * 120 : (q + 1) * 120].astype(BF)
        ownrt[l, q] = right[q * 56 : (q + 1) * 56].astype(BF)
    bufd[l, core, y, lo, hi] = owned[l, core * 2 + y]
    bufr[l, core, y, lo, hi] = ownrt[l, core * 2 + y]


def unpack_down(l, bufd, wd):
    for k in range(8):
        for q in range(4):
            wd[l, k, q * 120 : (q + 1) * 120, :] = bufd[l, q // 2, q % 2, k % 2, k // 2]


def unpack_right(l, bufr, wr, wk):
    for k in range(8):
        rows = jnp.concatenate(
            [bufr[l, q // 2, q % 2, k % 2, k // 2].astype(F32) for q in range(4)], axis=0
        ).astype(BF)
        wr[l, k * 160 : (k + 1) * 160, :] = rows[:160]
        wk[l, k * 40 : (k + 1) * 40, :] = rows[160:200, :C]


def gather_kernel(v1, v2, r1, vs, r2, wd, wr, wk, bufd, bufr, owned, ownrt, send_sems, recv_sems):
    ids = peers(HI)
    sems = (send_sems, recv_sems)
    meet(*ids, False)
    chains = []
    for l in range(LAYERS):
        pack_own(l, v1, v2, r1, vs, r2, bufd, bufr, owned, ownrt, ids)
        chains += [bufd.at[l], bufr.at[l]]
    flying = [None] * 4
    for slot in range(8):
        for c in range(4):
            stage = slot - c
            if 1 <= stage <= 4:
                wait_all(flying[c])
            if 0 <= stage <= 3:
                flying[c] = gather_stage(stage, sems, c * 6, chains[c], ids)
                start_all(flying[c])
            if stage == 4:
                if c % 2 == 0:
                    unpack_down(c // 2, bufd, wd)
                else:
                    unpack_right(c // 2, bufr, wr, wk)


def run_gather(v1, v2, r1, vs, r2):
    sds = jax.ShapeDtypeStruct
    vmem = pl.BlockSpec(memory_space=pltpu.VMEM)
    return pl.pallas_call(
        gather_kernel,
        in_specs=[vmem] * 5,
        out_specs=[vmem] * 3,
        out_shape=[sds((LAYERS, 8, 480, 256), BF), sds((LAYERS, 1280, 512), BF), sds((LAYERS, 320, 160), BF)],
        scratch_shapes=[
            pltpu.VMEM((LAYERS, 2, 2, 2, HI, 120, 256), BF),
            pltpu.VMEM((LAYERS, 2, 2, 2, HI, 56, 512), BF),
            pltpu.VMEM((LAYERS, 4, 120, 256), BF),
            pltpu.VMEM((LAYERS, 4, 56, 512), BF),
            pltpu.SemaphoreType.DMA((24,)),
            pltpu.SemaphoreType.DMA((24,)),
        ],
        compiler_params=pltpu.CompilerParams(
            vmem_limit_bytes=40 << 20, collective_id=0, has_side_effects=True
        ),
        name="gather",
    )(v1, v2, r1, vs, r2)


def add_into(dst, src):
    lead = dst.shape[:-2]
    count = 1
    for n in lead:
        count *= n

    def body(i, carry):
        where = []
        for n in reversed(lead):
            where.insert(0, lax.rem(i, n))
            i = i // n
        where = tuple(where)
        dst[where] = (dst[where].astype(F32) + src[where].astype(F32)).astype(BF)
        return carry

    lax.fori_loop(0, count, body, 0)


def reduce_stage(stage, sems, first, g, bufs, ids):
    me, grp, hi, lo, y, core = ids
    t1, t2, t3, t4, fin = bufs
    if stage == 0:
        return [send(g.at[1 - core], t1, sems, first, (me, y * 2 + 1 - core))]
    if stage == 1:
        add_into(t1, g.at[core])
        return [send(t1.at[1 - y], t2, sems, first + 1, (me, (1 - y) * 2 + core))]
    if stage == 2:
        add_into(t2, t1.at[y])
        return [send(t2.at[1 - lo], t3, sems, first + 2, (hi * 2 + 1 - lo, grp))]
    if stage == 3:
        add_into(t3, t2.at[lo])
        return [
            send(t3.at[lax.rem(hi + k, HI)], t4.at[k - 1], sems, first + 2 + k, (lax.rem(hi + k, HI) * 2 + lo, grp))
            for k in range(1, HI)
        ]
    total = t3[hi].astype(F32)
    for k in range(1, HI):
        total = total + t4[k - 1].astype(F32)
    fin[core, y] = total.astype(BF)
    mine = fin.at[core, y]
    return [
        send(mine, mine, sems, first + 2 + HI + k - 1, (me, lax.rem(grp + k, 4))) for k in range(1, 4)
    ]


def col_to_row(col):
    return jnp.broadcast_to(col, (col.shape[0], 128)).T[0:1, :]


def row_to_col(row):
    return jnp.broadcast_to(row, (128, row.shape[1])).T[:, 0:1]


def quarters(fin):
    return jnp.concatenate([fin[q // 2, q % 2].astype(F32) for q in range(4)], axis=0)


def reduce_kernel(
    gd0, gr0, gd1, gr1, bias0, bias1, kappa, gains, v1, v2, r1, vs, r2,
    o1, o2, or1, os, or2, ogain, obias,
    *scratch,
):
    chain_bufs = [scratch[5 * c : 5 * c + 5] for c in range(4)]
    near_rows, far_rows, send_sems, recv_sems, row_send, row_recv = scratch[20:]
    ids = peers(HI)
    me, grp, hi, lo, y, core = ids
    sems = (send_sems, recv_sems)
    rsems = (row_send, row_recv)
    meet(*ids, True)
    grads = [gd1, gr1, gd0, gr0]
    near_rows[grp] = jnp.zeros((8, 1152), F32)
    near_rows[grp, 0:1, :1120] = bias0[...]
    near_rows[grp, 1:2, :1120] = bias1[...]
    rows = near_rows.at[grp]
    row_copies = [send(rows, rows, rsems, k - 1, (me, lax.rem(grp + k, 4))) for k in range(1, 4)]
    start_all(row_copies)
    flying = [None] * 4
    for slot in range(9):
        for c in range(4):
            stage = slot - c
            if 1 <= stage <= 5:
                wait_all(flying[c])
            if 0 <= stage <= 4:
                flying[c] = reduce_stage(stage, sems, c * 12, grads[c], chain_bufs[c], ids)
                start_all(flying[c])
    wait_all(row_copies)
    biases = near_rows[0] + near_rows[1] + near_rows[2] + near_rows[3]
    far_rows[me] = jnp.zeros((8, 1152), F32)
    far_rows[me, 2:4, :1120] = biases[0:2, :1120]
    kept = []
    for l in range(LAYERS):
        find, finr = chain_bufs[0 if l else 2][4], chain_bufs[1 if l else 3][4]
        recip_row = col_to_row(kappa[:, l : l + 1]) / gains[l : l + 1, :]
        recip = row_to_col(recip_row)
        down = quarters(find).T
        d2, d1 = down[:C2, :240], down[C2:480, :240]
        right = quarters(finr)
        e2, e1, es = right[:160, :C2], right[:160, C2:480], right[160:200, :C]

        def span(m):
            return slice(*SPANS[m])

        u1 = v1[l].astype(F32) * recip[span(0)]
        u2 = v2[l].astype(F32) * recip[span(1)]
        w1 = r1[l].astype(F32) * recip_row[:, span(2)]
        ws = vs[l].astype(F32) * recip_row[:, span(3)]
        w2 = r2[l].astype(F32) * recip_row[:, span(4)]
        dots = jnp.concatenate(
            [
                col_to_row(jnp.sum(d1 * u1, axis=1, keepdims=True)),
                col_to_row(jnp.sum(d2 * u2, axis=1, keepdims=True)),
                jnp.sum(e1 * w1, axis=0, keepdims=True),
                jnp.sum(es * ws, axis=0, keepdims=True),
                jnp.sum(e2 * w2, axis=0, keepdims=True),
            ],
            axis=1,
        )
        far_rows[me, l : l + 1, :1120] = dots
        kept.append((d1, u1, d2, u2, e1, w1, es, ws, e2, w2))
    rows = far_rows.at[me]
    row_copies = []
    for k in range(1, 2 * HI):
        row_copies.append(send(rows, rows, rsems, 2 + k, (lax.rem(me + k, 2 * HI), grp)))
    start_all(row_copies)
    wait_all(row_copies)
    total = far_rows[0]
    for k in range(1, 2 * HI):
        total = total + far_rows[k]
    obias[...] = total[2:4, :1120]
    for l in range(LAYERS):
        row = total[l : l + 1, :1120]
        ogain[l : l + 1, :] = row / col_to_row(kappa[:, l : l + 1])
        col = row_to_col(row)
        d1, u1, d2, u2, e1, w1, es, ws, e2, w2 = kept[l]
        o1[l] = d1 - u1 * col[SPANS[0][0] : SPANS[0][1]]
        o2[l] = d2 - u2 * col[SPANS[1][0] : SPANS[1][1]]
        or1[l] = e1 - w1 * row[:, SPANS[2][0] : SPANS[2][1]]
        os[l] = es - ws * row[:, SPANS[3][0] : SPANS[3][1]]
        or2[l] = e2 - w2 * row[:, SPANS[4][0] : SPANS[4][1]]


def run_reduce(lower, upper, kappa, gains, v1, v2, r1, vs, r2):
    sds = jax.ShapeDtypeStruct
    vmem = pl.BlockSpec(memory_space=pltpu.VMEM)
    scratch = []
    for c in range(4):
        high = 64 if c % 2 == 0 else 56
        scratch += [
            pltpu.VMEM((2, 2, HI, high, 512), BF),
            pltpu.VMEM((2, HI, high, 512), BF),
            pltpu.VMEM((HI, high, 512), BF),
            pltpu.VMEM((HI - 1, high, 512), BF),
            pltpu.VMEM((2, 2, high, 512), BF),
        ]
    return pl.pallas_call(
        reduce_kernel,
        in_specs=[vmem] * 13,
        out_specs=[vmem] * 7,
        out_shape=[sds(v.shape, F32) for v in (v1, v2, r1, vs, r2)] + [sds((LAYERS, 1120), F32)] * 2,
        scratch_shapes=scratch
        + [
            pltpu.VMEM((4, 8, 1152), F32),
            pltpu.VMEM((2 * HI, 8, 1152), F32),
            pltpu.SemaphoreType.DMA((48,)),
            pltpu.SemaphoreType.DMA((48,)),
            pltpu.SemaphoreType.DMA((10,)),
            pltpu.SemaphoreType.DMA((10,)),
        ],
        compiler_params=pltpu.CompilerParams(
            vmem_limit_bytes=56 << 20, collective_id=1, has_side_effects=True
        ),
        name="reduce",
    )(*lower[:2], *upper[:2], lower[2], upper[2], kappa, gains, v1, v2, r1, vs, r2)


def general_finish(lower, upper, whole_v, shards, gains):
    bias_sum = lax.psum(jnp.concatenate([lower[2], upper[2]], axis=0), ("dp", "grp"))
    sums = []
    units = []
    inverse = []
    for m, (low, high) in enumerate(zip(unpack(*lower[:2]), unpack(*upper[:2]))):
        part = lax.psum_scatter(jnp.stack([low, high]), "dp", scatter_dimension=1, tiled=True)
        sums.append(lax.psum(part, "grp").astype(F32))
        vals = whole_v[m].astype(F32)
        inv = lax.rsqrt(jnp.sum(vals * vals, axis=1))
        inverse.append(inv)
        units.append(shards[m].astype(F32) * inv[:, None, :])
    dots = jnp.concatenate([jnp.sum(units[m] * sums[m], axis=1) for m in range(5)], axis=1)
    dots = lax.psum(dots, "dp")
    grads = [sums[m] - units[m] * dots[:, None, lo:hi] for m, (lo, hi) in enumerate(SPANS)]
    return (*grads, dots / (gains * jnp.concatenate(inverse, axis=1)), bias_sum)


def on_device(
    quick,
    down_in,
    right_in,
    pixel_mask,
    down_cot,
    right_cot,
    v_down1,
    v_down2,
    v_right1,
    v_skip,
    v_right2,
    gains,
    biases,
):
    shards = (v_down1, v_down2, v_right1, v_skip, v_right2)
    turned = (v_down1.swapaxes(1, 2), v_down2.swapaxes(1, 2), v_right1, v_skip, v_right2)
    if quick:
        weights = run_gather(*turned)
    else:
        whole_v = tuple(lax.all_gather(v, "dp", axis=1, tiled=True) for v in shards)
        weights = assemble(*whole_v)
    cols = jnp.concatenate([gains, biases], axis=0).T
    n = down_in.shape[0]
    down_out, right_out, *kept, kappa = run_forward(down_in, right_in, *weights, cols)
    mask = pixel_mask.reshape(n, 4, 8, 32).transpose(0, 2, 1, 3).reshape(n, 1, 1024).astype(F32)
    down_g, right_g, cells_g, *upper = run_backward(1, down_cot, right_cot, None, mask, kept, kappa, *weights)
    down_grad, right_grad, *lower = run_backward(0, down_g, right_g, cells_g, mask, kept, kappa, *weights)
    if quick:
        grads = list(run_reduce(lower, upper, kappa, gains, *turned))
        grads[0] = grads[0].swapaxes(1, 2)
        grads[1] = grads[1].swapaxes(1, 2)
    else:
        grads = general_finish(lower, upper, whole_v, shards, gains)
    return (down_out, right_out, down_grad, right_grad, *grads)


def solution(mesh):
    photo = P(("dp", "grp"), None, None, None)
    rows = P(None, "dp", None)
    quick = mesh.shape["dp"] == 2 * HI and mesh.shape["grp"] == 4
    return jax.shard_map(
        functools.partial(on_device, quick),
        mesh=mesh,
        in_specs=(photo, photo, P(("dp", "grp"), None, None), photo, photo) + (rows,) * 5 + (P(), P()),
        out_specs=(photo,) * 4 + (rows,) * 5 + (P(), P()),
        check_vma=False,
    )
```

```python
import functools
import jax
import jax.numpy as jnp
from jax import lax
from jax.experimental import pallas as pl
from jax.experimental.pallas import tpu as pltpu
from jax.sharding import PartitionSpec as P

BF = jnp.bfloat16
F32 = jnp.float32
LAYERS = 2
HI = 4
MESH = pl.DeviceIdType.MESH
C = 160
C2 = 320
SPANS = ((0, 160), (160, 480), (480, 640), (640, 800), (800, 1120))


def nt(a, b):
    return lax.dot_general(a, b, (((1,), (1,)), ((), ())), preferred_element_type=F32)


def nn(a, b):
    return lax.dot_general(a, b, (((1,), (0,)), ((), ())), preferred_element_type=F32)


def eye(n):
    same = lax.broadcasted_iota(jnp.int32, (n, n), 0) == lax.broadcasted_iota(jnp.int32, (n, n), 1)
    return jnp.where(same, 1.0, 0.0).astype(BF)


def lane():
    return lax.broadcasted_iota(jnp.int32, (1, 128), 1)


def keep(cond, tile):
    return jnp.where(cond, tile, jnp.zeros((), tile.dtype))


def col_shift(tile, off):
    if off == 0:
        return tile
    col = lane() & 31
    if off == 1:
        return keep(col != 31, pltpu.roll(tile, 127, 1))
    return keep(col != 0, pltpu.roll(tile, 1, 1))


def row_before(tile):
    return keep(lane() >= 32, pltpu.roll(tile, 32, 1))


def row_after(tile):
    return keep(lane() < 96, pltpu.roll(tile, 96, 1))


def at(v):
    return slice(v * 128, (v + 1) * 128)


def put_down(ext, v, tile):
    n = tile.shape[0]
    for c in range(3):
        moved = col_shift(tile, c - 1)
        ext[c * n : (c + 1) * n, at(v + 1)] = moved
        if v == 7:
            ext[c * n : (c + 1) * n, at(0)] = row_before(moved)


def put_right(ext, v, tile):
    n = tile.shape[0]
    for c in range(2):
        moved = col_shift(tile, c - 1)
        ext[(2 + c) * n : (3 + c) * n, at(v)] = moved
        if v == 7:
            ext[c * n : (c + 1) * n, at(0)] = row_before(moved)
        else:
            ext[c * n : (c + 1) * n, at(v + 1)] = moved


def put_down_back(ext, v, tile):
    n = tile.shape[0]
    for c in range(3):
        moved = col_shift(tile, 1 - c)
        ext[c * n : (c + 1) * n, at(v)] = moved
        if v == 0:
            ext[c * n : (c + 1) * n, at(8)] = row_after(moved)


def put_right_back(ext, v, tile):
    n = tile.shape[0]
    for c in range(2):
        moved = col_shift(tile, 1 - c)
        ext[(2 + c) * n : (3 + c) * n, at(v)] = moved
        if v == 0:
            ext[c * n : (c + 1) * n, at(7)] = row_after(moved)
        else:
            ext[c * n : (c + 1) * n, at(v - 1)] = moved


def pair_elu(x):
    e = jnp.exp(-jnp.abs(x)) - 1.0
    up = x > 0
    return jnp.concatenate([jnp.where(up, x, e), jnp.where(up, e, -x)], axis=0).astype(BF)


def elu_back(grad, act):
    slope = jnp.minimum(act.astype(F32), 0.0) + 1.0
    both = grad * slope
    return both[:C] - both[C:]


def sigmoid(x):
    return 1.0 / (1.0 + jnp.exp(-x))


def load_cells(ref, v):
    rows = jnp.concatenate([ref[g * 8 + v] for g in range(4)], axis=0)
    return rows.T.astype(F32)


def store_bf16(ref, v, tile):
    out = tile.astype(BF).T
    for g in range(4):
        ref[g * 8 + v] = out[g * 32 : (g + 1) * 32]


def store_f32(ref, v, tile):
    out = tile.T
    for g in range(4):
        ref[g * 8 + v] = out[g * 32 : (g + 1) * 32]


def scale_of(total, gain):
    return gain * lax.rsqrt(total)


def square_sum(vals):
    vals = vals.astype(F32)
    return jnp.sum(vals * vals, axis=1, keepdims=True)


def block_square_sum(weight, lo, hi):
    total = None
    for k in range(8):
        vals = weight[k, lo:hi, :240].astype(F32)
        total = vals * vals if total is None else total + vals * vals
    return jnp.sum(total, axis=1, keepdims=True)


def down_product(weight, first, count, ext, j):
    acc = None
    for k in range(8):
        lo = j * 256 + 128 * (k // 4)
        part = nn(weight[k, first : first + count, :240], ext[240 * (k % 4) : 240 * (k % 4) + 240, lo : lo + 256])
        acc = part if acc is None else acc + part
    return acc


def fwd_kernel(
    down_in, right_in, wd, wr, wk, cols,
    down_out, right_out, cells, actd, actr, acth, gated, gater, kappa,
    right_t, skip_t, ext, ext4, dflow, rflow,
):
    @pl.when(pl.program_id(0) == 0)
    def _():
        for l in range(LAYERS):
            for k in range(4):
                rows = wr[l, k * C2 : (k + 1) * C2, :480]
                right_t[l, :, k * C2 : (k + 1) * C2] = nt(eye(480), rows).astype(BF)
            skip_t[l] = nt(eye(C), wk[l]).astype(BF)
            down_total = sum(square_sum(wd[l, k, :, :240]) for k in range(8))
            right_total = square_sum(right_t[l])
            totals = (down_total[C2:], down_total[:C2], right_total[C2:], square_sum(skip_t[l]), right_total[:C2])
            for total, (lo, hi) in zip(totals, SPANS):
                kappa[lo:hi, l : l + 1] = scale_of(total, cols[lo:hi, l : l + 1])

    for v in range(8):
        x = load_cells(down_in.at[0], v)
        dflow[:, at(v)] = x
        act = pair_elu(x)
        cells[0, 0, :, at(v)] = act
        put_down(ext, v, act)
        rflow[:, at(v)] = load_cells(right_in.at[0], v)
    for l in range(LAYERS):
        def scale(m):
            lo, hi = SPANS[m]
            return kappa[lo:hi, l : l + 1]

        def bias(m):
            lo, hi = SPANS[m]
            return cols[lo:hi, 2 + l : 3 + l]

        for j in range(4):
            acc = down_product(wd.at[l], C2, C, ext, j)
            for h in range(2):
                v = 2 * j + h
                actd[l, 0, :, at(v)] = pair_elu(acc[:, at(h)] * scale(0) + bias(0))
        for v in range(8):
            put_down(ext, v, actd[l, 0, :, at(v)])
            act = pair_elu(rflow[:, at(v)])
            actr[l, 0, :, at(v)] = act
            put_right(ext4, v, act)
        for j in range(4):
            acc = down_product(wd.at[l], 0, C2, ext, j)
            for h in range(2):
                v = 2 * j + h
                gate = acc[:, at(h)] * scale(1) + bias(1)
                t = gate[:C]
                s = sigmoid(gate[C:])
                gated[l, 0, :C, at(v)] = t.astype(BF)
                gated[l, 0, C:, at(v)] = s.astype(BF)
                new = dflow[:, at(v)] + t * s
                dflow[:, at(v)] = new
                cells[l + 1, 0, :, at(v)] = pair_elu(new)
        skip_bias = bias(2) + bias(3)
        for j in range(4):
            acc = nn(right_t[l, C2:], ext4[:, j * 256 : j * 256 + 256]) * scale(2)
            acc = acc + nn(skip_t[l], cells[l + 1, 0, :, j * 256 : j * 256 + 256]) * scale(3)
            for h in range(2):
                v = 2 * j + h
                acth[l, 0, :, at(v)] = pair_elu(acc[:, at(h)] + skip_bias)
        for v in range(8):
            put_right(ext4, v, acth[l, 0, :, at(v)])
            if l + 1 < LAYERS:
                put_down(ext, v, cells[l + 1, 0, :, at(v)])
        for j in range(4):
            acc = nn(right_t[l, :C2], ext4[:, j * 256 : j * 256 + 256])
            for h in range(2):
                v = 2 * j + h
                gate = acc[:, at(h)] * scale(4) + bias(4)
                t = gate[:C]
                s = sigmoid(gate[C:])
                gater[l, 0, :C, at(v)] = t.astype(BF)
                gater[l, 0, C:, at(v)] = s.astype(BF)
                rflow[:, at(v)] = rflow[:, at(v)] + t * s
    for v in range(8):
        store_bf16(down_out.at[0], v, dflow[:, at(v)])
        store_bf16(right_out.at[0], v, rflow[:, at(v)])


def gate_back(g, t, s):
    p = g * s
    q = p * t * (1.0 - s)
    return jnp.concatenate([p, q], axis=0)


def bwd_kernel(
    top, down_g, right_g, mask, *refs,
):
    refs = list(refs)
    cells_g = None if top else refs.pop(0)
    (
        low_cells, high_cells, actd, actr, acth, gated, gater, kappa, wd, wr, wk,
    ) = refs[:11]
    refs = refs[11:]
    if top:
        down_out, right_out, cells_out = refs[:3]
        refs = refs[3:]
    else:
        down_out, right_out = refs[:2]
        refs = refs[2:]
    (
        od, orr, obias,
        b1, b2, br1, br2, g1, g2, gr1, gs, gr2, bsum, ext, ext1, ext4, ext41, dskip, gdown, gright,
    ) = refs
    layer = 1 if top else 0
    step = pl.program_id(0)

    @pl.when(step == 0)
    def _():
        for k in range(8):
            rows = nt(eye(240), wd[0, k, :, :240]).astype(BF)
            for p in range(3):
                tap, chan = divmod(240 * k + 80 * p, C2)
                a, c = divmod(tap, 3)
                b2[a, chan : chan + 80, c * C2 : (c + 1) * C2] = rows[80 * p : 80 * p + 80, :C2]
                b1[a, chan : chan + 80, c * C : (c + 1) * C] = rows[80 * p : 80 * p + 80, C2:]
        for t in range(4):
            rows = wr[0, t * C2 : (t + 1) * C2, :480]
            br2[:, t * C2 : (t + 1) * C2] = rows[:, :C2]
            br1[:, t * C : (t + 1) * C] = rows[:, C2:]
        for acc in (g1, g2, gr1, gs, gr2, bsum):
            acc[...] = jnp.zeros(acc.shape, F32)

    def scale(m):
        lo, hi = SPANS[m]
        return kappa[lo:hi, layer : layer + 1]

    def add_bias(m, total):
        lo, hi = SPANS[m]
        bsum[lo:hi, :] += total

    total = None
    for v in range(8):
        if top:
            m = mask[0, :, at(v)]
            gdown[:, at(v)] = load_cells(down_g.at[0], v) * m
            g = load_cells(right_g.at[0], v) * m
            gright[:, at(v)] = g
        else:
            g = right_g[0, :, at(v)]
        d = gate_back(g, gater[0, 0, :C, at(v)].astype(F32), gater[0, 0, C:, at(v)].astype(F32))
        total = d if total is None else total + d
        put_right_back(ext4, v, (d * scale(4)).astype(BF))
    add_bias(4, total)
    gr2[...] += nt(acth[0, 0], ext4[...])
    total = None
    for j in range(4):
        e = nn(br2[...], ext4[:, j * 256 : j * 256 + 256])
        for h in range(2):
            v = 2 * j + h
            d = elu_back(e[:, at(h)], acth[0, 0, :, at(v)])
            total = d if total is None else total + d
            put_right_back(ext41, v, (d * scale(2)).astype(BF))
            dskip[:, at(v)] = (d * scale(3)).astype(BF)
    add_bias(2, total)
    add_bias(3, total)
    gr1[...] += nt(actr[0, 0], ext41[...])
    gs[...] += nt(high_cells[0, 0], dskip[...])
    for j in range(4):
        e = nn(br1[...], ext41[:, j * 256 : j * 256 + 256])
        k = nn(wk[0], dskip[:, j * 256 : j * 256 + 256])
        for h in range(2):
            v = 2 * j + h
            old = gright[:, at(v)] if top else right_g[0, :, at(v)]
            new = old + elu_back(e[:, at(h)], actr[0, 0, :, at(v)])
            if top:
                right_out[0, :, at(v)] = new
            else:
                store_f32(right_out.at[0], v, new)
            gc = k[:, at(h)]
            if not top:
                gc = gc + cells_g[0, :, at(v)]
            old = gdown[:, at(v)] if top else down_g[0, :, at(v)]
            gdown[:, at(v)] = old + elu_back(gc, high_cells[0, 0, :, at(v)])
    total = None
    for v in range(8):
        g = gdown[:, at(v)]
        if top:
            down_out[0, :, at(v)] = g
        d = gate_back(g, gated[0, 0, :C, at(v)].astype(F32), gated[0, 0, C:, at(v)].astype(F32))
        total = d if total is None else total + d
        put_down_back(ext, v, (d * scale(1)).astype(BF))
    add_bias(1, total)
    for a in range(2):
        lo = 128 * (1 - a)
        g2[a] += nt(actd[0, 0], ext[:, lo : lo + 1024])
    total = None
    for j in range(4):
        e = nn(b2[1], ext[:, j * 256 : j * 256 + 256])
        e = e + nn(b2[0], ext[:, j * 256 + 128 : j * 256 + 384])
        for h in range(2):
            v = 2 * j + h
            d = elu_back(e[:, at(h)], actd[0, 0, :, at(v)])
            total = d if total is None else total + d
            put_down_back(ext1, v, (d * scale(0)).astype(BF))
    add_bias(0, total)
    for a in range(2):
        lo = 128 * (1 - a)
        g1[a] += nt(low_cells[0, 0], ext1[:, lo : lo + 1024])
    for j in range(4):
        e = nn(b1[1], ext1[:, j * 256 : j * 256 + 256])
        e = e + nn(b1[0], ext1[:, j * 256 + 128 : j * 256 + 384])
        if top:
            cells_out[0, :, j * 256 : j * 256 + 256] = e
        else:
            for h in range(2):
                v = 2 * j + h
                last = gdown[:, at(v)] + elu_back(e[:, at(h)], low_cells[0, 0, :, at(v)])
                store_f32(down_out.at[0], v, last)

    @pl.when(step == pl.num_programs(0) - 1)
    def _():
        def put(out, block, row, lanes, tile):
            high = out.shape[4]
            done = 0
            while done < tile.shape[0]:
                q, r = divmod(row + done, high)
                size = min(high - r, tile.shape[0] - done)
                out[q // 2, q % 2, block % 2, block // 2, r : r + size, lanes] = tile[done : done + size]
                done += size

        for k in range(8):
            for p in range(3):
                tap, chan = divmod(240 * k + 80 * p, C2)
                a, c = divmod(tap, 3)
                part = jnp.concatenate(
                    [g2[a, chan : chan + 80, c * C2 : (c + 1) * C2], g1[a, chan : chan + 80, c * C : (c + 1) * C]], axis=1
                )
                put(od, k, 80 * p, slice(0, 480), part.astype(BF))
        for k in range(8):
            t, half = divmod(k, 2)
            row = slice(half * C, (half + 1) * C)
            part = jnp.concatenate([gr2[row, t * C2 : (t + 1) * C2], gr1[row, t * C : (t + 1) * C]], axis=1)
            put(orr, k, 0, slice(0, 480), part.astype(BF))
            put(orr, k, C, slice(0, C), gs[40 * k : 40 * k + 40].astype(BF))
        obias[...] = jnp.sum(bsum[...].T, axis=0, keepdims=True)


def whole(shape, dtype=None):
    zeros = (0,) * len(shape)
    return pl.BlockSpec(shape, lambda i: zeros)


def once(shape):
    zeros = (0,) * len(shape)
    return pl.BlockSpec(shape, lambda i: zeros, pipeline_mode=pl.Buffered(1))


def image(shape):
    rest = (0,) * (len(shape) - 1)
    return pl.BlockSpec(shape, lambda i: (i,) + rest)


GD_SHAPE = (2, 2, 2, 4, 64, 512)
GR_SHAPE = (2, 2, 2, 4, 56, 512)
PX = 1024


def run_forward(down_in, right_in, wd, wr, wk, cols):
    n = down_in.shape[0]
    sds = jax.ShapeDtypeStruct
    kept = [(3, C2, PX)] + [(LAYERS, C2, PX)] * 5
    return pl.pallas_call(
        fwd_kernel,
        grid=(n,),
        in_specs=[image((1, 32, 32, C))] * 2 + [once(w.shape) for w in (wd, wr, wk)] + [once((1120, 4))],
        out_specs=[image((1, 32, 32, C))] * 2
        + [pl.BlockSpec((s[0], 1) + s[1:], lambda i: (0, i, 0, 0)) for s in kept]
        + [once((1120, 2))],
        out_shape=[sds((n, 32, 32, C), BF)] * 2
        + [sds((s[0], n) + s[1:], BF) for s in kept]
        + [sds((1120, 2), F32)],
        scratch_shapes=[
            pltpu.VMEM((LAYERS, 480, 1280), BF),
            pltpu.VMEM((LAYERS, C, C2), BF),
            pltpu.VMEM((960, 1152), BF),
            pltpu.VMEM((1280, PX), BF),
            pltpu.VMEM((C, PX), F32),
            pltpu.VMEM((C, PX), F32),
        ],
        compiler_params=pltpu.CompilerParams(vmem_limit_bytes=60 << 20),
        name="forward",
    )(down_in, right_in, wd, wr, wk, cols)


def run_backward(layer, down_g, right_g, cells_g, mask, kept, kappa, wd, wr, wk):
    n = down_g.shape[0]
    top = layer == 1
    sds = jax.ShapeDtypeStruct
    flow = image((1, C, PX))
    wide = image((1, C2, PX))

    def pick(which):
        return pl.BlockSpec((1, 1, C2, PX), lambda i: (which, i, 0, 0))

    def one_layer(shape):
        rest = (0,) * (len(shape) - 1)
        return pl.BlockSpec((1,) + shape[1:], lambda i: (layer,) + rest, pipeline_mode=pl.Buffered(1))

    cells = kept[0]
    ins = [down_g, right_g, mask] + ([] if top else [cells_g]) + [cells, cells] + list(kept[1:]) + [kappa, wd, wr, wk]
    photo = image((1, 32, 32, C))
    in_specs = (
        ([photo] * 2 if top else [flow] * 2)
        + [image((1, 1, PX))]
        + ([] if top else [wide])
        + [pick(layer), pick(layer + 1)]
        + [pick(layer)] * 5
        + [once((1120, 2))]
        + [one_layer(w.shape) for w in (wd, wr, wk)]
    )
    if top:
        out_specs = [flow, flow, wide]
        out_shape = [sds((n, C, PX), F32)] * 2 + [sds((n, C2, PX), F32)]
    else:
        out_specs = [photo] * 2
        out_shape = [sds((n, 32, 32, C), F32)] * 2
    return pl.pallas_call(
        functools.partial(bwd_kernel, top),
        grid=(n,),
        in_specs=in_specs,
        out_specs=out_specs + [once(GD_SHAPE), once(GR_SHAPE), once((1, 1120))],
        out_shape=out_shape + [sds(GD_SHAPE, BF), sds(GR_SHAPE, BF), sds((1, 1120), F32)],
        scratch_shapes=[
            pltpu.VMEM((2, 320, 480), BF),
            pltpu.VMEM((2, 320, 960), BF),
            pltpu.VMEM((320, 640), BF),
            pltpu.VMEM((320, 1280), BF),
            pltpu.VMEM((2, 320, 480), F32),
            pltpu.VMEM((2, 320, 960), F32),
            pltpu.VMEM((320, 640), F32),
            pltpu.VMEM((320, 160), F32),
            pltpu.VMEM((320, 1280), F32),
            pltpu.VMEM((1120, 128), F32),
            pltpu.VMEM((960, 1152), BF),
            pltpu.VMEM((480, 1152), BF),
            pltpu.VMEM((1280, 1024), BF),
            pltpu.VMEM((640, 1024), BF),
            pltpu.VMEM((160, 1024), BF),
            pltpu.VMEM((C, PX), F32),
            pltpu.VMEM((C, PX), F32),
        ],
        compiler_params=pltpu.CompilerParams(vmem_limit_bytes=60 << 20),
        name="backward%d" % layer,
    )(*ins)


def assemble(v1, v2, r1, vs, r2):
    rows = jnp.concatenate([v2, v1], axis=2).reshape(LAYERS, 8, 240, 480)
    wd = jnp.pad(rows.swapaxes(2, 3), ((0, 0), (0, 0), (0, 0), (0, 16)))
    wr = jnp.pad(jnp.concatenate([r2, r1], axis=2), ((0, 0), (0, 0), (0, 32)))
    return wd, wr, vs


def unpack(gd, gr):
    d = gd.transpose(3, 2, 0, 1, 4, 5).reshape(8, 256, 512)[:, :240].reshape(1920, 512)
    r = gr.transpose(3, 2, 0, 1, 4, 5).reshape(8, 224, 512)
    right = r[:, :160].reshape(1280, 512)
    skip = r[:, 160:200, :C].reshape(320, C)
    return d[:, C2:480], d[:, :C2], right[:, C2:480], skip, right[:, :C2]


def peers(hi_count):
    me = lax.axis_index("dp")
    grp = lax.axis_index("grp")
    hi, lo = me // 2, lax.rem(me, 2)
    y, core = grp // 2, lax.rem(grp, 2)
    return me, grp, hi, lo, y, core


def meet(me, grp, hi, lo, y, core, everyone):
    barrier = pltpu.get_barrier_semaphore()
    near = [((hi + k) % HI * 2 + lo, grp) for k in range(1, HI)]
    near += [(hi * 2 + 1 - lo, grp)]
    if everyone:
        near += [((hi + k) % HI * 2 + 1 - lo, grp) for k in range(1, HI)]
    near += [(me, (grp + k) % 4) for k in range(1, 4)]
    for device in near:
        pl.semaphore_signal(barrier, inc=1, device_id=device, device_id_type=MESH)
    pl.semaphore_wait(barrier, len(near))


def send(src, dst, sems, at_, device):
    return pltpu.make_async_remote_copy(
        src_ref=src,
        dst_ref=dst,
        send_sem=sems[0].at[at_],
        recv_sem=sems[1].at[at_],
        device_id=device,
        device_id_type=MESH,
    )


def start_all(copies):
    for copy in copies:
        copy.start()


def wait_all(copies):
    for copy in copies:
        copy.wait()


def add_into(dst, src):
    lead = dst.shape[:-2]
    count = 1
    for n in lead:
        count *= n

    def body(i, carry):
        where = []
        for n in reversed(lead):
            where.insert(0, lax.rem(i, n))
            i = i // n
        where = tuple(where)
        dst[where] = (dst[where].astype(F32) + src[where].astype(F32)).astype(BF)
        return carry

    lax.fori_loop(0, count, body, 0)


def reduce_stage(stage, sems, first, g, bufs, ids):
    me, grp, hi, lo, y, core = ids
    t1, t2, t3, t4, fin = bufs
    if stage == 0:
        return [send(g.at[1 - core], t1, sems, first, (me, y * 2 + 1 - core))]
    if stage == 1:
        add_into(t1, g.at[core])
        return [send(t1.at[1 - y], t2, sems, first + 1, (me, (1 - y) * 2 + core))]
    if stage == 2:
        add_into(t2, t1.at[y])
        return [send(t2.at[1 - lo], t3, sems, first + 2, (hi * 2 + 1 - lo, grp))]
    if stage == 3:
        add_into(t3, t2.at[lo])
        return [
            send(t3.at[lax.rem(hi + k, HI)], t4.at[k - 1], sems, first + 2 + k, (lax.rem(hi + k, HI) * 2 + lo, grp))
            for k in range(1, HI)
        ]
    total = t3[hi].astype(F32)
    for k in range(1, HI):
        total = total + t4[k - 1].astype(F32)
    fin[core, y] = total.astype(BF)
    mine = fin.at[core, y]
    return [
        send(mine, mine, sems, first + 2 + HI + k - 1, (me, lax.rem(grp + k, 4))) for k in range(1, 4)
    ]


def col_to_row(col):
    return jnp.broadcast_to(col, (col.shape[0], 128)).T[0:1, :]


def row_to_col(row):
    return jnp.broadcast_to(row, (128, row.shape[1])).T[:, 0:1]


def quarters(fin):
    return jnp.concatenate([fin[q // 2, q % 2].astype(F32) for q in range(4)], axis=0)


def reduce_kernel(
    gd0, gr0, gd1, gr1, bias0, bias1, kappa, gains, v1, v2, r1, vs, r2,
    o1, o2, or1, os, or2, ogain, obias,
    *scratch,
):
    chain_bufs = [scratch[5 * c : 5 * c + 5] for c in range(4)]
    near_rows, far_rows, send_sems, recv_sems, row_send, row_recv = scratch[20:]
    ids = peers(HI)
    me, grp, hi, lo, y, core = ids
    sems = (send_sems, recv_sems)
    rsems = (row_send, row_recv)
    meet(*ids, True)
    grads = [gd1, gr1, gd0, gr0]
    near_rows[grp] = jnp.zeros((8, 1152), F32)
    near_rows[grp, 0:1, :1120] = bias0[...]
    near_rows[grp, 1:2, :1120] = bias1[...]
    rows = near_rows.at[grp]
    row_copies = [send(rows, rows, rsems, k - 1, (me, lax.rem(grp + k, 4))) for k in range(1, 4)]
    start_all(row_copies)
    flying = [None] * 4
    for slot in range(9):
        for c in range(4):
            stage = slot - c
            if 1 <= stage <= 5:
                wait_all(flying[c])
            if 0 <= stage <= 4:
                flying[c] = reduce_stage(stage, sems, c * 12, grads[c], chain_bufs[c], ids)
                start_all(flying[c])
    wait_all(row_copies)
    biases = near_rows[0] + near_rows[1] + near_rows[2] + near_rows[3]
    far_rows[me] = jnp.zeros((8, 1152), F32)
    far_rows[me, 2:4, :1120] = biases[0:2, :1120]
    kept = []
    for l in range(LAYERS):
        find, finr = chain_bufs[0 if l else 2][4], chain_bufs[1 if l else 3][4]
        recip_row = col_to_row(kappa[:, l : l + 1]) / gains[l : l + 1, :]
        recip = row_to_col(recip_row)
        down = quarters(find).T
        d2, d1 = down[:C2, :240], down[C2:480, :240]
        right = quarters(finr)
        e2, e1, es = right[:160, :C2], right[:160, C2:480], right[160:200, :C]

        def span(m):
            return slice(*SPANS[m])

        u1 = v1[l].astype(F32) * recip[span(0)]
        u2 = v2[l].astype(F32) * recip[span(1)]
        w1 = r1[l].astype(F32) * recip_row[:, span(2)]
        ws = vs[l].astype(F32) * recip_row[:, span(3)]
        w2 = r2[l].astype(F32) * recip_row[:, span(4)]
        dots = jnp.concatenate(
            [
                col_to_row(jnp.sum(d1 * u1, axis=1, keepdims=True)),
                col_to_row(jnp.sum(d2 * u2, axis=1, keepdims=True)),
                jnp.sum(e1 * w1, axis=0, keepdims=True),
                jnp.sum(es * ws, axis=0, keepdims=True),
                jnp.sum(e2 * w2, axis=0, keepdims=True),
            ],
            axis=1,
        )
        far_rows[me, l : l + 1, :1120] = dots
        kept.append((d1, u1, d2, u2, e1, w1, es, ws, e2, w2))
    rows = far_rows.at[me]
    row_copies = []
    for k in range(1, 2 * HI):
        row_copies.append(send(rows, rows, rsems, 2 + k, (lax.rem(me + k, 2 * HI), grp)))
    start_all(row_copies)
    wait_all(row_copies)
    total = far_rows[0]
    for k in range(1, 2 * HI):
        total = total + far_rows[k]
    obias[...] = total[2:4, :1120]
    for l in range(LAYERS):
        row = total[l : l + 1, :1120]
        ogain[l : l + 1, :] = row / col_to_row(kappa[:, l : l + 1])
        col = row_to_col(row)
        d1, u1, d2, u2, e1, w1, es, ws, e2, w2 = kept[l]
        o1[l] = d1 - u1 * col[SPANS[0][0] : SPANS[0][1]]
        o2[l] = d2 - u2 * col[SPANS[1][0] : SPANS[1][1]]
        or1[l] = e1 - w1 * row[:, SPANS[2][0] : SPANS[2][1]]
        os[l] = es - ws * row[:, SPANS[3][0] : SPANS[3][1]]
        or2[l] = e2 - w2 * row[:, SPANS[4][0] : SPANS[4][1]]


def run_reduce(lower, upper, kappa, gains, v1, v2, r1, vs, r2):
    sds = jax.ShapeDtypeStruct
    vmem = pl.BlockSpec(memory_space=pltpu.VMEM)
    scratch = []
    for c in range(4):
        high = 64 if c % 2 == 0 else 56
        scratch += [
            pltpu.VMEM((2, 2, HI, high, 512), BF),
            pltpu.VMEM((2, HI, high, 512), BF),
            pltpu.VMEM((HI, high, 512), BF),
            pltpu.VMEM((HI - 1, high, 512), BF),
            pltpu.VMEM((2, 2, high, 512), BF),
        ]
    return pl.pallas_call(
        reduce_kernel,
        in_specs=[vmem] * 13,
        out_specs=[vmem] * 7,
        out_shape=[sds(v.shape, F32) for v in (v1, v2, r1, vs, r2)] + [sds((LAYERS, 1120), F32)] * 2,
        scratch_shapes=scratch
        + [
            pltpu.VMEM((4, 8, 1152), F32),
            pltpu.VMEM((2 * HI, 8, 1152), F32),
            pltpu.SemaphoreType.DMA((48,)),
            pltpu.SemaphoreType.DMA((48,)),
            pltpu.SemaphoreType.DMA((10,)),
            pltpu.SemaphoreType.DMA((10,)),
        ],
        compiler_params=pltpu.CompilerParams(
            vmem_limit_bytes=56 << 20, collective_id=1, has_side_effects=True
        ),
        name="reduce",
    )(*lower[:2], *upper[:2], lower[2], upper[2], kappa, gains, v1, v2, r1, vs, r2)


D1, D2A, D2B, RT = 0, 1, 2, 3
PIECE = {D1: (80, 256), D2A: (40, 256), D2B: (80, 256), RT: (112, 512)}


def gather_copies(kind, stage, buf, sems, first, ids):
    me, grp, hi, lo, y, core = ids
    if kind == D2A:
        mine, line, plane = buf.at[core, y, lo, hi], buf.at[core, y, lo], buf.at[core, y]
    else:
        mine, line, plane = buf.at[core, lo, hi], buf.at[core, lo], None
    if stage == "z":
        return [
            send(mine, mine, sems, first + k - 1, (lax.rem(hi + k, HI) * 2 + lo, grp)) for k in range(1, HI)
        ]
    if stage == "x":
        return [send(line, line, sems, first + HI - 1, (hi * 2 + 1 - lo, grp))]
    if stage == "y":
        return [send(plane, plane, sems, first + HI, (me, (1 - y) * 2 + core))]
    part = buf.at[core]
    return [send(part, part, sems, first + HI + 1, (me, y * 2 + 1 - core))]


def forward_kernel(
    down_in, right_in, v1, v2, r1, vs, r2, gains, biases,
    down_out, right_out, cells_o, actd_o, actr_o, acth_o, gated_o, gater_o, wd_o, wr_o, wk_o, kappa,
    cells, actd, actr, acth, gated, gater, wd, wr, wk,
    b_d1, b_d2a, b_d2b, b_rt, own_d, own_q, own_r, right_t, skip_t, ext, ext4, dflow, rflow, photo_d, photo_r, bias_col,
    send_sems, recv_sems, in_sems, out_sems,
):
    n = down_in.shape[0]
    ids = peers(HI)
    me, grp, hi, lo, y, core = ids
    sems = (send_sems, recv_sems)
    load_d = pltpu.make_async_copy(down_in, photo_d, in_sems.at[0])
    load_r = pltpu.make_async_copy(right_in, photo_r, in_sems.at[1])
    load_d.start()
    load_r.start()
    meet(*ids, False)
    bufs = {D1: b_d1, D2A: b_d2a, D2B: b_d2b, RT: b_rt}

    def copies(l, kind, stage):
        return gather_copies(kind, stage, bufs[kind].at[l], sems, (l * 4 + kind) * 6, ids)

    def start(l, kind, stage):
        start_all(copies(l, kind, stage))

    def wait(l, kind, stage):
        wait_all(copies(l, kind, stage))

    for l in range(LAYERS):
        own_d[l, :C2, :240] = v2[l]
        own_d[l, C2:, :240] = v1[l]
        own_d[l, :, 240:] = jnp.zeros((480, 16), BF)
        right = jnp.concatenate([r2[l], r1[l]], axis=1).astype(F32)
        right = jnp.concatenate([right, jnp.zeros((160, 32), F32)], axis=1)
        skip = jnp.concatenate([vs[l].astype(F32), jnp.zeros((40, 352), F32)], axis=1)
        own_r[l] = jnp.concatenate([right, skip, jnp.zeros((24, 512), F32)], axis=0).astype(BF)
        b_d1[l, core, lo, hi] = own_d[l, pl.ds(pl.multiple_of(C2 + core * 80, 16), 80), :]
        for q in range(4):
            own_q[l, q] = own_d[l, q * 40 : q * 40 + 40, :]
        b_d2a[l, core, y, lo, hi] = own_q[l, core * 2 + y]
        b_d2b[l, core, lo, hi] = own_d[l, pl.ds(pl.multiple_of(C + core * 80, 16), 80), :]
        b_rt[l, core, lo, hi] = own_r[l, pl.ds(pl.multiple_of(core * 112, 16), 112), :]
        if l == 0:
            start(0, D1, "z")
            start(0, D2A, "z")

    def unpack_d1(l):
        for k in range(8):
            for c in range(2):
                wd[l, k, C2 + c * 80 : C2 + c * 80 + 80, :] = b_d1[l, c, k % 2, k // 2]

    def unpack_d2(l):
        for k in range(8):
            for q in range(4):
                wd[l, k, q * 40 : q * 40 + 40, :] = b_d2a[l, q // 2, q % 2, k % 2, k // 2]
            for c in range(2):
                wd[l, k, C + c * 80 : C + c * 80 + 80, :] = b_d2b[l, c, k % 2, k // 2]

    def unpack_rt(l):
        for k in range(8):
            wr[l, k * 160 : k * 160 + 112, :] = b_rt[l, 0, k % 2, k // 2]
            wr[l, k * 160 + 112 : k * 160 + 160, :] = b_rt[l, 1, k % 2, k // 2, :48]
            wk[l, k * 40 : k * 40 + 40, :] = b_rt[l, 1, k % 2, k // 2, 48:88, :C]
        for k in range(4):
            rows = wr[l, k * C2 : (k + 1) * C2, :480]
            right_t[l, :, k * C2 : (k + 1) * C2] = nt(eye(480), rows).astype(BF)
        skip_t[l] = nt(eye(C), wk[l]).astype(BF)

    def set_scale(l, m, total):
        lo_, hi_ = SPANS[m]
        gain = row_to_col(gains[l : l + 1, lo_:hi_])
        kappa[lo_:hi_, l : l + 1] = scale_of(total, gain)

    def scale(l, m):
        lo_, hi_ = SPANS[m]
        return kappa[lo_:hi_, l : l + 1]

    def bias(l, m):
        lo_, hi_ = SPANS[m]
        return bias_col[lo_:hi_, l : l + 1]

    keep_out = []

    def save(src, dst):
        copy = pltpu.make_async_copy(src, dst, out_sems.at[len(keep_out)])
        copy.start()
        keep_out.append(copy)

    for l in range(LAYERS):
        bias_col[:, l : l + 1] = row_to_col(biases[l : l + 1, :])
    load_d.wait()
    load_r.wait()

    def begin(i, carry):
        for v in range(8):
            x = load_cells(photo_d.at[i], v)
            dflow[i, :, at(v)] = x
            cells[0, i, :, at(v)] = pair_elu(x)
            rflow[i, :, at(v)] = load_cells(photo_r.at[i], v)
        return carry

    wait(0, D1, "z")
    start(0, D1, "x")
    start(0, D2B, "z")
    wait(0, D2A, "z")
    start(0, D2A, "x")
    lax.fori_loop(0, n, begin, 0)
    save(cells.at[0], cells_o.at[0])
    wait(0, D1, "x")
    start(0, D1, "core")
    start(0, RT, "z")
    wait(0, D2A, "x")
    start(0, D2A, "y")
    wait(0, D1, "core")

    def finish(flow, photo, i, carry):
        for v in range(8):
            store_bf16(photo.at[i], v, flow[i, :, at(v)])
        return carry

    def part_a(l, hooks):
        unpack_d1(l)
        set_scale(l, 0, block_square_sum(wd.at[l], C2, 480))

        def body(i, carry):
            for v in range(8):
                put_down(ext, v, cells[l, i, :, at(v)])
            for j in range(4):
                acc = down_product(wd.at[l], C2, C, ext, j)
                for h in range(2):
                    v = 2 * j + h
                    actd[l, i, :, at(v)] = pair_elu(acc[:, at(h)] * scale(l, 0) + bias(l, 0))
            for k, hook in hooks.items():
                pl.when(i == k)(hook)
            return carry

        lax.fori_loop(0, n, body, 0)
        save(actd.at[l], actd_o.at[l])

    def part_b(l, hooks):
        unpack_d2(l)
        set_scale(l, 1, block_square_sum(wd.at[l], 0, C2))
        save(wd.at[l], wd_o.at[l])

        def body(i, carry):
            for v in range(8):
                put_down(ext, v, actd[l, i, :, at(v)])
            for j in range(4):
                acc = down_product(wd.at[l], 0, C2, ext, j)
                for h in range(2):
                    v = 2 * j + h
                    gate = acc[:, at(h)] * scale(l, 1) + bias(l, 1)
                    t = gate[:C]
                    s = sigmoid(gate[C:])
                    gated[l, i, :C, at(v)] = t.astype(BF)
                    gated[l, i, C:, at(v)] = s.astype(BF)
                    new = dflow[i, :, at(v)] + t * s
                    dflow[i, :, at(v)] = new
                    cells[l + 1, i, :, at(v)] = pair_elu(new)
            for k, hook in hooks.items():
                pl.when(i == k)(hook)
            return carry

        lax.fori_loop(0, n, body, 0)
        save(gated.at[l], gated_o.at[l])
        save(cells.at[l + 1], cells_o.at[l + 1])
        if l == LAYERS - 1:
            lax.fori_loop(0, n, functools.partial(finish, dflow, photo_d), 0)
            save(photo_d, down_out)

    def part_c(l, hooks):
        unpack_rt(l)
        total = square_sum(right_t[l])
        set_scale(l, 2, total[C2:])
        set_scale(l, 3, square_sum(skip_t[l]))
        set_scale(l, 4, total[:C2])
        save(wr.at[l], wr_o.at[l])
        save(wk.at[l], wk_o.at[l])

        def body(i, carry):
            for v in range(8):
                act = pair_elu(rflow[i, :, at(v)])
                actr[l, i, :, at(v)] = act
                put_right(ext4, v, act)
            skip_bias = bias(l, 2) + bias(l, 3)
            for j in range(4):
                acc = nn(right_t[l, C2:], ext4[:, j * 256 : j * 256 + 256]) * scale(l, 2)
                acc = acc + nn(skip_t[l], cells[l + 1, i, :, j * 256 : j * 256 + 256]) * scale(l, 3)
                for h in range(2):
                    v = 2 * j + h
                    acth[l, i, :, at(v)] = pair_elu(acc[:, at(h)] + skip_bias)
            for v in range(8):
                put_right(ext4, v, acth[l, i, :, at(v)])
            for j in range(4):
                acc = nn(right_t[l, :C2], ext4[:, j * 256 : j * 256 + 256])
                for h in range(2):
                    v = 2 * j + h
                    gate = acc[:, at(h)] * scale(l, 4) + bias(l, 4)
                    t = gate[:C]
                    s = sigmoid(gate[C:])
                    gater[l, i, :C, at(v)] = t.astype(BF)
                    gater[l, i, C:, at(v)] = s.astype(BF)
                    new = rflow[i, :, at(v)] + t * s
                    rflow[i, :, at(v)] = new
            for k, hook in hooks.items():
                pl.when(i == k)(hook)
            return carry

        lax.fori_loop(0, n, body, 0)
        save(actr.at[l], actr_o.at[l])
        save(acth.at[l], acth_o.at[l])
        save(gater.at[l], gater_o.at[l])
        if l == LAYERS - 1:
            lax.fori_loop(0, n, functools.partial(finish, rflow, photo_r), 0)
            save(photo_r, right_out)

    last = n - 1

    def a0_first():
        wait(0, D2B, "z")
        start(0, D2B, "x")

    def a0_last():
        wait(0, D2A, "y")
        start(0, D2A, "core")
        wait(0, D2B, "x")
        start(0, D2B, "core")
        wait(0, RT, "z")
        start(0, RT, "x")
        start(1, D1, "z")
        start(1, D2A, "z")

    def b0_mid():
        wait(1, D1, "z")
        start(1, D1, "x")
        wait(1, D2A, "z")
        start(1, D2A, "x")
        start(1, D2B, "z")

    def b0_last():
        wait(0, RT, "x")
        start(0, RT, "core")
        wait(1, D2B, "z")
        start(1, D2B, "x")
        start(1, RT, "z")

    def c0_first():
        wait(1, D1, "x")
        start(1, D1, "core")
        wait(1, D2A, "x")
        start(1, D2A, "y")

    def c0_last():
        wait(1, D2B, "x")
        start(1, D2B, "core")
        wait(1, D2A, "y")
        start(1, D2A, "core")
        wait(1, RT, "z")
        start(1, RT, "x")

    def b1_last():
        wait(1, RT, "x")
        start(1, RT, "core")

    part_a(0, {0: a0_first, last: a0_last})
    wait(0, D2A, "core")
    wait(0, D2B, "core")
    part_b(0, {1: b0_mid, last: b0_last})
    wait(0, RT, "core")
    part_c(0, {0: c0_first, last: c0_last})
    wait(1, D1, "core")
    part_a(1, {})
    wait(1, D2A, "core")
    wait(1, D2B, "core")
    part_b(1, {last: b1_last})
    wait(1, RT, "core")
    part_c(1, {})
    for copy in keep_out:
        copy.wait()


def run_forward_gather(down_in, right_in, v1, v2, r1, vs, r2, gains, biases):
    n = down_in.shape[0]
    sds = jax.ShapeDtypeStruct
    vmem = pl.BlockSpec(memory_space=pltpu.VMEM)
    hbm = pl.BlockSpec(memory_space=pl.ANY)
    act = (LAYERS, n, C2, PX)
    kept = [(LAYERS + 1, n, C2, PX)] + [act] * 5
    weights = [(LAYERS, 8, 480, 256), (LAYERS, 1280, 512), (LAYERS, C2, C)]
    photo = (n, 32, 32, C)
    return pl.pallas_call(
        forward_kernel,
        in_specs=[hbm] * 2 + [vmem] * 7,
        out_specs=[hbm] * 11 + [vmem],
        out_shape=[sds(photo, BF)] * 2 + [sds(s, BF) for s in kept + weights] + [sds((1120, 2), F32)],
        scratch_shapes=[pltpu.VMEM(s, BF) for s in kept + weights]
        + [
            pltpu.VMEM((LAYERS, 2, 2, HI) + PIECE[D1], BF),
            pltpu.VMEM((LAYERS, 2, 2, 2, HI) + PIECE[D2A], BF),
            pltpu.VMEM((LAYERS, 2, 2, HI) + PIECE[D2B], BF),
            pltpu.VMEM((LAYERS, 2, 2, HI) + PIECE[RT], BF),
            pltpu.VMEM((LAYERS, 480, 256), BF),
            pltpu.VMEM((LAYERS, 4, 40, 256), BF),
            pltpu.VMEM((LAYERS, 224, 512), BF),
            pltpu.VMEM((LAYERS, 480, 1280), BF),
            pltpu.VMEM((LAYERS, C, C2), BF),
            pltpu.VMEM((960, 1152), BF),
            pltpu.VMEM((1280, PX), BF),
            pltpu.VMEM((n, C, PX), F32),
            pltpu.VMEM((n, C, PX), F32),
            pltpu.VMEM(photo, BF),
            pltpu.VMEM(photo, BF),
            pltpu.VMEM((1120, LAYERS), F32),
            pltpu.SemaphoreType.DMA((48,)),
            pltpu.SemaphoreType.DMA((48,)),
            pltpu.SemaphoreType.DMA((2,)),
            pltpu.SemaphoreType.DMA((32,)),
        ],
        compiler_params=pltpu.CompilerParams(
            vmem_limit_bytes=62 << 20, collective_id=0, has_side_effects=True
        ),
        name="forward_gather",
    )(down_in, right_in, v1, v2, r1, vs, r2, gains, biases)


def general_finish(lower, upper, whole_v, shards, gains):
    bias_sum = lax.psum(jnp.concatenate([lower[2], upper[2]], axis=0), ("dp", "grp"))
    sums = []
    units = []
    inverse = []
    for m, (low, high) in enumerate(zip(unpack(*lower[:2]), unpack(*upper[:2]))):
        part = lax.psum_scatter(jnp.stack([low, high]), "dp", scatter_dimension=1, tiled=True)
        sums.append(lax.psum(part, "grp").astype(F32))
        vals = whole_v[m].astype(F32)
        inv = lax.rsqrt(jnp.sum(vals * vals, axis=1))
        inverse.append(inv)
        units.append(shards[m].astype(F32) * inv[:, None, :])
    dots = jnp.concatenate([jnp.sum(units[m] * sums[m], axis=1) for m in range(5)], axis=1)
    dots = lax.psum(dots, "dp")
    grads = [sums[m] - units[m] * dots[:, None, lo:hi] for m, (lo, hi) in enumerate(SPANS)]
    return (*grads, dots / (gains * jnp.concatenate(inverse, axis=1)), bias_sum)


def on_device(
    quick,
    down_in,
    right_in,
    pixel_mask,
    down_cot,
    right_cot,
    v_down1,
    v_down2,
    v_right1,
    v_skip,
    v_right2,
    gains,
    biases,
):
    shards = (v_down1, v_down2, v_right1, v_skip, v_right2)
    turned = (v_down1.swapaxes(1, 2), v_down2.swapaxes(1, 2), v_right1, v_skip, v_right2)
    n = down_in.shape[0]
    if quick:
        down_out, right_out, *rest = run_forward_gather(down_in, right_in, *turned, gains, biases)
        kept, weights, kappa = rest[:6], rest[6:9], rest[9]
    else:
        whole_v = tuple(lax.all_gather(v, "dp", axis=1, tiled=True) for v in shards)
        weights = assemble(*whole_v)
        cols = jnp.concatenate([gains, biases], axis=0).T
        down_out, right_out, *kept, kappa = run_forward(down_in, right_in, *weights, cols)
    mask = pixel_mask.reshape(n, 4, 8, 32).transpose(0, 2, 1, 3).reshape(n, 1, 1024).astype(F32)
    down_g, right_g, cells_g, *upper = run_backward(1, down_cot, right_cot, None, mask, kept, kappa, *weights)
    down_grad, right_grad, *lower = run_backward(0, down_g, right_g, cells_g, mask, kept, kappa, *weights)
    if quick:
        grads = list(run_reduce(lower, upper, kappa, gains, *turned))
        grads[0] = grads[0].swapaxes(1, 2)
        grads[1] = grads[1].swapaxes(1, 2)
    else:
        grads = general_finish(lower, upper, whole_v, shards, gains)
    return (down_out, right_out, down_grad, right_grad, *grads)


def solution(mesh):
    photo = P(("dp", "grp"), None, None, None)
    rows = P(None, "dp", None)
    quick = mesh.shape["dp"] == 2 * HI and mesh.shape["grp"] == 4
    return jax.shard_map(
        functools.partial(on_device, quick),
        mesh=mesh,
        in_specs=(photo, photo, P(("dp", "grp"), None, None), photo, photo) + (rows,) * 5 + (P(), P()),
        out_specs=(photo,) * 4 + (rows,) * 5 + (P(), P()),
        check_vma=False,
    )
```

```python
import functools
import jax
import jax.numpy as jnp
from jax import lax
from jax.experimental import pallas as pl
from jax.experimental.pallas import tpu as pltpu
from jax.sharding import PartitionSpec as P

BF = jnp.bfloat16
F32 = jnp.float32
LAYERS = 2
HI = 4
MESH = pl.DeviceIdType.MESH
C = 160
C2 = 320
SPANS = ((0, 160), (160, 480), (480, 640), (640, 800), (800, 1120))


def nt(a, b):
    return lax.dot_general(a, b, (((1,), (1,)), ((), ())), preferred_element_type=F32)


def nn(a, b):
    return lax.dot_general(a, b, (((1,), (0,)), ((), ())), preferred_element_type=F32)


def eye(n):
    same = lax.broadcasted_iota(jnp.int32, (n, n), 0) == lax.broadcasted_iota(jnp.int32, (n, n), 1)
    return jnp.where(same, 1.0, 0.0).astype(BF)


def lane():
    return lax.broadcasted_iota(jnp.int32, (1, 128), 1)


def keep(cond, tile):
    return jnp.where(cond, tile, jnp.zeros((), tile.dtype))


def col_shift(tile, off):
    if off == 0:
        return tile
    col = lane() & 31
    if off == 1:
        return keep(col != 31, pltpu.roll(tile, 127, 1))
    return keep(col != 0, pltpu.roll(tile, 1, 1))


def row_before(tile):
    return keep(lane() >= 32, pltpu.roll(tile, 32, 1))


def row_after(tile):
    return keep(lane() < 96, pltpu.roll(tile, 96, 1))


def at(v):
    return slice(v * 128, (v + 1) * 128)


def put_down(ext, v, tile):
    n = tile.shape[0]
    for c in range(3):
        moved = col_shift(tile, c - 1)
        ext[c * n : (c + 1) * n, at(v + 1)] = moved
        if v == 7:
            ext[c * n : (c + 1) * n, at(0)] = row_before(moved)


def put_right(ext, v, tile):
    n = tile.shape[0]
    for c in range(2):
        moved = col_shift(tile, c - 1)
        ext[(2 + c) * n : (3 + c) * n, at(v)] = moved
        if v == 7:
            ext[c * n : (c + 1) * n, at(0)] = row_before(moved)
        else:
            ext[c * n : (c + 1) * n, at(v + 1)] = moved


def put_down_back(ext, v, tile):
    n = tile.shape[0]
    for c in range(3):
        moved = col_shift(tile, 1 - c)
        ext[c * n : (c + 1) * n, at(v)] = moved
        if v == 0:
            ext[c * n : (c + 1) * n, at(8)] = row_after(moved)


def put_right_back(ext, v, tile):
    n = tile.shape[0]
    for c in range(2):
        moved = col_shift(tile, 1 - c)
        ext[(2 + c) * n : (3 + c) * n, at(v)] = moved
        if v == 0:
            ext[c * n : (c + 1) * n, at(7)] = row_after(moved)
        else:
            ext[c * n : (c + 1) * n, at(v - 1)] = moved


def pair_elu(x):
    e = jnp.exp(-jnp.abs(x)) - 1.0
    up = x > 0
    return jnp.concatenate([jnp.where(up, x, e), jnp.where(up, e, -x)], axis=0).astype(BF)


def elu_back(grad, act):
    slope = jnp.minimum(act.astype(F32), 0.0) + 1.0
    both = grad * slope
    return both[:C] - both[C:]


def sigmoid(x):
    return 1.0 / (1.0 + jnp.exp(-x))


def load_cells(ref, v):
    rows = jnp.concatenate([ref[g * 8 + v] for g in range(4)], axis=0)
    return rows.T.astype(F32)


def store_bf16(ref, v, tile):
    out = tile.astype(BF).T
    for g in range(4):
        ref[g * 8 + v] = out[g * 32 : (g + 1) * 32]


def store_f32(ref, v, tile):
    out = tile.T
    for g in range(4):
        ref[g * 8 + v] = out[g * 32 : (g + 1) * 32]


def scale_of(total, gain):
    return gain * lax.rsqrt(total)


def square_sum(vals):
    vals = vals.astype(F32)
    return jnp.sum(vals * vals, axis=1, keepdims=True)


def block_square_sum(weight, lo, hi):
    total = None
    for k in range(8):
        vals = weight[k, lo:hi, :240].astype(F32)
        total = vals * vals if total is None else total + vals * vals
    return jnp.sum(total, axis=1, keepdims=True)


def down_product(weight, first, count, ext, j):
    acc = None
    for k in range(8):
        lo = j * 256 + 128 * (k // 4)
        part = nn(weight[k, first : first + count, :240], ext[240 * (k % 4) : 240 * (k % 4) + 240, lo : lo + 256])
        acc = part if acc is None else acc + part
    return acc


def fwd_kernel(
    down_in, right_in, wd, wr, wk, cols,
    down_out, right_out, cells, actd, actr, acth, gated, gater, kappa,
    right_t, skip_t, ext, ext4, dflow, rflow,
):
    @pl.when(pl.program_id(0) == 0)
    def _():
        for l in range(LAYERS):
            for k in range(4):
                rows = wr[l, k * C2 : (k + 1) * C2, :480]
                right_t[l, :, k * C2 : (k + 1) * C2] = nt(eye(480), rows).astype(BF)
            skip_t[l] = nt(eye(C), wk[l]).astype(BF)
            down_total = sum(square_sum(wd[l, k, :, :240]) for k in range(8))
            right_total = square_sum(right_t[l])
            totals = (down_total[C2:], down_total[:C2], right_total[C2:], square_sum(skip_t[l]), right_total[:C2])
            for total, (lo, hi) in zip(totals, SPANS):
                kappa[lo:hi, l : l + 1] = scale_of(total, cols[lo:hi, l : l + 1])

    for v in range(8):
        x = load_cells(down_in.at[0], v)
        dflow[:, at(v)] = x
        act = pair_elu(x)
        cells[0, 0, :, at(v)] = act
        put_down(ext, v, act)
        rflow[:, at(v)] = load_cells(right_in.at[0], v)
    for l in range(LAYERS):
        def scale(m):
            lo, hi = SPANS[m]
            return kappa[lo:hi, l : l + 1]

        def bias(m):
            lo, hi = SPANS[m]
            return cols[lo:hi, 2 + l : 3 + l]

        for j in range(4):
            acc = down_product(wd.at[l], C2, C, ext, j)
            for h in range(2):
                v = 2 * j + h
                actd[l, 0, :, at(v)] = pair_elu(acc[:, at(h)] * scale(0) + bias(0))
        for v in range(8):
            put_down(ext, v, actd[l, 0, :, at(v)])
            act = pair_elu(rflow[:, at(v)])
            actr[l, 0, :, at(v)] = act
            put_right(ext4, v, act)
        for j in range(4):
            acc = down_product(wd.at[l], 0, C2, ext, j)
            for h in range(2):
                v = 2 * j + h
                gate = acc[:, at(h)] * scale(1) + bias(1)
                t = gate[:C]
                s = sigmoid(gate[C:])
                gated[l, 0, :C, at(v)] = t.astype(BF)
                gated[l, 0, C:, at(v)] = s.astype(BF)
                new = dflow[:, at(v)] + t * s
                dflow[:, at(v)] = new
                cells[l + 1, 0, :, at(v)] = pair_elu(new)
        skip_bias = bias(2) + bias(3)
        for j in range(4):
            acc = nn(right_t[l, C2:], ext4[:, j * 256 : j * 256 + 256]) * scale(2)
            acc = acc + nn(skip_t[l], cells[l + 1, 0, :, j * 256 : j * 256 + 256]) * scale(3)
            for h in range(2):
                v = 2 * j + h
                acth[l, 0, :, at(v)] = pair_elu(acc[:, at(h)] + skip_bias)
        for v in range(8):
            put_right(ext4, v, acth[l, 0, :, at(v)])
            if l + 1 < LAYERS:
                put_down(ext, v, cells[l + 1, 0, :, at(v)])
        for j in range(4):
            acc = nn(right_t[l, :C2], ext4[:, j * 256 : j * 256 + 256])
            for h in range(2):
                v = 2 * j + h
                gate = acc[:, at(h)] * scale(4) + bias(4)
                t = gate[:C]
                s = sigmoid(gate[C:])
                gater[l, 0, :C, at(v)] = t.astype(BF)
                gater[l, 0, C:, at(v)] = s.astype(BF)
                rflow[:, at(v)] = rflow[:, at(v)] + t * s
    for v in range(8):
        store_bf16(down_out.at[0], v, dflow[:, at(v)])
        store_bf16(right_out.at[0], v, rflow[:, at(v)])


def gate_back(g, t, s):
    p = g * s
    q = p * t * (1.0 - s)
    return jnp.concatenate([p, q], axis=0)


def bwd_kernel(
    top, down_g, right_g, mask, *refs,
):
    refs = list(refs)
    cells_g = None if top else refs.pop(0)
    (
        low_cells, high_cells, actd, actr, acth, gated, gater, kappa, wd, wr, wk,
    ) = refs[:11]
    refs = refs[11:]
    if top:
        down_out, right_out, cells_out = refs[:3]
        refs = refs[3:]
    else:
        down_out, right_out = refs[:2]
        refs = refs[2:]
    (
        o_rg, o_da, o_db, o_dc, orows,
        b1, b2, br1, br2, g1, g2, gr1, gs, gr2, bsum, ext, ext1, ext4, ext41, dskip, gdown, gright,
    ) = refs
    layer = 1 if top else 0
    step = pl.program_id(0)

    @pl.when(step == 0)
    def _():
        down_taps(wd.at[0], b1, b2)
        right_taps(wr.at[0], br1, br2)
        for acc in (g1, g2, gr1, gs, gr2, bsum):
            acc[...] = jnp.zeros(acc.shape, F32)

    def scale(m):
        lo, hi = SPANS[m]
        return kappa[lo:hi, layer : layer + 1]

    def add_bias(m, total):
        lo, hi = SPANS[m]
        bsum[lo:hi, :] += total

    total = None
    for v in range(8):
        if top:
            m = mask[0, :, at(v)]
            gdown[:, at(v)] = load_cells(down_g.at[0], v) * m
            g = load_cells(right_g.at[0], v) * m
            gright[:, at(v)] = g
        else:
            g = right_g[0, :, at(v)]
        d = gate_back(g, gater[0, 0, :C, at(v)].astype(F32), gater[0, 0, C:, at(v)].astype(F32))
        total = d if total is None else total + d
        put_right_back(ext4, v, (d * scale(4)).astype(BF))
    add_bias(4, total)
    gr2[...] += nt(acth[0, 0], ext4[...])
    total = None
    for j in range(4):
        e = nn(br2[...], ext4[:, j * 256 : j * 256 + 256])
        for h in range(2):
            v = 2 * j + h
            d = elu_back(e[:, at(h)], acth[0, 0, :, at(v)])
            total = d if total is None else total + d
            put_right_back(ext41, v, (d * scale(2)).astype(BF))
            dskip[:, at(v)] = (d * scale(3)).astype(BF)
    add_bias(2, total)
    add_bias(3, total)
    gr1[...] += nt(actr[0, 0], ext41[...])
    gs[...] += nt(high_cells[0, 0], dskip[...])
    for j in range(4):
        e = nn(br1[...], ext41[:, j * 256 : j * 256 + 256])
        k = nn(wk[0], dskip[:, j * 256 : j * 256 + 256])
        for h in range(2):
            v = 2 * j + h
            old = gright[:, at(v)] if top else right_g[0, :, at(v)]
            new = old + elu_back(e[:, at(h)], actr[0, 0, :, at(v)])
            if top:
                right_out[0, :, at(v)] = new
            else:
                store_f32(right_out.at[0], v, new)
            gc = k[:, at(h)]
            if not top:
                gc = gc + cells_g[0, :, at(v)].astype(F32)
            old = gdown[:, at(v)] if top else down_g[0, :, at(v)]
            gdown[:, at(v)] = old + elu_back(gc, high_cells[0, 0, :, at(v)])
    total = None
    for v in range(8):
        g = gdown[:, at(v)]
        if top:
            down_out[0, :, at(v)] = g
        d = gate_back(g, gated[0, 0, :C, at(v)].astype(F32), gated[0, 0, C:, at(v)].astype(F32))
        total = d if total is None else total + d
        put_down_back(ext, v, (d * scale(1)).astype(BF))
    add_bias(1, total)
    for a in range(2):
        lo = 128 * (1 - a)
        g2[a] += nt(actd[0, 0], ext[:, lo : lo + 1024])
    total = None
    for j in range(4):
        e = nn(b2[1], ext[:, j * 256 : j * 256 + 256])
        e = e + nn(b2[0], ext[:, j * 256 + 128 : j * 256 + 384])
        for h in range(2):
            v = 2 * j + h
            d = elu_back(e[:, at(h)], actd[0, 0, :, at(v)])
            total = d if total is None else total + d
            put_down_back(ext1, v, (d * scale(0)).astype(BF))
    add_bias(0, total)
    for a in range(2):
        lo = 128 * (1 - a)
        g1[a] += nt(low_cells[0, 0], ext1[:, lo : lo + 1024])
    for j in range(4):
        e = nn(b1[1], ext1[:, j * 256 : j * 256 + 256])
        e = e + nn(b1[0], ext1[:, j * 256 + 128 : j * 256 + 384])
        if top:
            cells_out[0, :, j * 256 : j * 256 + 256] = e.astype(BF)
        else:
            for h in range(2):
                v = 2 * j + h
                last = gdown[:, at(v)] + elu_back(e[:, at(h)], low_cells[0, 0, :, at(v)])
                store_f32(down_out.at[0], v, last)

    @pl.when(step == pl.num_programs(0) - 1)
    def _():
        pack_right(o_rg, gr2, gr1, gs)
        pack_down(o_da, DA, g2, C2, 0)
        pack_down(o_db, DB, g2, C2, C)
        pack_down(o_dc, DC, g1, C, 0)
        orows[0:1, :] = jnp.concatenate(
            [
                dot_rows(b1[0], g1[0], C, 3) + dot_rows(b1[1], g1[1], C, 3),
                dot_rows(b2[0], g2[0], C2, 3) + dot_rows(b2[1], g2[1], C2, 3),
                dot_rows(br1[...], gr1[...], C, 4),
                dot_rows(wk[0], gs[...], C, 1),
                dot_rows(br2[...], gr2[...], C2, 4),
            ],
            axis=1,
        )
        orows[1:2, :] = jnp.sum(bsum[...].T, axis=0, keepdims=True)


def whole(shape, dtype=None):
    zeros = (0,) * len(shape)
    return pl.BlockSpec(shape, lambda i: zeros)


def once(shape):
    zeros = (0,) * len(shape)
    return pl.BlockSpec(shape, lambda i: zeros, pipeline_mode=pl.Buffered(1))


def image(shape):
    rest = (0,) * (len(shape) - 1)
    return pl.BlockSpec(shape, lambda i: (i,) + rest)


PX = 1024


def run_forward(down_in, right_in, wd, wr, wk, cols):
    n = down_in.shape[0]
    sds = jax.ShapeDtypeStruct
    kept = [(3, C2, PX)] + [(LAYERS, C2, PX)] * 5
    return pl.pallas_call(
        fwd_kernel,
        grid=(n,),
        in_specs=[image((1, 32, 32, C))] * 2 + [once(w.shape) for w in (wd, wr, wk)] + [once((1120, 4))],
        out_specs=[image((1, 32, 32, C))] * 2
        + [pl.BlockSpec((s[0], 1) + s[1:], lambda i: (0, i, 0, 0)) for s in kept]
        + [once((1120, 2))],
        out_shape=[sds((n, 32, 32, C), BF)] * 2
        + [sds((s[0], n) + s[1:], BF) for s in kept]
        + [sds((1120, 2), F32)],
        scratch_shapes=[
            pltpu.VMEM((LAYERS, 480, 1280), BF),
            pltpu.VMEM((LAYERS, C, C2), BF),
            pltpu.VMEM((960, 1152), BF),
            pltpu.VMEM((1280, PX), BF),
            pltpu.VMEM((C, PX), F32),
            pltpu.VMEM((C, PX), F32),
        ],
        compiler_params=pltpu.CompilerParams(vmem_limit_bytes=60 << 20),
        name="forward",
    )(down_in, right_in, wd, wr, wk, cols)


def run_backward(layer, down_g, right_g, cells_g, mask, kept, kappa, wd, wr, wk):
    n = down_g.shape[0]
    top = layer == 1
    sds = jax.ShapeDtypeStruct
    flow = image((1, C, PX))
    wide = image((1, C2, PX))

    def pick(which):
        return pl.BlockSpec((1, 1, C2, PX), lambda i: (which, i, 0, 0))

    def one_layer(shape):
        rest = (0,) * (len(shape) - 1)
        return pl.BlockSpec((1,) + shape[1:], lambda i: (layer,) + rest, pipeline_mode=pl.Buffered(1))

    cells = kept[0]
    ins = [down_g, right_g, mask] + ([] if top else [cells_g]) + [cells, cells] + list(kept[1:]) + [kappa, wd, wr, wk]
    photo = image((1, 32, 32, C))
    in_specs = (
        ([photo] * 2 if top else [flow] * 2)
        + [image((1, 1, PX))]
        + ([] if top else [wide])
        + [pick(layer), pick(layer + 1)]
        + [pick(layer)] * 5
        + [once((1120, 2))]
        + [one_layer(w.shape) for w in (wd, wr, wk)]
    )
    if top:
        out_specs = [flow, flow, wide]
        out_shape = [sds((n, C, PX), F32)] * 2 + [sds((n, C2, PX), BF)]
    else:
        out_specs = [photo] * 2
        out_shape = [sds((n, 32, 32, C), F32)] * 2
    return pl.pallas_call(
        functools.partial(bwd_kernel, top),
        grid=(n,),
        in_specs=in_specs,
        out_specs=out_specs + [once(sum_shape(kind)) for kind in KINDS] + [once((2, 1120))],
        out_shape=out_shape + [sds(sum_shape(kind), BF) for kind in KINDS] + [sds((2, 1120), F32)],
        scratch_shapes=[
            pltpu.VMEM((2, 320, 480), BF),
            pltpu.VMEM((2, 320, 960), BF),
            pltpu.VMEM((320, 640), BF),
            pltpu.VMEM((320, 1280), BF),
            pltpu.VMEM((2, 320, 480), F32),
            pltpu.VMEM((2, 320, 960), F32),
            pltpu.VMEM((320, 640), F32),
            pltpu.VMEM((320, 160), F32),
            pltpu.VMEM((320, 1280), F32),
            pltpu.VMEM((1120, 128), F32),
            pltpu.VMEM((960, 1152), BF),
            pltpu.VMEM((480, 1152), BF),
            pltpu.VMEM((1280, 1024), BF),
            pltpu.VMEM((640, 1024), BF),
            pltpu.VMEM((160, 1024), BF),
            pltpu.VMEM((C, PX), F32),
            pltpu.VMEM((C, PX), F32),
        ],
        compiler_params=pltpu.CompilerParams(vmem_limit_bytes=60 << 20),
        name="backward%d" % layer,
    )(*ins)


def assemble(v1, v2, r1, vs, r2):
    rows = jnp.concatenate([v2, v1], axis=2).reshape(LAYERS, 8, 240, 480)
    wd = jnp.pad(rows.swapaxes(2, 3), ((0, 0), (0, 0), (0, 0), (0, 16)))
    wr = jnp.pad(jnp.concatenate([r2, r1], axis=2), ((0, 0), (0, 0), (0, 32)))
    return wd, wr, vs


def unpack(*packed):
    rows = []
    for kind, g in zip(KINDS, packed):
        order = (3, 1, 0, 2, 4, 5) if X_FIRST[kind] else (3, 2, 0, 1, 4, 5)
        rows.append(g.transpose(order).reshape(8, 4 * ROWS[kind], 512))

    def down(block):
        return block[:, :80, :480].reshape(8, 80, 3, C).swapaxes(1, 2).reshape(1920, C)

    right = rows[0][:, :C].reshape(1280, 512)
    skip = rows[0][:, C:200, :C].reshape(C2, C)
    down2 = jnp.concatenate([down(rows[1]), down(rows[2])], axis=1)
    return down(rows[3]), down2, right[:, C2:480], skip, right[:, :C2]


def peers(hi_count):
    me = lax.axis_index("dp")
    grp = lax.axis_index("grp")
    hi, lo = me // 2, lax.rem(me, 2)
    y, core = grp // 2, lax.rem(grp, 2)
    return me, grp, hi, lo, y, core


def meet(me, grp, hi, lo, y, core, everyone):
    barrier = pltpu.get_barrier_semaphore()
    near = [((hi + k) % HI * 2 + lo, grp) for k in range(1, HI)]
    near += [(hi * 2 + 1 - lo, grp)]
    if everyone:
        near += [((hi + k) % HI * 2 + 1 - lo, grp) for k in range(1, HI)]
    near += [(me, (grp + k) % 4) for k in range(1, 4)]
    for device in near:
        pl.semaphore_signal(barrier, inc=1, device_id=device, device_id_type=MESH)
    pl.semaphore_wait(barrier, len(near))


def send(src, dst, sems, at_, device):
    return pltpu.make_async_remote_copy(
        src_ref=src,
        dst_ref=dst,
        send_sem=sems[0].at[at_],
        recv_sem=sems[1].at[at_],
        device_id=device,
        device_id_type=MESH,
    )


def start_all(copies):
    for copy in copies:
        copy.start()


def wait_all(copies):
    for copy in copies:
        copy.wait()


def add_into(dst, src):
    lead = dst.shape[:-2]
    count = 1
    for n in lead:
        count *= n

    def body(i, carry):
        where = []
        for n in reversed(lead):
            where.insert(0, lax.rem(i, n))
            i = i // n
        where = tuple(where)
        dst[where] = (dst[where].astype(F32) + src[where].astype(F32)).astype(BF)
        return carry

    lax.fori_loop(0, count, body, 0)


def col_to_row(col):
    return jnp.broadcast_to(col, (col.shape[0], 128)).T[0:1, :]


def row_to_col(row):
    return jnp.broadcast_to(row, (128, row.shape[1])).T[:, 0:1]


def quarters(fin, kind):
    rows = []
    for q in range(4):
        core, y = divmod(q, 2)
        rows.append(fin[core, y].astype(F32))
    return jnp.concatenate(rows, axis=0)


D1, D2A, D2B, RT = 0, 1, 2, 3
PIECE = {D1: (80, 256), D2A: (40, 256), D2B: (80, 256), RT: (112, 512)}


def gather_copies(kind, stage, buf, sems, first, ids):
    me, grp, hi, lo, y, core = ids
    if kind == D2A:
        mine, line, plane = buf.at[core, y, lo, hi], buf.at[core, y, lo], buf.at[core, y]
    else:
        mine, line, plane = buf.at[core, lo, hi], buf.at[core, lo], None
    if stage == "z":
        return [
            send(mine, mine, sems, first + k - 1, (lax.rem(hi + k, HI) * 2 + lo, grp)) for k in range(1, HI)
        ]
    if stage == "x":
        return [send(line, line, sems, first + HI - 1, (hi * 2 + 1 - lo, grp))]
    if stage == "y":
        return [send(plane, plane, sems, first + HI, (me, (1 - y) * 2 + core))]
    part = buf.at[core]
    return [send(part, part, sems, first + HI + 1, (me, y * 2 + 1 - core))]


def forward_kernel(
    down_in, right_in, v1, v2, r1, vs, r2, gains, biases,
    down_out, right_out, cells_o, actd_o, actr_o, acth_o, gated_o, gater_o, wd_o, wr_o, wk_o, kappa,
    cells, actd, actr, acth, gated, gater, wd, wr, wk,
    b_d1, b_d2a, b_d2b, b_rt, own_d, own_q, own_r, right_t, skip_t, ext, ext4, dflow, rflow, photo_d, photo_r, bias_col,
    send_sems, recv_sems, in_sems, out_sems,
):
    n = down_in.shape[0]
    ids = peers(HI)
    me, grp, hi, lo, y, core = ids
    sems = (send_sems, recv_sems)
    load_d = pltpu.make_async_copy(down_in, photo_d, in_sems.at[0])
    load_r = pltpu.make_async_copy(right_in, photo_r, in_sems.at[1])
    load_d.start()
    load_r.start()
    meet(*ids, False)
    bufs = {D1: b_d1, D2A: b_d2a, D2B: b_d2b, RT: b_rt}

    def copies(l, kind, stage):
        return gather_copies(kind, stage, bufs[kind].at[l], sems, (l * 4 + kind) * 6, ids)

    def start(l, kind, stage):
        start_all(copies(l, kind, stage))

    def wait(l, kind, stage):
        wait_all(copies(l, kind, stage))

    for l in range(LAYERS):
        own_d[l, :C2, :240] = v2[l]
        own_d[l, C2:, :240] = v1[l]
        own_d[l, :, 240:] = jnp.zeros((480, 16), BF)
        right = jnp.concatenate([r2[l], r1[l]], axis=1).astype(F32)
        right = jnp.concatenate([right, jnp.zeros((160, 32), F32)], axis=1)
        skip = jnp.concatenate([vs[l].astype(F32), jnp.zeros((40, 352), F32)], axis=1)
        own_r[l] = jnp.concatenate([right, skip, jnp.zeros((24, 512), F32)], axis=0).astype(BF)
        b_d1[l, core, lo, hi] = own_d[l, pl.ds(pl.multiple_of(C2 + core * 80, 16), 80), :]
        for q in range(4):
            own_q[l, q] = own_d[l, q * 40 : q * 40 + 40, :]
        b_d2a[l, core, y, lo, hi] = own_q[l, core * 2 + y]
        b_d2b[l, core, lo, hi] = own_d[l, pl.ds(pl.multiple_of(C + core * 80, 16), 80), :]
        b_rt[l, core, lo, hi] = own_r[l, pl.ds(pl.multiple_of(core * 112, 16), 112), :]
        if l == 0:
            start(0, D1, "z")
            start(0, D2A, "z")

    def unpack_d1(l):
        for k in range(8):
            for c in range(2):
                wd[l, k, C2 + c * 80 : C2 + c * 80 + 80, :] = b_d1[l, c, k % 2, k // 2]

    def unpack_d2(l):
        for k in range(8):
            for q in range(4):
                wd[l, k, q * 40 : q * 40 + 40, :] = b_d2a[l, q // 2, q % 2, k % 2, k // 2]
            for c in range(2):
                wd[l, k, C + c * 80 : C + c * 80 + 80, :] = b_d2b[l, c, k % 2, k // 2]

    def unpack_rt(l):
        for k in range(8):
            wr[l, k * 160 : k * 160 + 112, :] = b_rt[l, 0, k % 2, k // 2]
            wr[l, k * 160 + 112 : k * 160 + 160, :] = b_rt[l, 1, k % 2, k // 2, :48]
            wk[l, k * 40 : k * 40 + 40, :] = b_rt[l, 1, k % 2, k // 2, 48:88, :C]
        for k in range(4):
            rows = wr[l, k * C2 : (k + 1) * C2, :480]
            right_t[l, :, k * C2 : (k + 1) * C2] = nt(eye(480), rows).astype(BF)
        skip_t[l] = nt(eye(C), wk[l]).astype(BF)

    def set_scale(l, m, total):
        lo_, hi_ = SPANS[m]
        gain = row_to_col(gains[l : l + 1, lo_:hi_])
        kappa[lo_:hi_, l : l + 1] = scale_of(total, gain)

    def scale(l, m):
        lo_, hi_ = SPANS[m]
        return kappa[lo_:hi_, l : l + 1]

    def bias(l, m):
        lo_, hi_ = SPANS[m]
        return bias_col[lo_:hi_, l : l + 1]

    keep_out = []

    def save(src, dst):
        copy = pltpu.make_async_copy(src, dst, out_sems.at[len(keep_out)])
        copy.start()
        keep_out.append(copy)

    for l in range(LAYERS):
        bias_col[:, l : l + 1] = row_to_col(biases[l : l + 1, :])
    load_d.wait()
    load_r.wait()

    def begin(i, carry):
        for v in range(8):
            x = load_cells(photo_d.at[i], v)
            dflow[i, :, at(v)] = x
            cells[0, i, :, at(v)] = pair_elu(x)
            rflow[i, :, at(v)] = load_cells(photo_r.at[i], v)
        return carry

    wait(0, D1, "z")
    start(0, D1, "x")
    start(0, D2B, "z")
    wait(0, D2A, "z")
    start(0, D2A, "x")
    lax.fori_loop(0, n, begin, 0)
    save(cells.at[0], cells_o.at[0])
    wait(0, D1, "x")
    start(0, D1, "core")
    start(0, RT, "z")
    wait(0, D2A, "x")
    start(0, D2A, "y")
    wait(0, D1, "core")

    def finish(flow, photo, i, carry):
        for v in range(8):
            store_bf16(photo.at[i], v, flow[i, :, at(v)])
        return carry

    def part_a(l, hooks):
        unpack_d1(l)
        set_scale(l, 0, block_square_sum(wd.at[l], C2, 480))

        def body(i, carry):
            for v in range(8):
                put_down(ext, v, cells[l, i, :, at(v)])
            for j in range(4):
                acc = down_product(wd.at[l], C2, C, ext, j)
                for h in range(2):
                    v = 2 * j + h
                    actd[l, i, :, at(v)] = pair_elu(acc[:, at(h)] * scale(l, 0) + bias(l, 0))
            for k, hook in hooks.items():
                pl.when(i == k)(hook)
            return carry

        lax.fori_loop(0, n, body, 0)
        save(actd.at[l], actd_o.at[l])

    def part_b(l, hooks):
        unpack_d2(l)
        set_scale(l, 1, block_square_sum(wd.at[l], 0, C2))
        save(wd.at[l], wd_o.at[l])

        def body(i, carry):
            for v in range(8):
                put_down(ext, v, actd[l, i, :, at(v)])
            for j in range(4):
                acc = down_product(wd.at[l], 0, C2, ext, j)
                for h in range(2):
                    v = 2 * j + h
                    gate = acc[:, at(h)] * scale(l, 1) + bias(l, 1)
                    t = gate[:C]
                    s = sigmoid(gate[C:])
                    gated[l, i, :C, at(v)] = t.astype(BF)
                    gated[l, i, C:, at(v)] = s.astype(BF)
                    new = dflow[i, :, at(v)] + t * s
                    dflow[i, :, at(v)] = new
                    cells[l + 1, i, :, at(v)] = pair_elu(new)
            for k, hook in hooks.items():
                pl.when(i == k)(hook)
            return carry

        lax.fori_loop(0, n, body, 0)
        save(gated.at[l], gated_o.at[l])
        save(cells.at[l + 1], cells_o.at[l + 1])
        if l == LAYERS - 1:
            lax.fori_loop(0, n, functools.partial(finish, dflow, photo_d), 0)
            save(photo_d, down_out)

    def part_c(l, hooks):
        unpack_rt(l)
        total = square_sum(right_t[l])
        set_scale(l, 2, total[C2:])
        set_scale(l, 3, square_sum(skip_t[l]))
        set_scale(l, 4, total[:C2])
        save(wr.at[l], wr_o.at[l])
        save(wk.at[l], wk_o.at[l])

        def body(i, carry):
            for v in range(8):
                act = pair_elu(rflow[i, :, at(v)])
                actr[l, i, :, at(v)] = act
                put_right(ext4, v, act)
            skip_bias = bias(l, 2) + bias(l, 3)
            for j in range(4):
                acc = nn(right_t[l, C2:], ext4[:, j * 256 : j * 256 + 256]) * scale(l, 2)
                acc = acc + nn(skip_t[l], cells[l + 1, i, :, j * 256 : j * 256 + 256]) * scale(l, 3)
                for h in range(2):
                    v = 2 * j + h
                    acth[l, i, :, at(v)] = pair_elu(acc[:, at(h)] + skip_bias)
            for v in range(8):
                put_right(ext4, v, acth[l, i, :, at(v)])
            for j in range(4):
                acc = nn(right_t[l, :C2], ext4[:, j * 256 : j * 256 + 256])
                for h in range(2):
                    v = 2 * j + h
                    gate = acc[:, at(h)] * scale(l, 4) + bias(l, 4)
                    t = gate[:C]
                    s = sigmoid(gate[C:])
                    gater[l, i, :C, at(v)] = t.astype(BF)
                    gater[l, i, C:, at(v)] = s.astype(BF)
                    new = rflow[i, :, at(v)] + t * s
                    rflow[i, :, at(v)] = new
            for k, hook in hooks.items():
                pl.when(i == k)(hook)
            return carry

        lax.fori_loop(0, n, body, 0)
        save(actr.at[l], actr_o.at[l])
        save(acth.at[l], acth_o.at[l])
        save(gater.at[l], gater_o.at[l])
        if l == LAYERS - 1:
            lax.fori_loop(0, n, functools.partial(finish, rflow, photo_r), 0)
            save(photo_r, right_out)

    last = n - 1

    def a0_first():
        wait(0, D2B, "z")
        start(0, D2B, "x")

    def a0_last():
        wait(0, D2A, "y")
        start(0, D2A, "core")
        wait(0, D2B, "x")
        start(0, D2B, "core")
        wait(0, RT, "z")
        start(0, RT, "x")
        start(1, D1, "z")
        start(1, D2A, "z")

    def b0_mid():
        wait(1, D1, "z")
        start(1, D1, "x")
        wait(1, D2A, "z")
        start(1, D2A, "x")
        start(1, D2B, "z")

    def b0_last():
        wait(0, RT, "x")
        start(0, RT, "core")
        wait(1, D2B, "z")
        start(1, D2B, "x")
        start(1, RT, "z")

    def c0_first():
        wait(1, D1, "x")
        start(1, D1, "core")
        wait(1, D2A, "x")
        start(1, D2A, "y")

    def c0_last():
        wait(1, D2B, "x")
        start(1, D2B, "core")
        wait(1, D2A, "y")
        start(1, D2A, "core")
        wait(1, RT, "z")
        start(1, RT, "x")

    def b1_last():
        wait(1, RT, "x")
        start(1, RT, "core")

    part_a(0, {0: a0_first, last: a0_last})
    wait(0, D2A, "core")
    wait(0, D2B, "core")
    part_b(0, {1: b0_mid, last: b0_last})
    wait(0, RT, "core")
    part_c(0, {0: c0_first, last: c0_last})
    wait(1, D1, "core")
    part_a(1, {})
    wait(1, D2A, "core")
    wait(1, D2B, "core")
    part_b(1, {last: b1_last})
    wait(1, RT, "core")
    part_c(1, {})
    for copy in keep_out:
        copy.wait()


def run_forward_gather(down_in, right_in, v1, v2, r1, vs, r2, gains, biases):
    n = down_in.shape[0]
    sds = jax.ShapeDtypeStruct
    vmem = pl.BlockSpec(memory_space=pltpu.VMEM)
    hbm = pl.BlockSpec(memory_space=pl.ANY)
    act = (LAYERS, n, C2, PX)
    kept = [(LAYERS + 1, n, C2, PX)] + [act] * 5
    weights = [(LAYERS, 8, 480, 256), (LAYERS, 1280, 512), (LAYERS, C2, C)]
    photo = (n, 32, 32, C)
    return pl.pallas_call(
        forward_kernel,
        in_specs=[hbm] * 2 + [vmem] * 7,
        out_specs=[hbm] * 11 + [vmem],
        out_shape=[sds(photo, BF)] * 2 + [sds(s, BF) for s in kept + weights] + [sds((1120, 2), F32)],
        scratch_shapes=[pltpu.VMEM(s, BF) for s in kept + weights]
        + [
            pltpu.VMEM((LAYERS, 2, 2, HI) + PIECE[D1], BF),
            pltpu.VMEM((LAYERS, 2, 2, 2, HI) + PIECE[D2A], BF),
            pltpu.VMEM((LAYERS, 2, 2, HI) + PIECE[D2B], BF),
            pltpu.VMEM((LAYERS, 2, 2, HI) + PIECE[RT], BF),
            pltpu.VMEM((LAYERS, 480, 256), BF),
            pltpu.VMEM((LAYERS, 4, 40, 256), BF),
            pltpu.VMEM((LAYERS, 224, 512), BF),
            pltpu.VMEM((LAYERS, 480, 1280), BF),
            pltpu.VMEM((LAYERS, C, C2), BF),
            pltpu.VMEM((960, 1152), BF),
            pltpu.VMEM((1280, PX), BF),
            pltpu.VMEM((n, C, PX), F32),
            pltpu.VMEM((n, C, PX), F32),
            pltpu.VMEM(photo, BF),
            pltpu.VMEM(photo, BF),
            pltpu.VMEM((1120, LAYERS), F32),
            pltpu.SemaphoreType.DMA((48,)),
            pltpu.SemaphoreType.DMA((48,)),
            pltpu.SemaphoreType.DMA((2,)),
            pltpu.SemaphoreType.DMA((32,)),
        ],
        compiler_params=pltpu.CompilerParams(
            vmem_limit_bytes=62 << 20, collective_id=0, has_side_effects=True
        ),
        name="forward_gather",
    )(down_in, right_in, v1, v2, r1, vs, r2, gains, biases)


RG, DA, DB, DC = 0, 1, 2, 3
KINDS = (RG, DA, DB, DC)
ROWS = {RG: 56, DA: 24, DB: 24, DC: 24}
X_FIRST = {RG: True, DA: True, DB: False, DC: False}


def place(kind, k, q):
    core, y = divmod(q, 2)
    hi, lo = divmod(k, 2)
    return (core, lo, y, hi) if X_FIRST[kind] else (core, y, lo, hi)


def put_rows(out, kind, k, tile, row, lanes):
    high = ROWS[kind]
    done = 0
    while done < tile.shape[0]:
        q, r = divmod(row + done, high)
        size = min(high - r, tile.shape[0] - done)
        out[place(kind, k, q) + (slice(r, r + size), lanes)] = tile[done : done + size]
        done += size


def pack_down(out, kind, acc, width, first):
    for k in range(8):
        parts = []
        for p in range(3):
            tap, chan = divmod(240 * k + 80 * p, C2)
            a, c = divmod(tap, 3)
            lo = c * width + first
            parts.append(acc[a, chan : chan + 80, lo : lo + C])
        put_rows(out, kind, k, jnp.concatenate(parts, axis=1).astype(BF), 0, slice(0, 480))


def pack_right(out, gr2, gr1, gs):
    for k in range(8):
        t, half = divmod(k, 2)
        row = slice(half * C, (half + 1) * C)
        part = jnp.concatenate([gr2[row, t * C2 : (t + 1) * C2], gr1[row, t * C : (t + 1) * C]], axis=1)
        put_rows(out, RG, k, part.astype(BF), 0, slice(0, 480))
        put_rows(out, RG, k, gs[40 * k : 40 * k + 40].astype(BF), C, slice(0, C))


def dot_rows(weight, grad, width, count):
    row = jnp.sum(weight.astype(F32) * grad, axis=0, keepdims=True)
    return sum(row[:, k * width : (k + 1) * width] for k in range(count))


def right_taps(wr, br1, br2):
    for t in range(4):
        rows = wr[t * C2 : (t + 1) * C2, :480]
        br2[:, t * C2 : (t + 1) * C2] = rows[:, :C2]
        br1[:, t * C : (t + 1) * C] = rows[:, C2:]


def down_taps(wd, b1, b2):
    for k in range(8):
        rows = wd[k, :, :240].T
        for p in range(3):
            tap, chan = divmod(240 * k + 80 * p, C2)
            a, c = divmod(tap, 3)
            b2[a, chan : chan + 80, c * C2 : (c + 1) * C2] = rows[80 * p : 80 * p + 80, :C2]
            b1[a, chan : chan + 80, c * C : (c + 1) * C] = rows[80 * p : 80 * p + 80, C2:]


def sum_stage(kind, stage, sems, first, g, own, bufs, ids):
    me, grp, hi, lo, y, core = ids
    t1, t2, t3, t4, fin = bufs
    to_x = (hi * 2 + 1 - lo, grp)
    to_y = (me, (1 - y) * 2 + core)
    f, s, to_f, to_s = (lo, y, to_x, to_y) if X_FIRST[kind] else (y, lo, to_y, to_x)
    if stage == 0:
        return [send(g.at[1 - core], t1, sems, first, (me, y * 2 + 1 - core))]
    if stage == 1:
        return [send(t1.at[1 - f], t2, sems, first + 1, to_f)]
    if stage == 2:
        return [send(t2.at[1 - s], t3, sems, first + 2, to_s)]
    if stage == 3:
        return [
            send(t3.at[lax.rem(hi + k, HI)], t4.at[k - 1], sems, first + 2 + k, (lax.rem(hi + k, HI) * 2 + lo, grp))
            for k in range(1, HI)
        ]
    mine = fin.at[core, y]
    return [send(mine, mine, sems, first + 2 + HI + k - 1, (me, lax.rem(grp + k, 4))) for k in range(1, 4)]


def sum_adds(kind, stage, own, bufs, ids):
    me, grp, hi, lo, y, core = ids
    t1, t2, t3, t4, fin = bufs
    f, s = (lo, y) if X_FIRST[kind] else (y, lo)
    if stage == 1:
        add_into(t1, own)
    if stage == 2:
        add_into(t2, t1.at[f])
    if stage == 3:
        add_into(t3, t2.at[s])
    if stage == 4:
        total = t3[hi].astype(F32)
        for k in range(1, HI):
            total = total + t4[k - 1].astype(F32)
        fin[core, y] = total.astype(BF)


def lower_kernel(
    down_g, right_g, cells_g, cells, actd, actr, acth, gated, gater, wd_in, wr_in, wk_in, u0, u1, u2, u3,
    kappa, rows1, gains, v1, v2, r1, vs, r2,
    down_grad, right_grad, o1, o2, or1, os, or2, ogain, obias,
    *scratch,
):
    scratch = list(scratch)

    def take(count):
        out = scratch[:count]
        del scratch[:count]
        return out

    gdown, gright, gcells, low, high, xd, xr, xh, gtd, gtr, wd, wr, wk = take(13)
    b1, b2, br1, br2, g1, g2, gr1, gr2, gs, bsum = take(10)
    ext, ext1, ext41, dskip, dhd, photo = take(6)
    packed = take(4)
    own = take(4)
    bufs = {(l, kind): take(5) for l in range(LAYERS) for kind in KINDS}
    near_rows, far_rows, send_sems, recv_sems, row_send, row_recv, in_sems, out_sems = take(8)
    n = gdown.shape[0]
    ids = peers(HI)
    me, grp, hi, lo, y, core = ids
    sems = (send_sems, recv_sems)
    rsems = (row_send, row_recv)
    upper = [u0, u1, u2, u3]

    loads = {}
    for src, dst, name in (
        (wr_in.at[0], wr, "wr"),
        (wk_in.at[0], wk, "wk"),
        (gater.at[0], gtr, "gtr"),
        (right_g, gright, "gright"),
        (acth.at[0], xh, "xh"),
        (actr.at[0], xr, "xr"),
        (cells.at[1], high, "high"),
        (cells_g, gcells, "gcells"),
        (down_g, gdown, "gdown"),
        (u0.at[core], own[0], "own0"),
        (u1.at[core], own[1], "own1"),
        (u2.at[core], own[2], "own2"),
        (u3.at[core], own[3], "own3"),
        (wd_in.at[0], wd, "wd"),
        (gated.at[0], gtd, "gtd"),
        (actd.at[0], xd, "xd"),
        (cells.at[0], low, "low"),
    ):
        loads[name] = pltpu.make_async_copy(src, dst, in_sems.at[len(loads)])
        loads[name].start()

    def need(*names):
        for name in names:
            loads[name].wait()

    meet(*ids, True)

    def copies(l, kind, stage):
        g = upper[kind] if l else packed[kind]
        return sum_stage(kind, stage, sems, (l * 4 + kind) * 9, g, None, bufs[l, kind], ids)

    def wait(l, kind, stage):
        wait_all(copies(l, kind, stage))

    def start(l, kind, stage):
        mine = own[kind] if l else packed[kind].at[core]
        sum_adds(kind, stage, mine, bufs[l, kind], ids)
        start_all(copies(l, kind, stage))

    def step(l, kind, stage):
        wait(l, kind, stage - 1)
        start(l, kind, stage)

    for kind in KINDS:
        start(1, kind, 0)

    def scale(m):
        lo_, hi_ = SPANS[m]
        return kappa[lo_:hi_, 0:1]

    def add_bias(m, total):
        lo_, hi_ = SPANS[m]
        bsum[lo_:hi_, :] += total

    for acc in (g1, g2, gr1, gs, gr2, bsum):
        acc[...] = jnp.zeros(acc.shape, F32)
    need("wr", "wk")
    right_taps(wr, br1, br2)
    need("gtr", "gright", "xh", "xr", "high", "gcells", "gdown")
    ext4 = ext.at[:, :PX]

    def right_part(i, carry):
        total = None
        for v in range(8):
            d = gate_back(
                gright[i, :, at(v)], gtr[i, :C, at(v)].astype(F32), gtr[i, C:, at(v)].astype(F32)
            )
            total = d if total is None else total + d
            put_right_back(ext4, v, (d * scale(4)).astype(BF))
        add_bias(4, total)
        gr2[...] += nt(xh[i], ext4[...])
        total = None
        for j in range(4):
            e = nn(br2[...], ext4[:, j * 256 : j * 256 + 256])
            for h in range(2):
                v = 2 * j + h
                d = elu_back(e[:, at(h)], xh[i, :, at(v)])
                total = d if total is None else total + d
                put_right_back(ext41, v, (d * scale(2)).astype(BF))
                dskip[:, at(v)] = (d * scale(3)).astype(BF)
        add_bias(2, total)
        add_bias(3, total)
        gr1[...] += nt(xr[i], ext41[...])
        gs[...] += nt(high[i], dskip[...])
        for j in range(4):
            e = nn(br1[...], ext41[:, j * 256 : j * 256 + 256])
            k = nn(wk[...], dskip[:, j * 256 : j * 256 + 256])
            for h in range(2):
                v = 2 * j + h
                gright[i, :, at(v)] += elu_back(e[:, at(h)], xr[i, :, at(v)])
                gc = k[:, at(h)] + gcells[i, :, at(v)].astype(F32)
                gdown[i, :, at(v)] += elu_back(gc, high[i, :, at(v)])

        @pl.when(i == 0)
        def _():
            step(1, RG, 1)
            step(1, DB, 1)
            step(1, DA, 1)
            step(1, DC, 1)

        return carry

    need("own0", "own1", "own2", "own3")
    lax.fori_loop(0, n, right_part, 0)
    pack_right(packed[RG], gr2, gr1, gs)
    start(0, RG, 0)
    step(1, DB, 2)
    step(1, DA, 2)
    step(1, RG, 2)

    def finish(flow, i, carry):
        for v in range(8):
            store_f32(photo.at[i], v, flow[i, :, at(v)])
        return carry

    lax.fori_loop(0, n, functools.partial(finish, gright), 0)
    out_right = pltpu.make_async_copy(photo, right_grad, out_sems.at[0])
    out_right.start()
    need("wd")
    down_taps(wd, b1, b2)
    need("gtd", "xd")
    step(0, RG, 1)

    def down_part(i, carry):
        total = None
        for v in range(8):
            d = gate_back(
                gdown[i, :, at(v)], gtd[i, :C, at(v)].astype(F32), gtd[i, C:, at(v)].astype(F32)
            )
            total = d if total is None else total + d
            put_down_back(ext, v, (d * scale(1)).astype(BF))
        add_bias(1, total)
        for a in range(2):
            first = 128 * (1 - a)
            g2[a] += nt(xd[i], ext[:960, first : first + PX])
        total = None
        for j in range(4):
            e = nn(b2[1], ext[:960, j * 256 : j * 256 + 256])
            e = e + nn(b2[0], ext[:960, j * 256 + 128 : j * 256 + 384])
            for h in range(2):
                v = 2 * j + h
                d = elu_back(e[:, at(h)], xd[i, :, at(v)])
                total = d if total is None else total + d
                dhd[i, :, at(v)] = (d * scale(0)).astype(BF)
        add_bias(0, total)

        @pl.when(i == 0)
        def _():
            step(1, DB, 3)
            step(1, DA, 3)
            step(1, DC, 2)
            step(1, RG, 3)

        @pl.when(i == 1)
        def _():
            step(1, DC, 3)

        return carry

    lax.fori_loop(0, n, down_part, 0)
    pack_down(packed[DA], DA, g2, C2, 0)
    start(0, DA, 0)
    pack_down(packed[DB], DB, g2, C2, C)
    start(0, DB, 0)
    step(1, DB, 4)
    step(1, DA, 4)
    step(1, RG, 4)
    step(1, DC, 4)
    need("low")

    def first_part(i, carry):
        for v in range(8):
            put_down_back(ext1, v, dhd[i, :, at(v)])
        for a in range(2):
            first = 128 * (1 - a)
            g1[a] += nt(low[i], ext1[:, first : first + PX])
        return carry

    lax.fori_loop(0, n, first_part, 0)
    step(0, RG, 2)
    step(0, DA, 1)
    step(0, DB, 1)
    pack_down(packed[DC], DC, g1, C, 0)
    start(0, DC, 0)
    dots = jnp.concatenate(
        [
            dot_rows(b1[0], g1[0], C, 3) + dot_rows(b1[1], g1[1], C, 3),
            dot_rows(b2[0], g2[0], C2, 3) + dot_rows(b2[1], g2[1], C2, 3),
            dot_rows(br1[...], gr1[...], C, 4),
            dot_rows(wk[...], gs[...], C, 1),
            dot_rows(br2[...], gr2[...], C2, 4),
        ],
        axis=1,
    )
    near_rows[grp] = jnp.zeros((8, 1152), F32)
    near_rows[grp, 0:1, :1120] = dots
    near_rows[grp, 1:2, :1120] = rows1[0:1, :]
    near_rows[grp, 2:3, :1120] = jnp.sum(bsum[...].T, axis=0, keepdims=True)
    near_rows[grp, 3:4, :1120] = rows1[1:2, :]
    mine = near_rows.at[grp]
    near = [send(mine, mine, rsems, k - 1, (me, lax.rem(grp + k, 4))) for k in range(1, 4)]
    start_all(near)
    out_right.wait()
    step(0, DC, 1)

    def last_part(i, carry):
        for v in range(8):
            put_down_back(ext1, v, dhd[i, :, at(v)])
        for j in range(4):
            e = nn(b1[1], ext1[:, j * 256 : j * 256 + 256])
            e = e + nn(b1[0], ext1[:, j * 256 + 128 : j * 256 + 384])
            for h in range(2):
                v = 2 * j + h
                gdown[i, :, at(v)] += elu_back(e[:, at(h)], low[i, :, at(v)])

        @pl.when(i == 0)
        def _():
            wait_all(near)
            far_rows[me] = near_rows[0] + near_rows[1] + near_rows[2] + near_rows[3]
            start_all(far())

        return carry

    def far():
        part = far_rows.at[me]
        return [
            send(part, part, rsems, 2 + k, (lax.rem(me + k, 2 * HI), grp)) for k in range(1, 2 * HI)
        ]

    lax.fori_loop(0, n, last_part, 0)
    step(0, DA, 2)
    step(0, RG, 3)
    step(0, DB, 2)
    step(0, DC, 2)
    lax.fori_loop(0, n, functools.partial(finish, gdown), 0)
    out_down = pltpu.make_async_copy(photo, down_grad, out_sems.at[1])
    out_down.start()
    for kind in KINDS:
        wait(1, kind, 4)
    wait_all(far())
    total = far_rows[0]
    for k in range(1, 2 * HI):
        total = total + far_rows[k]
    obias[...] = total[2:4, :1120]
    ogain[...] = total[0:2, :1120] / gains[...]

    def factors(l):
        recip = col_to_row(kappa[:, l : l + 1]) / gains[l : l + 1, :]
        row = recip * recip * total[l : l + 1, :1120]
        return row, row_to_col(row[:, : SPANS[1][1]])

    def write_right(l, row):
        right = quarters(bufs[l, RG][4], RG)
        or1[l] = right[:C, C2:480] - r1[l].astype(F32) * row[:, SPANS[2][0] : SPANS[2][1]]
        os[l] = right[C:200, :C] - vs[l].astype(F32) * row[:, SPANS[3][0] : SPANS[3][1]]
        or2[l] = right[:C, :C2] - r2[l].astype(F32) * row[:, SPANS[4][0] : SPANS[4][1]]

    def turned(l, kind):
        flat = quarters(bufs[l, kind][4], kind).T
        return jnp.concatenate([flat[C * p : C * (p + 1), :80] for p in range(3)], axis=1)

    def write_down(l, kind, col):
        if kind == DC:
            o1[l] = turned(l, kind) - v1[l].astype(F32) * col[:C]
        else:
            first = 0 if kind == DA else C
            part = slice(first, first + C)
            o2[l, part] = turned(l, kind) - v2[l, part].astype(F32) * col[C + first : C2 + first]

    row_1, col_1 = factors(1)
    row_0, col_0 = factors(0)
    step(0, DA, 3)
    step(0, RG, 4)
    step(0, DB, 3)
    step(0, DC, 3)
    write_right(1, row_1)
    for kind in (DA, DB, DC):
        write_down(1, kind, col_1)
    step(0, DA, 4)
    step(0, DB, 4)
    step(0, DC, 4)
    wait(0, RG, 4)
    write_right(0, row_0)
    for kind in (DA, DB, DC):
        wait(0, kind, 4)
        write_down(0, kind, col_0)
    out_down.wait()


def sum_shape(kind):
    return (2, 2, 2, HI, ROWS[kind], 512)


def run_lower(down_g, right_g, cells_g, kept, kappa, weights, upper, rows1, gains, v1, v2, r1, vs, r2):
    n = down_g.shape[0]
    sds = jax.ShapeDtypeStruct
    vmem = pl.BlockSpec(memory_space=pltpu.VMEM)
    hbm = pl.BlockSpec(memory_space=pl.ANY)
    photo = (n, 32, 32, C)
    V = pltpu.VMEM
    wide = V((n, C2, PX), BF)
    scratch = [V((n, C, PX), F32)] * 2 + [wide] * 8 + [V((8, 480, 256), BF), V((1280, 512), BF), V((C2, C), BF)]
    scratch += [V((2, C2, 480), BF), V((2, C2, 960), BF), V((C2, 640), BF), V((C2, 1280), BF)]
    scratch += [V((2, C2, 480), F32), V((2, C2, 960), F32), V((C2, 640), F32), V((C2, 1280), F32), V((C2, C), F32)]
    scratch += [V((1120, 128), F32)]
    scratch += [V((1280, 1152), BF), V((480, 1152), BF), V((640, PX), BF), V((C, PX), BF), V((n, C, PX), BF), V(photo, F32)]
    scratch += [V(sum_shape(kind), BF) for kind in KINDS]
    scratch += [V(sum_shape(kind)[1:], BF) for kind in KINDS]
    for l in range(LAYERS):
        for kind in KINDS:
            tail = (ROWS[kind], 512)
            scratch += [
                V((2, 2, HI) + tail, BF),
                V((2, HI) + tail, BF),
                V((HI,) + tail, BF),
                V((HI - 1,) + tail, BF),
                V((2, 2) + tail, BF),
            ]
    sem = pltpu.SemaphoreType.DMA
    scratch += [V((4, 8, 1152), F32), V((2 * HI, 8, 1152), F32), sem((72,)), sem((72,)), sem((10,)), sem((10,)), sem((17,)), sem((2,))]
    return pl.pallas_call(
        lower_kernel,
        in_specs=[hbm] * 16 + [vmem] * 8,
        out_specs=[hbm] * 2 + [vmem] * 7,
        out_shape=[sds(photo, F32)] * 2 + [sds(v.shape, F32) for v in (v1, v2, r1, vs, r2)] + [sds((LAYERS, 1120), F32)] * 2,
        scratch_shapes=scratch,
        compiler_params=pltpu.CompilerParams(
            vmem_limit_bytes=63 << 20, collective_id=1, has_side_effects=True
        ),
        name="lower",
    )(down_g, right_g, cells_g, *kept, *weights, *upper, kappa, rows1, gains, v1, v2, r1, vs, r2)


def general_finish(lower, upper, whole_v, shards, gains):
    rows = lax.psum(jnp.stack([lower[4], upper[4]]), ("dp", "grp"))
    sums = []
    units = []
    inverse = []
    for m, (low, high) in enumerate(zip(unpack(*lower[:4]), unpack(*upper[:4]))):
        part = lax.psum_scatter(jnp.stack([low, high]), "dp", scatter_dimension=1, tiled=True)
        sums.append(lax.psum(part, "grp").astype(F32))
        vals = whole_v[m].astype(F32)
        inv = lax.rsqrt(jnp.sum(vals * vals, axis=1))
        inverse.append(inv)
        units.append(shards[m].astype(F32) * inv[:, None, :])
    inverse = jnp.concatenate(inverse, axis=1)
    dots = rows[:, 0] * inverse
    grads = [sums[m] - units[m] * dots[:, None, lo:hi] for m, (lo, hi) in enumerate(SPANS)]
    return (*grads, rows[:, 0] / gains, rows[:, 1])


def on_device(
    quick,
    down_in,
    right_in,
    pixel_mask,
    down_cot,
    right_cot,
    v_down1,
    v_down2,
    v_right1,
    v_skip,
    v_right2,
    gains,
    biases,
):
    shards = (v_down1, v_down2, v_right1, v_skip, v_right2)
    turned = (v_down1.swapaxes(1, 2), v_down2.swapaxes(1, 2), v_right1, v_skip, v_right2)
    n = down_in.shape[0]
    if quick:
        down_out, right_out, *rest = run_forward_gather(down_in, right_in, *turned, gains, biases)
        kept, weights, kappa = rest[:6], rest[6:9], rest[9]
    else:
        whole_v = tuple(lax.all_gather(v, "dp", axis=1, tiled=True) for v in shards)
        weights = assemble(*whole_v)
        cols = jnp.concatenate([gains, biases], axis=0).T
        down_out, right_out, *kept, kappa = run_forward(down_in, right_in, *weights, cols)
    mask = pixel_mask.reshape(n, 4, 8, 32).transpose(0, 2, 1, 3).reshape(n, 1, 1024).astype(F32)
    down_g, right_g, cells_g, *upper = run_backward(1, down_cot, right_cot, None, mask, kept, kappa, *weights)
    if quick:
        down_grad, right_grad, *grads = run_lower(
            down_g, right_g, cells_g, kept, kappa, weights, upper[:4], upper[4], gains, *turned
        )
        grads[0] = grads[0].swapaxes(1, 2)
        grads[1] = grads[1].swapaxes(1, 2)
    else:
        down_grad, right_grad, *lower = run_backward(0, down_g, right_g, cells_g, mask, kept, kappa, *weights)
        grads = general_finish(lower, upper, whole_v, shards, gains)
    return (down_out, right_out, down_grad, right_grad, *grads)


def solution(mesh):
    photo = P(("dp", "grp"), None, None, None)
    rows = P(None, "dp", None)
    quick = mesh.shape["dp"] == 2 * HI and mesh.shape["grp"] == 4
    return jax.shard_map(
        functools.partial(on_device, quick),
        mesh=mesh,
        in_specs=(photo, photo, P(("dp", "grp"), None, None), photo, photo) + (rows,) * 5 + (P(), P()),
        out_specs=(photo,) * 4 + (rows,) * 5 + (P(), P()),
        check_vma=False,
    )
```

```python
import functools
import jax
import jax.numpy as jnp
from jax import lax
from jax.experimental import pallas as pl
from jax.experimental.pallas import tpu as pltpu
from jax.sharding import PartitionSpec as P

BF = jnp.bfloat16
F32 = jnp.float32
LAYERS = 2
HI = 4
MESH = pl.DeviceIdType.MESH
C = 160
C2 = 320
SPANS = ((0, 160), (160, 480), (480, 640), (640, 800), (800, 1120))


def nt(a, b):
    return lax.dot_general(a, b, (((1,), (1,)), ((), ())), preferred_element_type=F32)


def nn(a, b):
    return lax.dot_general(a, b, (((1,), (0,)), ((), ())), preferred_element_type=F32)


def eye(n):
    same = lax.broadcasted_iota(jnp.int32, (n, n), 0) == lax.broadcasted_iota(jnp.int32, (n, n), 1)
    return jnp.where(same, 1.0, 0.0).astype(BF)


def lane():
    return lax.broadcasted_iota(jnp.int32, (1, 128), 1)


def keep(cond, tile):
    return jnp.where(cond, tile, jnp.zeros((), tile.dtype))


def col_shift(tile, off):
    if off == 0:
        return tile
    col = lane() & 31
    if off == 1:
        return keep(col != 31, pltpu.roll(tile, 127, 1))
    return keep(col != 0, pltpu.roll(tile, 1, 1))


def row_before(tile):
    return keep(lane() >= 32, pltpu.roll(tile, 32, 1))


def row_after(tile):
    return keep(lane() < 96, pltpu.roll(tile, 96, 1))


def at(v):
    return slice(v * 128, (v + 1) * 128)


def put_down(ext, v, tile):
    n = tile.shape[0]
    for c in range(3):
        moved = col_shift(tile, c - 1)
        ext[c * n : (c + 1) * n, at(v + 1)] = moved
        if v == 7:
            ext[c * n : (c + 1) * n, at(0)] = row_before(moved)


def put_right(ext, v, tile):
    n = tile.shape[0]
    for c in range(2):
        moved = col_shift(tile, c - 1)
        ext[(2 + c) * n : (3 + c) * n, at(v)] = moved
        if v == 7:
            ext[c * n : (c + 1) * n, at(0)] = row_before(moved)
        else:
            ext[c * n : (c + 1) * n, at(v + 1)] = moved


def put_down_back(ext, v, tile):
    n = tile.shape[0]
    for c in range(3):
        moved = col_shift(tile, 1 - c)
        ext[c * n : (c + 1) * n, at(v)] = moved
        if v == 0:
            ext[c * n : (c + 1) * n, at(8)] = row_after(moved)


def put_right_back(ext, v, tile):
    n = tile.shape[0]
    for c in range(2):
        moved = col_shift(tile, 1 - c)
        ext[(2 + c) * n : (3 + c) * n, at(v)] = moved
        if v == 0:
            ext[c * n : (c + 1) * n, at(7)] = row_after(moved)
        else:
            ext[c * n : (c + 1) * n, at(v - 1)] = moved


def pair_elu(x):
    e = jnp.exp(-jnp.abs(x)) - 1.0
    up = x > 0
    return jnp.concatenate([jnp.where(up, x, e), jnp.where(up, e, -x)], axis=0).astype(BF)


def elu_back(grad, act):
    slope = jnp.minimum(act.astype(F32), 0.0) + 1.0
    both = grad * slope
    return both[:C] - both[C:]


def sigmoid(x):
    return 1.0 / (1.0 + jnp.exp(-x))


def load_cells(ref, v):
    rows = jnp.concatenate([ref[g * 8 + v] for g in range(4)], axis=0)
    return rows.T.astype(F32)


def store_bf16(ref, v, tile):
    out = tile.astype(BF).T
    for g in range(4):
        ref[g * 8 + v] = out[g * 32 : (g + 1) * 32]


def store_f32(ref, v, tile):
    out = tile.T
    for g in range(4):
        ref[g * 8 + v] = out[g * 32 : (g + 1) * 32]


def scale_of(total, gain):
    return gain * lax.rsqrt(total)


def square_sum(vals):
    vals = vals.astype(F32)
    return jnp.sum(vals * vals, axis=1, keepdims=True)


def block_square_sum(weight, lo, hi):
    total = None
    for k in range(8):
        vals = weight[k, lo:hi, :240].astype(F32)
        total = vals * vals if total is None else total + vals * vals
    return jnp.sum(total, axis=1, keepdims=True)


def down_product(weight, first, count, ext, j):
    acc = None
    for k in range(8):
        lo = j * 256 + 128 * (k // 4)
        part = nn(weight[k, first : first + count, :240], ext[240 * (k % 4) : 240 * (k % 4) + 240, lo : lo + 256])
        acc = part if acc is None else acc + part
    return acc


def fwd_kernel(
    down_in, right_in, wd, wr, wk, cols,
    down_out, right_out, cells, actd, actr, acth, gated, gater, kappa,
    right_t, skip_t, ext, ext4, dflow, rflow,
):
    @pl.when(pl.program_id(0) == 0)
    def _():
        for l in range(LAYERS):
            for k in range(4):
                rows = wr[l, k * C2 : (k + 1) * C2, :480]
                right_t[l, :, k * C2 : (k + 1) * C2] = nt(eye(480), rows).astype(BF)
            skip_t[l] = nt(eye(C), wk[l]).astype(BF)
            down_total = sum(square_sum(wd[l, k, :, :240]) for k in range(8))
            right_total = square_sum(right_t[l])
            totals = (down_total[C2:], down_total[:C2], right_total[C2:], square_sum(skip_t[l]), right_total[:C2])
            for total, (lo, hi) in zip(totals, SPANS):
                kappa[lo:hi, l : l + 1] = scale_of(total, cols[lo:hi, l : l + 1])

    for v in range(8):
        x = load_cells(down_in.at[0], v)
        dflow[:, at(v)] = x
        act = pair_elu(x)
        cells[0, 0, :, at(v)] = act
        put_down(ext, v, act)
        rflow[:, at(v)] = load_cells(right_in.at[0], v)
    for l in range(LAYERS):
        def scale(m):
            lo, hi = SPANS[m]
            return kappa[lo:hi, l : l + 1]

        def bias(m):
            lo, hi = SPANS[m]
            return cols[lo:hi, 2 + l : 3 + l]

        for j in range(4):
            acc = down_product(wd.at[l], C2, C, ext, j)
            for h in range(2):
                v = 2 * j + h
                actd[l, 0, :, at(v)] = pair_elu(acc[:, at(h)] * scale(0) + bias(0))
        for v in range(8):
            put_down(ext, v, actd[l, 0, :, at(v)])
            act = pair_elu(rflow[:, at(v)])
            actr[l, 0, :, at(v)] = act
            put_right(ext4, v, act)
        for j in range(4):
            acc = down_product(wd.at[l], 0, C2, ext, j)
            for h in range(2):
                v = 2 * j + h
                gate = acc[:, at(h)] * scale(1) + bias(1)
                t = gate[:C]
                s = sigmoid(gate[C:])
                gated[l, 0, :C, at(v)] = t.astype(BF)
                gated[l, 0, C:, at(v)] = s.astype(BF)
                new = dflow[:, at(v)] + t * s
                dflow[:, at(v)] = new
                cells[l + 1, 0, :, at(v)] = pair_elu(new)
        skip_bias = bias(2) + bias(3)
        for j in range(4):
            acc = nn(right_t[l, C2:], ext4[:, j * 256 : j * 256 + 256]) * scale(2)
            acc = acc + nn(skip_t[l], cells[l + 1, 0, :, j * 256 : j * 256 + 256]) * scale(3)
            for h in range(2):
                v = 2 * j + h
                acth[l, 0, :, at(v)] = pair_elu(acc[:, at(h)] + skip_bias)
        for v in range(8):
            put_right(ext4, v, acth[l, 0, :, at(v)])
            if l + 1 < LAYERS:
                put_down(ext, v, cells[l + 1, 0, :, at(v)])
        for j in range(4):
            acc = nn(right_t[l, :C2], ext4[:, j * 256 : j * 256 + 256])
            for h in range(2):
                v = 2 * j + h
                gate = acc[:, at(h)] * scale(4) + bias(4)
                t = gate[:C]
                s = sigmoid(gate[C:])
                gater[l, 0, :C, at(v)] = t.astype(BF)
                gater[l, 0, C:, at(v)] = s.astype(BF)
                rflow[:, at(v)] = rflow[:, at(v)] + t * s
    for v in range(8):
        store_bf16(down_out.at[0], v, dflow[:, at(v)])
        store_bf16(right_out.at[0], v, rflow[:, at(v)])


def gate_back(g, t, s):
    p = g * s
    q = p * t * (1.0 - s)
    return jnp.concatenate([p, q], axis=0)


def bwd_kernel(
    top, down_g, right_g, mask, *refs,
):
    refs = list(refs)
    cells_g = None if top else refs.pop(0)
    (
        low_cells, high_cells, actd, actr, acth, gated, gater, kappa, wd, wr, wk,
    ) = refs[:11]
    refs = refs[11:]
    if top:
        down_out, right_out, cells_out = refs[:3]
        refs = refs[3:]
    else:
        down_out, right_out = refs[:2]
        refs = refs[2:]
    (
        o_rg, o_da, o_db, o_dc, orows,
        b1, b2, br1, br2, g1, g2, gr1, gs, gr2, bsum, ext, ext1, ext4, ext41, dskip, gdown, gright,
    ) = refs
    layer = 1 if top else 0
    step = pl.program_id(0)

    @pl.when(step == 0)
    def _():
        down_taps(wd.at[0], b1, b2)
        right_taps(wr.at[0], br1, br2)
        for acc in (g1, g2, gr1, gs, gr2, bsum):
            acc[...] = jnp.zeros(acc.shape, F32)

    def scale(m):
        lo, hi = SPANS[m]
        return kappa[lo:hi, layer : layer + 1]

    def add_bias(m, total):
        lo, hi = SPANS[m]
        bsum[lo:hi, :] += total

    total = None
    for v in range(8):
        if top:
            m = mask[0, :, at(v)]
            gdown[:, at(v)] = load_cells(down_g.at[0], v) * m
            g = load_cells(right_g.at[0], v) * m
            gright[:, at(v)] = g
        else:
            g = right_g[0, :, at(v)]
        d = gate_back(g, gater[0, 0, :C, at(v)].astype(F32), gater[0, 0, C:, at(v)].astype(F32))
        total = d if total is None else total + d
        put_right_back(ext4, v, (d * scale(4)).astype(BF))
    add_bias(4, total)
    gr2[...] += nt(acth[0, 0], ext4[...])
    total = None
    for j in range(4):
        e = nn(br2[...], ext4[:, j * 256 : j * 256 + 256])
        for h in range(2):
            v = 2 * j + h
            d = elu_back(e[:, at(h)], acth[0, 0, :, at(v)])
            total = d if total is None else total + d
            put_right_back(ext41, v, (d * scale(2)).astype(BF))
            dskip[:, at(v)] = (d * scale(3)).astype(BF)
    add_bias(2, total)
    add_bias(3, total)
    gr1[...] += nt(actr[0, 0], ext41[...])
    gs[...] += nt(high_cells[0, 0], dskip[...])
    for j in range(4):
        e = nn(br1[...], ext41[:, j * 256 : j * 256 + 256])
        k = nn(wk[0], dskip[:, j * 256 : j * 256 + 256])
        for h in range(2):
            v = 2 * j + h
            old = gright[:, at(v)] if top else right_g[0, :, at(v)]
            new = old + elu_back(e[:, at(h)], actr[0, 0, :, at(v)])
            if top:
                right_out[0, :, at(v)] = new
            else:
                store_f32(right_out.at[0], v, new)
            gc = k[:, at(h)]
            if not top:
                gc = gc + cells_g[0, :, at(v)].astype(F32)
            old = gdown[:, at(v)] if top else down_g[0, :, at(v)]
            gdown[:, at(v)] = old + elu_back(gc, high_cells[0, 0, :, at(v)])
    total = None
    for v in range(8):
        g = gdown[:, at(v)]
        if top:
            down_out[0, :, at(v)] = g
        d = gate_back(g, gated[0, 0, :C, at(v)].astype(F32), gated[0, 0, C:, at(v)].astype(F32))
        total = d if total is None else total + d
        put_down_back(ext, v, (d * scale(1)).astype(BF))
    add_bias(1, total)
    for a in range(2):
        lo = 128 * (1 - a)
        g2[a] += nt(actd[0, 0], ext[:, lo : lo + 1024])
    total = None
    for j in range(4):
        e = nn(b2[1], ext[:, j * 256 : j * 256 + 256])
        e = e + nn(b2[0], ext[:, j * 256 + 128 : j * 256 + 384])
        for h in range(2):
            v = 2 * j + h
            d = elu_back(e[:, at(h)], actd[0, 0, :, at(v)])
            total = d if total is None else total + d
            put_down_back(ext1, v, (d * scale(0)).astype(BF))
    add_bias(0, total)
    for a in range(2):
        lo = 128 * (1 - a)
        g1[a] += nt(low_cells[0, 0], ext1[:, lo : lo + 1024])
    for j in range(4):
        e = nn(b1[1], ext1[:, j * 256 : j * 256 + 256])
        e = e + nn(b1[0], ext1[:, j * 256 + 128 : j * 256 + 384])
        if top:
            cells_out[0, :, j * 256 : j * 256 + 256] = e.astype(BF)
        else:
            for h in range(2):
                v = 2 * j + h
                last = gdown[:, at(v)] + elu_back(e[:, at(h)], low_cells[0, 0, :, at(v)])
                store_f32(down_out.at[0], v, last)

    @pl.when(step == pl.num_programs(0) - 1)
    def _():
        pack_right(o_rg, gr2, gr1, gs)
        pack_down(o_da, DA, g2, C2, 0)
        pack_down(o_db, DB, g2, C2, C)
        pack_down(o_dc, DC, g1, C, 0)
        orows[0:1, :] = jnp.concatenate(
            [
                dot_rows(b1[0], g1[0], C, 3) + dot_rows(b1[1], g1[1], C, 3),
                dot_rows(b2[0], g2[0], C2, 3) + dot_rows(b2[1], g2[1], C2, 3),
                dot_rows(br1[...], gr1[...], C, 4),
                dot_rows(wk[0], gs[...], C, 1),
                dot_rows(br2[...], gr2[...], C2, 4),
            ],
            axis=1,
        )
        orows[1:2, :] = jnp.sum(bsum[...].T, axis=0, keepdims=True)


def whole(shape, dtype=None):
    zeros = (0,) * len(shape)
    return pl.BlockSpec(shape, lambda i: zeros)


def once(shape):
    zeros = (0,) * len(shape)
    return pl.BlockSpec(shape, lambda i: zeros, pipeline_mode=pl.Buffered(1))


def image(shape):
    rest = (0,) * (len(shape) - 1)
    return pl.BlockSpec(shape, lambda i: (i,) + rest)


PX = 1024


def run_forward(down_in, right_in, wd, wr, wk, cols):
    n = down_in.shape[0]
    sds = jax.ShapeDtypeStruct
    kept = [(3, C2, PX)] + [(LAYERS, C2, PX)] * 5
    return pl.pallas_call(
        fwd_kernel,
        grid=(n,),
        in_specs=[image((1, 32, 32, C))] * 2 + [once(w.shape) for w in (wd, wr, wk)] + [once((1120, 4))],
        out_specs=[image((1, 32, 32, C))] * 2
        + [pl.BlockSpec((s[0], 1) + s[1:], lambda i: (0, i, 0, 0)) for s in kept]
        + [once((1120, 2))],
        out_shape=[sds((n, 32, 32, C), BF)] * 2
        + [sds((s[0], n) + s[1:], BF) for s in kept]
        + [sds((1120, 2), F32)],
        scratch_shapes=[
            pltpu.VMEM((LAYERS, 480, 1280), BF),
            pltpu.VMEM((LAYERS, C, C2), BF),
            pltpu.VMEM((960, 1152), BF),
            pltpu.VMEM((1280, PX), BF),
            pltpu.VMEM((C, PX), F32),
            pltpu.VMEM((C, PX), F32),
        ],
        compiler_params=pltpu.CompilerParams(vmem_limit_bytes=60 << 20),
        name="forward",
    )(down_in, right_in, wd, wr, wk, cols)


def run_backward(layer, down_g, right_g, cells_g, mask, kept, kappa, wd, wr, wk):
    n = down_g.shape[0]
    top = layer == 1
    sds = jax.ShapeDtypeStruct
    flow = image((1, C, PX))
    wide = image((1, C2, PX))

    def pick(which):
        return pl.BlockSpec((1, 1, C2, PX), lambda i: (which, i, 0, 0))

    def one_layer(shape):
        rest = (0,) * (len(shape) - 1)
        return pl.BlockSpec((1,) + shape[1:], lambda i: (layer,) + rest, pipeline_mode=pl.Buffered(1))

    cells = kept[0]
    ins = [down_g, right_g, mask] + ([] if top else [cells_g]) + [cells, cells] + list(kept[1:]) + [kappa, wd, wr, wk]
    photo = image((1, 32, 32, C))
    in_specs = (
        ([photo] * 2 if top else [flow] * 2)
        + [image((1, 1, PX))]
        + ([] if top else [wide])
        + [pick(layer), pick(layer + 1)]
        + [pick(layer)] * 5
        + [once((1120, 2))]
        + [one_layer(w.shape) for w in (wd, wr, wk)]
    )
    if top:
        out_specs = [flow, flow, wide]
        out_shape = [sds((n, C, PX), F32)] * 2 + [sds((n, C2, PX), BF)]
    else:
        out_specs = [photo] * 2
        out_shape = [sds((n, 32, 32, C), F32)] * 2
    return pl.pallas_call(
        functools.partial(bwd_kernel, top),
        grid=(n,),
        in_specs=in_specs,
        out_specs=out_specs + [once(sum_shape(kind)) for kind in KINDS] + [once((2, 1120))],
        out_shape=out_shape + [sds(sum_shape(kind), BF) for kind in KINDS] + [sds((2, 1120), F32)],
        scratch_shapes=[
            pltpu.VMEM((2, 320, 480), BF),
            pltpu.VMEM((2, 320, 960), BF),
            pltpu.VMEM((320, 640), BF),
            pltpu.VMEM((320, 1280), BF),
            pltpu.VMEM((2, 320, 480), F32),
            pltpu.VMEM((2, 320, 960), F32),
            pltpu.VMEM((320, 640), F32),
            pltpu.VMEM((320, 160), F32),
            pltpu.VMEM((320, 1280), F32),
            pltpu.VMEM((1120, 128), F32),
            pltpu.VMEM((960, 1152), BF),
            pltpu.VMEM((480, 1152), BF),
            pltpu.VMEM((1280, 1024), BF),
            pltpu.VMEM((640, 1024), BF),
            pltpu.VMEM((160, 1024), BF),
            pltpu.VMEM((C, PX), F32),
            pltpu.VMEM((C, PX), F32),
        ],
        compiler_params=pltpu.CompilerParams(vmem_limit_bytes=60 << 20),
        name="backward%d" % layer,
    )(*ins)


def assemble(v1, v2, r1, vs, r2):
    rows = jnp.concatenate([v2, v1], axis=2).reshape(LAYERS, 8, 240, 480)
    wd = jnp.pad(rows.swapaxes(2, 3), ((0, 0), (0, 0), (0, 0), (0, 16)))
    wr = jnp.pad(jnp.concatenate([r2, r1], axis=2), ((0, 0), (0, 0), (0, 32)))
    return wd, wr, vs


def unpack(*packed):
    blocks = []
    for kind, g in zip(KINDS, packed):
        order = (3, 1, 4, 0, 2, 5) if X_FIRST[kind] else (3, 2, 4, 0, 1, 5)
        blocks.append(g.transpose(order).reshape(8, ROWS[kind], 512))

    def down(block):
        return block[:, :, :480].reshape(8, 80, 3, C).swapaxes(1, 2).reshape(1920, C)

    right = blocks[0][:, :C].reshape(1280, 512)
    tail = blocks[0][:, C:, :480].reshape(8, 16, 3, C).swapaxes(1, 2).reshape(8, 48, C)
    skip = tail[:, :40].reshape(C2, C)
    down2 = jnp.concatenate([down(blocks[1]), down(blocks[2])], axis=1)
    return down(blocks[3]), down2, right[:, C2:480], skip, right[:, :C2]


def peers(hi_count):
    me = lax.axis_index("dp")
    grp = lax.axis_index("grp")
    hi, lo = me // 2, lax.rem(me, 2)
    y, core = grp // 2, lax.rem(grp, 2)
    return me, grp, hi, lo, y, core


def meet(me, grp, hi, lo, y, core, everyone):
    barrier = pltpu.get_barrier_semaphore()
    near = [((hi + k) % HI * 2 + lo, grp) for k in range(1, HI)]
    near += [(hi * 2 + 1 - lo, grp)]
    if everyone:
        near += [((hi + k) % HI * 2 + 1 - lo, grp) for k in range(1, HI)]
    near += [(me, (grp + k) % 4) for k in range(1, 4)]
    for device in near:
        pl.semaphore_signal(barrier, inc=1, device_id=device, device_id_type=MESH)
    pl.semaphore_wait(barrier, len(near))


def send(src, dst, sems, at_, device):
    return pltpu.make_async_remote_copy(
        src_ref=src,
        dst_ref=dst,
        send_sem=sems[0].at[at_],
        recv_sem=sems[1].at[at_],
        device_id=device,
        device_id_type=MESH,
    )


def start_all(copies):
    for copy in copies:
        copy.start()


def wait_all(copies):
    for copy in copies:
        copy.wait()


def add_into(dst, src):
    dst[...] = (dst[...].astype(F32) + src[...].astype(F32)).astype(BF)


def col_to_row(col):
    return jnp.broadcast_to(col, (col.shape[0], 128)).T[0:1, :]


def row_to_col(row):
    return jnp.broadcast_to(row, (128, row.shape[1])).T[:, 0:1]


def quarters(fin):
    return jnp.concatenate([fin[q // 2, q % 2].astype(F32) for q in range(4)], axis=1)


D1, D2A, D2B, RT = 0, 1, 2, 3
PIECE = {D1: (80, 256), D2A: (40, 256), D2B: (80, 256), RT: (112, 512)}


def gather_copies(kind, stage, buf, sems, first, ids):
    me, grp, hi, lo, y, core = ids
    if kind == D2A:
        mine, line, plane = buf.at[core, y, lo, hi], buf.at[core, y, lo], buf.at[core, y]
    else:
        mine, line, plane = buf.at[core, lo, hi], buf.at[core, lo], None
    if stage == "z":
        return [
            send(mine, mine, sems, first + k - 1, (lax.rem(hi + k, HI) * 2 + lo, grp)) for k in range(1, HI)
        ]
    if stage == "x":
        return [send(line, line, sems, first + HI - 1, (hi * 2 + 1 - lo, grp))]
    if stage == "y":
        return [send(plane, plane, sems, first + HI, (me, (1 - y) * 2 + core))]
    part = buf.at[core]
    return [send(part, part, sems, first + HI + 1, (me, y * 2 + 1 - core))]


def forward_kernel(
    down_in, right_in, v1, v2, r1, vs, r2, gains, biases,
    down_out, right_out, cells_o, actd_o, actr_o, acth_o, gated_o, gater_o, wd_o, wr_o, wk_o, kappa,
    cells, actd, actr, acth, gated, gater, wd, wr, wk,
    b_d1, b_d2a, b_d2b, b_rt, own_d, own_q, own_r, right_t, skip_t, ext, ext4, dflow, rflow, photo_d, photo_r, dlast, rlast, bias_col,
    send_sems, recv_sems, in_sems, out_sems,
):
    n = down_in.shape[0]
    ids = peers(HI)
    me, grp, hi, lo, y, core = ids
    sems = (send_sems, recv_sems)
    load_d = pltpu.make_async_copy(down_in, photo_d, in_sems.at[0])
    load_r = pltpu.make_async_copy(right_in, photo_r, in_sems.at[1])
    load_d.start()
    load_r.start()
    meet(*ids, False)
    bufs = {D1: b_d1, D2A: b_d2a, D2B: b_d2b, RT: b_rt}

    def copies(l, kind, stage):
        return gather_copies(kind, stage, bufs[kind].at[l], sems, (l * 4 + kind) * 6, ids)

    def start(l, kind, stage):
        start_all(copies(l, kind, stage))

    def wait(l, kind, stage):
        wait_all(copies(l, kind, stage))

    for l in range(LAYERS):
        own_d[l, :C2, :240] = v2[l]
        own_d[l, C2:, :240] = v1[l]
        own_d[l, :, 240:] = jnp.zeros((480, 16), BF)
        right = jnp.concatenate([r2[l], r1[l]], axis=1).astype(F32)
        right = jnp.concatenate([right, jnp.zeros((160, 32), F32)], axis=1)
        skip = jnp.concatenate([vs[l].astype(F32), jnp.zeros((40, 352), F32)], axis=1)
        own_r[l] = jnp.concatenate([right, skip, jnp.zeros((24, 512), F32)], axis=0).astype(BF)
        b_d1[l, core, lo, hi] = own_d[l, pl.ds(pl.multiple_of(C2 + core * 80, 16), 80), :]
        for q in range(4):
            own_q[l, q] = own_d[l, q * 40 : q * 40 + 40, :]
        b_d2a[l, core, y, lo, hi] = own_q[l, core * 2 + y]
        b_d2b[l, core, lo, hi] = own_d[l, pl.ds(pl.multiple_of(C + core * 80, 16), 80), :]
        b_rt[l, core, lo, hi] = own_r[l, pl.ds(pl.multiple_of(core * 112, 16), 112), :]
        if l == 0:
            start(0, D1, "z")
            start(0, D2A, "z")

    def unpack_d1(l):
        for k in range(8):
            for c in range(2):
                wd[l, k, C2 + c * 80 : C2 + c * 80 + 80, :] = b_d1[l, c, k % 2, k // 2]

    def unpack_d2(l):
        for k in range(8):
            for q in range(4):
                wd[l, k, q * 40 : q * 40 + 40, :] = b_d2a[l, q // 2, q % 2, k % 2, k // 2]
            for c in range(2):
                wd[l, k, C + c * 80 : C + c * 80 + 80, :] = b_d2b[l, c, k % 2, k // 2]

    def unpack_rt(l):
        for k in range(8):
            wr[l, k * 160 : k * 160 + 112, :] = b_rt[l, 0, k % 2, k // 2]
            wr[l, k * 160 + 112 : k * 160 + 160, :] = b_rt[l, 1, k % 2, k // 2, :48]
            wk[l, k * 40 : k * 40 + 40, :] = b_rt[l, 1, k % 2, k // 2, 48:88, :C]
        for k in range(4):
            rows = wr[l, k * C2 : (k + 1) * C2, :480]
            right_t[l, :, k * C2 : (k + 1) * C2] = nt(eye(480), rows).astype(BF)
        skip_t[l] = nt(eye(C), wk[l]).astype(BF)

    def set_scale(l, m, total):
        lo_, hi_ = SPANS[m]
        gain = row_to_col(gains[l : l + 1, lo_:hi_])
        kappa[lo_:hi_, l : l + 1] = scale_of(total, gain)

    def scale(l, m):
        lo_, hi_ = SPANS[m]
        return kappa[lo_:hi_, l : l + 1]

    def bias(l, m):
        lo_, hi_ = SPANS[m]
        return bias_col[lo_:hi_, l : l + 1]

    keep_out = []

    def save(src, dst):
        copy = pltpu.make_async_copy(src, dst, out_sems.at[len(keep_out)])
        copy.start()
        keep_out.append(copy)

    for l in range(LAYERS):
        bias_col[:, l : l + 1] = row_to_col(biases[l : l + 1, :])
    load_d.wait()
    load_r.wait()

    def begin(i, carry):
        for v in range(8):
            x = load_cells(photo_d.at[i], v)
            dflow[i, :, at(v)] = x
            cells[0, i, :, at(v)] = pair_elu(x)
            rflow[i, :, at(v)] = load_cells(photo_r.at[i], v)
        return carry

    wait(0, D1, "z")
    start(0, D1, "x")
    start(0, D2B, "z")
    wait(0, D2A, "z")
    start(0, D2A, "x")
    lax.fori_loop(0, n, begin, 0)
    save(cells.at[0], cells_o.at[0])
    wait(0, D1, "x")
    start(0, D1, "core")
    start(0, RT, "z")
    wait(0, D2A, "x")
    start(0, D2A, "y")
    wait(0, D1, "core")

    def part_a(l, hooks):
        unpack_d1(l)
        set_scale(l, 0, block_square_sum(wd.at[l], C2, 480))

        def body(i, carry):
            for v in range(8):
                put_down(ext, v, cells[l, i, :, at(v)])
            for j in range(4):
                acc = down_product(wd.at[l], C2, C, ext, j)
                for h in range(2):
                    v = 2 * j + h
                    actd[l, i, :, at(v)] = pair_elu(acc[:, at(h)] * scale(l, 0) + bias(l, 0))
            for k, hook in hooks.items():
                pl.when(i == k)(hook)
            return carry

        lax.fori_loop(0, n, body, 0)
        save(actd.at[l], actd_o.at[l])

    def part_b(l, hooks):
        unpack_d2(l)
        set_scale(l, 1, block_square_sum(wd.at[l], 0, C2))
        save(wd.at[l], wd_o.at[l])

        def body(i, carry):
            for v in range(8):
                put_down(ext, v, actd[l, i, :, at(v)])
            for j in range(4):
                acc = down_product(wd.at[l], 0, C2, ext, j)
                for h in range(2):
                    v = 2 * j + h
                    gate = acc[:, at(h)] * scale(l, 1) + bias(l, 1)
                    t = gate[:C]
                    s = sigmoid(gate[C:])
                    gated[l, i, :C, at(v)] = t.astype(BF)
                    gated[l, i, C:, at(v)] = s.astype(BF)
                    new = dflow[i, :, at(v)] + t * s
                    dflow[i, :, at(v)] = new
                    cells[l + 1, i, :, at(v)] = pair_elu(new)
                    if l == LAYERS - 1:
                        dlast[i, :, at(v)] = new.astype(BF)
            for k, hook in hooks.items():
                pl.when(i == k)(hook)
            return carry

        lax.fori_loop(0, n, body, 0)
        save(gated.at[l], gated_o.at[l])
        save(cells.at[l + 1], cells_o.at[l + 1])
        if l == LAYERS - 1:
            save(dlast, down_out)

    def part_c(l, hooks):
        unpack_rt(l)
        total = square_sum(right_t[l])
        set_scale(l, 2, total[C2:])
        set_scale(l, 3, square_sum(skip_t[l]))
        set_scale(l, 4, total[:C2])
        save(wr.at[l], wr_o.at[l])
        save(wk.at[l], wk_o.at[l])

        def body(i, carry):
            for v in range(8):
                act = pair_elu(rflow[i, :, at(v)])
                actr[l, i, :, at(v)] = act
                put_right(ext4, v, act)
            skip_bias = bias(l, 2) + bias(l, 3)
            for j in range(4):
                acc = nn(right_t[l, C2:], ext4[:, j * 256 : j * 256 + 256]) * scale(l, 2)
                acc = acc + nn(skip_t[l], cells[l + 1, i, :, j * 256 : j * 256 + 256]) * scale(l, 3)
                for h in range(2):
                    v = 2 * j + h
                    acth[l, i, :, at(v)] = pair_elu(acc[:, at(h)] + skip_bias)
            for v in range(8):
                put_right(ext4, v, acth[l, i, :, at(v)])
            for j in range(4):
                acc = nn(right_t[l, :C2], ext4[:, j * 256 : j * 256 + 256])
                for h in range(2):
                    v = 2 * j + h
                    gate = acc[:, at(h)] * scale(l, 4) + bias(l, 4)
                    t = gate[:C]
                    s = sigmoid(gate[C:])
                    gater[l, i, :C, at(v)] = t.astype(BF)
                    gater[l, i, C:, at(v)] = s.astype(BF)
                    new = rflow[i, :, at(v)] + t * s
                    if l == LAYERS - 1:
                        rlast[i, :, at(v)] = new.astype(BF)
                    else:
                        rflow[i, :, at(v)] = new
            for k, hook in hooks.items():
                pl.when(i == k)(hook)
            return carry

        lax.fori_loop(0, n, body, 0)
        save(actr.at[l], actr_o.at[l])
        save(acth.at[l], acth_o.at[l])
        save(gater.at[l], gater_o.at[l])
        if l == LAYERS - 1:
            save(rlast, right_out)

    last = n - 1

    def a0_first():
        wait(0, D2B, "z")
        start(0, D2B, "x")

    def a0_last():
        wait(0, D2A, "y")
        start(0, D2A, "core")
        wait(0, D2B, "x")
        start(0, D2B, "core")
        wait(0, RT, "z")
        start(0, RT, "x")
        start(1, D1, "z")
        start(1, D2A, "z")

    def b0_mid():
        wait(1, D1, "z")
        start(1, D1, "x")
        wait(1, D2A, "z")
        start(1, D2A, "x")
        start(1, D2B, "z")

    def b0_last():
        wait(0, RT, "x")
        start(0, RT, "core")
        wait(1, D2B, "z")
        start(1, D2B, "x")
        start(1, RT, "z")

    def c0_first():
        wait(1, D1, "x")
        start(1, D1, "core")
        wait(1, D2A, "x")
        start(1, D2A, "y")

    def c0_last():
        wait(1, D2B, "x")
        start(1, D2B, "core")
        wait(1, D2A, "y")
        start(1, D2A, "core")
        wait(1, RT, "z")
        start(1, RT, "x")

    def b1_last():
        wait(1, RT, "x")
        start(1, RT, "core")

    part_a(0, {0: a0_first, last: a0_last})
    wait(0, D2A, "core")
    wait(0, D2B, "core")
    part_b(0, {1: b0_mid, last: b0_last})
    wait(0, RT, "core")
    part_c(0, {0: c0_first, last: c0_last})
    wait(1, D1, "core")
    part_a(1, {})
    wait(1, D2A, "core")
    wait(1, D2B, "core")
    part_b(1, {last: b1_last})
    wait(1, RT, "core")
    part_c(1, {})
    for copy in keep_out:
        copy.wait()


def run_forward_gather(down_in, right_in, v1, v2, r1, vs, r2, gains, biases):
    n = down_in.shape[0]
    sds = jax.ShapeDtypeStruct
    vmem = pl.BlockSpec(memory_space=pltpu.VMEM)
    hbm = pl.BlockSpec(memory_space=pl.ANY)
    act = (LAYERS, n, C2, PX)
    kept = [(LAYERS + 1, n, C2, PX)] + [act] * 5
    weights = [(LAYERS, 8, 480, 256), (LAYERS, 1280, 512), (LAYERS, C2, C)]
    photo = (n, 32, 32, C)
    return pl.pallas_call(
        forward_kernel,
        in_specs=[hbm] * 2 + [vmem] * 7,
        out_specs=[hbm] * 11 + [vmem],
        out_shape=[sds((n, C, PX), BF)] * 2 + [sds(s, BF) for s in kept + weights] + [sds((1120, 2), F32)],
        scratch_shapes=[pltpu.VMEM(s, BF) for s in kept + weights]
        + [
            pltpu.VMEM((LAYERS, 2, 2, HI) + PIECE[D1], BF),
            pltpu.VMEM((LAYERS, 2, 2, 2, HI) + PIECE[D2A], BF),
            pltpu.VMEM((LAYERS, 2, 2, HI) + PIECE[D2B], BF),
            pltpu.VMEM((LAYERS, 2, 2, HI) + PIECE[RT], BF),
            pltpu.VMEM((LAYERS, 480, 256), BF),
            pltpu.VMEM((LAYERS, 4, 40, 256), BF),
            pltpu.VMEM((LAYERS, 224, 512), BF),
            pltpu.VMEM((LAYERS, 480, 1280), BF),
            pltpu.VMEM((LAYERS, C, C2), BF),
            pltpu.VMEM((960, 1152), BF),
            pltpu.VMEM((1280, PX), BF),
            pltpu.VMEM((n, C, PX), F32),
            pltpu.VMEM((n, C, PX), F32),
            pltpu.VMEM(photo, BF),
            pltpu.VMEM(photo, BF),
            pltpu.VMEM((n, C, PX), BF),
            pltpu.VMEM((n, C, PX), BF),
            pltpu.VMEM((1120, LAYERS), F32),
            pltpu.SemaphoreType.DMA((48,)),
            pltpu.SemaphoreType.DMA((48,)),
            pltpu.SemaphoreType.DMA((2,)),
            pltpu.SemaphoreType.DMA((32,)),
        ],
        compiler_params=pltpu.CompilerParams(
            vmem_limit_bytes=62 << 20, collective_id=0, has_side_effects=True
        ),
        name="forward_gather",
    )(down_in, right_in, v1, v2, r1, vs, r2, gains, biases)


RG, DA, DB, DC = 0, 1, 2, 3
KINDS = (RG, DA, DB, DC)
ROWS = {RG: 176, DA: 80, DB: 80, DC: 80}
X_FIRST = {RG: True, DA: True, DB: False, DC: False}


def place(kind, k, q):
    core, y = divmod(q, 2)
    hi, lo = divmod(k, 2)
    return (core, lo, y, hi) if X_FIRST[kind] else (core, y, lo, hi)


def put_block(out, kind, k, row, tile):
    tile = jnp.concatenate([tile, jnp.zeros((tile.shape[0], 32), F32)], axis=1).astype(BF)
    for q in range(4):
        out[place(kind, k, q) + (slice(row, row + tile.shape[0]),)] = tile[:, at(q)]


def pack_down(out, kind, acc, width, first):
    for k in range(8):
        parts = []
        for p in range(3):
            tap, chan = divmod(240 * k + 80 * p, C2)
            a, c = divmod(tap, 3)
            lo = c * width + first
            parts.append(acc[a, chan : chan + 80, lo : lo + C])
        put_block(out, kind, k, 0, jnp.concatenate(parts, axis=1))


def pack_right(out, gr2, gr1, gs):
    for k in range(8):
        t, half = divmod(k, 2)
        row = slice(half * C, (half + 1) * C)
        part = jnp.concatenate([gr2[row, t * C2 : (t + 1) * C2], gr1[row, t * C : (t + 1) * C]], axis=1)
        put_block(out, RG, k, 0, part)
        skip = gs[40 * k : 40 * k + 40]
        third = jnp.concatenate([skip[32:], jnp.zeros((8, C), F32)], axis=0)
        put_block(out, RG, k, C, jnp.concatenate([skip[:16], skip[16:32], third], axis=1))


def dot_rows(weight, grad, width, count):
    row = jnp.sum(weight.astype(F32) * grad, axis=0, keepdims=True)
    return sum(row[:, k * width : (k + 1) * width] for k in range(count))


def right_taps(wr, br1, br2):
    for t in range(4):
        rows = wr[t * C2 : (t + 1) * C2, :480]
        br2[:, t * C2 : (t + 1) * C2] = rows[:, :C2]
        br1[:, t * C : (t + 1) * C] = rows[:, C2:]


def down_taps(wd, b1, b2):
    for k in range(8):
        rows = wd[k, :, :240].T
        for p in range(3):
            tap, chan = divmod(240 * k + 80 * p, C2)
            a, c = divmod(tap, 3)
            b2[a, chan : chan + 80, c * C2 : (c + 1) * C2] = rows[80 * p : 80 * p + 80, :C2]
            b1[a, chan : chan + 80, c * C : (c + 1) * C] = rows[80 * p : 80 * p + 80, C2:]


def sum_stage(kind, stage, sems, first, g, bufs, ids):
    me, grp, hi, lo, y, core = ids
    t1, t2, t3, t4, fin = bufs
    to_x = (hi * 2 + 1 - lo, grp)
    to_y = (me, (1 - y) * 2 + core)
    f, s, to_f, to_s = (lo, y, to_x, to_y) if X_FIRST[kind] else (y, lo, to_y, to_x)
    if stage == 0:
        return [send(g.at[1 - core], t1, sems, first, (me, y * 2 + 1 - core))]
    if stage == 1:
        return [send(t1.at[1 - f], t2, sems, first + 1, to_f)]
    if stage == 2:
        return [send(t2.at[1 - s], t3, sems, first + 2, to_s)]
    if stage == 3:
        return [
            send(t3.at[lax.rem(hi + k, HI)], t4.at[k - 1], sems, first + 2 + k, (lax.rem(hi + k, HI) * 2 + lo, grp))
            for k in range(1, HI)
        ]
    mine = fin.at[core, y]
    return [send(mine, mine, sems, first + 2 + HI + k - 1, (me, lax.rem(grp + k, 4))) for k in range(1, 4)]


def sum_adds(kind, stage, g, bufs, ids):
    me, grp, hi, lo, y, core = ids
    t1, t2, t3, t4, fin = bufs
    f, s = (lo, y) if X_FIRST[kind] else (y, lo)
    if stage == 1:
        add_into(t1, g.at[core])
    if stage == 2:
        add_into(t2, t1.at[f])
    if stage == 3:
        add_into(t3, t2.at[s])
    if stage == 4:
        total = t3[hi].astype(F32)
        for k in range(1, HI):
            total = total + t4[k - 1].astype(F32)
        fin[core, y] = total.astype(BF)


def backward_kernel(
    down_cot, right_cot, cells, actd, actr, acth, gated, gater, wd_in, wr_in, wk_in,
    mask, kappa, gains, v1, v2, r1, vs, r2,
    down_flow, right_flow, o1, o2, or1, os, or2, ogain, obias,
    *scratch,
):
    scratch = list(scratch)

    def take(count):
        out = scratch[:count]
        del scratch[:count]
        return out

    cot_d, cot_r, gdown, gright, gcells, cells_a, cells_b, xd, xr, xh, gtd, gtr, wd, wr, wk = take(15)
    b1, b2, br1, br2, g1, g2, gr1, gr2, gs, bsum = take(10)
    ext, ext1, ext41, dskip, dhd = take(5)
    packed = {(l, kind): take(1)[0] for l in range(LAYERS) for kind in KINDS}
    bufs = {(l, kind): take(5) for l in range(LAYERS) for kind in KINDS}
    near_rows, far_rows, send_sems, recv_sems, row_send, row_recv, in_sems, out_sems = take(8)
    n = gdown.shape[0]
    last = n - 1
    ids = peers(HI)
    me, grp, hi, lo, y, core = ids
    sems = (send_sems, recv_sems)
    rsems = (row_send, row_recv)
    loads = {}

    def load(name, src, dst):
        loads[name] = pltpu.make_async_copy(src, dst, in_sems.at[len(loads)])
        loads[name].start()

    def need(*names):
        for name in names:
            loads[name].wait()

    def load_right(l):
        load(("wr", l), wr_in.at[l], wr)
        load(("wk", l), wk_in.at[l], wk)
        load(("gtr", l), gater.at[l], gtr)
        load(("xh", l), acth.at[l], xh)
        load(("xr", l), actr.at[l], xr)

    load("cot_r", right_cot, cot_r)
    load("cot_d", down_cot, cot_d)
    load_right(1)
    load("cells2", cells.at[2], cells_a)
    load(("wd", 1), wd_in.at[1], wd)
    load(("gtd", 1), gated.at[1], gtd)
    load(("xd", 1), actd.at[1], xd)
    load("cells1", cells.at[1], cells_b)
    meet(*ids, True)

    def copies(l, kind, stage):
        return sum_stage(kind, stage, sems, (l * 4 + kind) * 9, packed[l, kind], bufs[l, kind], ids)

    def wait(l, kind, stage):
        wait_all(copies(l, kind, stage))

    def start(l, kind, stage):
        sum_adds(kind, stage, packed[l, kind], bufs[l, kind], ids)
        start_all(copies(l, kind, stage))

    def step(l, kind, stage):
        wait(l, kind, stage - 1)
        start(l, kind, stage)

    def steps(*moves):
        def hook():
            for move in moves:
                step(*move)

        return hook

    def run_hooks(i, hooks):
        for k, hook in hooks.items():
            pl.when(i == k)(hook)

    def begin(i, carry):
        for v in range(8):
            m = jnp.concatenate([mask[i, g * 8 + v : g * 8 + v + 1, :] for g in range(4)], axis=1).astype(F32)
            gdown[i, :, at(v)] = load_cells(cot_d.at[i], v) * m
            gright[i, :, at(v)] = load_cells(cot_r.at[i], v) * m
        return carry

    ext4 = ext.at[:, :PX]

    def clear(*accs):
        for acc in accs:
            acc[...] = jnp.zeros(acc.shape, F32)

    def right_part(l, high, hooks):
        def scale(m):
            return kappa[SPANS[m][0] : SPANS[m][1], l : l + 1]

        def body(i, carry):
            total = None
            for v in range(8):
                d = gate_back(
                    gright[i, :, at(v)], gtr[i, :C, at(v)].astype(F32), gtr[i, C:, at(v)].astype(F32)
                )
                total = d if total is None else total + d
                put_right_back(ext4, v, (d * scale(4)).astype(BF))
            bsum[l, SPANS[4][0] : SPANS[4][1], :] += total
            gr2[...] += nt(xh[i], ext4[...])
            total = None
            for j in range(4):
                e = nn(br2[...], ext4[:, j * 256 : j * 256 + 256])
                for h in range(2):
                    v = 2 * j + h
                    d = elu_back(e[:, at(h)], xh[i, :, at(v)])
                    total = d if total is None else total + d
                    put_right_back(ext41, v, (d * scale(2)).astype(BF))
                    dskip[:, at(v)] = (d * scale(3)).astype(BF)
            bsum[l, SPANS[2][0] : SPANS[2][1], :] += total
            bsum[l, SPANS[3][0] : SPANS[3][1], :] += total
            gr1[...] += nt(xr[i], ext41[...])
            gs[...] += nt(high[i], dskip[...])
            for j in range(4):
                e = nn(br1[...], ext41[:, j * 256 : j * 256 + 256])
                k = nn(wk[...], dskip[:, j * 256 : j * 256 + 256])
                for h in range(2):
                    v = 2 * j + h
                    gright[i, :, at(v)] += elu_back(e[:, at(h)], xr[i, :, at(v)])
                    gc = k[:, at(h)]
                    if l + 1 < LAYERS:
                        gc = gc + gcells[i, :, at(v)].astype(F32)
                    gdown[i, :, at(v)] += elu_back(gc, high[i, :, at(v)])
            run_hooks(i, hooks)
            return carry

        lax.fori_loop(0, n, body, 0)

    def down_part(l, hooks):
        def scale(m):
            return kappa[SPANS[m][0] : SPANS[m][1], l : l + 1]

        def body(i, carry):
            total = None
            for v in range(8):
                d = gate_back(
                    gdown[i, :, at(v)], gtd[i, :C, at(v)].astype(F32), gtd[i, C:, at(v)].astype(F32)
                )
                total = d if total is None else total + d
                put_down_back(ext, v, (d * scale(1)).astype(BF))
            bsum[l, SPANS[1][0] : SPANS[1][1], :] += total
            for a in range(2):
                first = 128 * (1 - a)
                g2[a] += nt(xd[i], ext[:960, first : first + PX])
            total = None
            for j in range(4):
                e = nn(b2[1], ext[:960, j * 256 : j * 256 + 256])
                e = e + nn(b2[0], ext[:960, j * 256 + 128 : j * 256 + 384])
                for h in range(2):
                    v = 2 * j + h
                    d = elu_back(e[:, at(h)], xd[i, :, at(v)])
                    total = d if total is None else total + d
                    dhd[i, :, at(v)] = (d * scale(0)).astype(BF)
            bsum[l, SPANS[0][0] : SPANS[0][1], :] += total
            run_hooks(i, hooks)
            return carry

        lax.fori_loop(0, n, body, 0)

    def first_part(low):
        def body(i, carry):
            for v in range(8):
                put_down_back(ext1, v, dhd[i, :, at(v)])
            for a in range(2):
                first = 128 * (1 - a)
                g1[a] += nt(low[i], ext1[:, first : first + PX])
            return carry

        lax.fori_loop(0, n, body, 0)

    def input_part(l, low, hooks):
        def body(i, carry):
            for v in range(8):
                put_down_back(ext1, v, dhd[i, :, at(v)])
            for j in range(4):
                e = nn(b1[1], ext1[:, j * 256 : j * 256 + 256])
                e = e + nn(b1[0], ext1[:, j * 256 + 128 : j * 256 + 384])
                if l > 0:
                    gcells[i, :, j * 256 : j * 256 + 256] = e.astype(BF)
                else:
                    for h in range(2):
                        v = 2 * j + h
                        gdown[i, :, at(v)] += elu_back(e[:, at(h)], low[i, :, at(v)])
            run_hooks(i, hooks)
            return carry

        lax.fori_loop(0, n, body, 0)

    def right_end(l):
        pack_right(packed[l, RG], gr2, gr1, gs)
        start(l, RG, 0)
        near_rows[grp, l : l + 1, SPANS[2][0] : SPANS[4][1]] = jnp.concatenate(
            [
                dot_rows(br1[...], gr1[...], C, 4),
                dot_rows(wk[...], gs[...], C, 1),
                dot_rows(br2[...], gr2[...], C2, 4),
            ],
            axis=1,
        )

    def down_end(l):
        pack_down(packed[l, DA], DA, g2, C2, 0)
        start(l, DA, 0)
        pack_down(packed[l, DB], DB, g2, C2, C)
        start(l, DB, 0)

    def first_end(l):
        pack_down(packed[l, DC], DC, g1, C, 0)
        start(l, DC, 0)
        near_rows[grp, l : l + 1, : SPANS[1][1]] = jnp.concatenate(
            [
                dot_rows(b1[0], g1[0], C, 3) + dot_rows(b1[1], g1[1], C, 3),
                dot_rows(b2[0], g2[0], C2, 3) + dot_rows(b2[1], g2[1], C2, 3),
            ],
            axis=1,
        )
        near_rows[grp, 2 + l : 3 + l, :1120] = jnp.sum(bsum[l].T, axis=0, keepdims=True)

    near_rows[grp] = jnp.zeros((8, 1152), F32)
    clear(bsum, gr1, gr2, gs, g1, g2)
    need("cot_r", "cot_d")
    lax.fori_loop(0, n, begin, 0)
    need(("wr", 1), ("wk", 1))
    right_taps(wr, br1, br2)
    need(("gtr", 1), ("xh", 1), ("xr", 1), "cells2")
    right_part(1, cells_a, {})
    right_end(1)
    load_right(0)
    load("cells0", cells.at[0], cells_a)
    need(("wd", 1))
    down_taps(wd, b1, b2)
    load(("wd", 0), wd_in.at[0], wd)
    need(("gtd", 1), ("xd", 1))
    down_part(1, {0: steps((1, RG, 1))})
    down_end(1)
    load(("gtd", 0), gated.at[0], gtd)
    load(("xd", 0), actd.at[0], xd)
    need("cells1")
    first_part(cells_b)
    first_end(1)
    steps((1, DA, 1), (1, DB, 1), (1, RG, 2))()
    input_part(1, cells_b, {last: steps((1, DC, 1))})
    clear(gr1, gr2, gs, g1, g2)
    need(("wr", 0), ("wk", 0))
    right_taps(wr, br1, br2)
    need(("gtr", 0), ("xh", 0), ("xr", 0))
    right_part(
        0,
        cells_b,
        {
            0: steps((1, DA, 2), (1, DB, 2), (1, RG, 3), (1, DC, 2)),
            1: steps((1, DA, 3), (1, DB, 3), (1, RG, 4)),
            last: steps((1, DC, 3), (1, DA, 4), (1, DB, 4)),
        },
    )
    right_end(0)
    out_right = pltpu.make_async_copy(gright, right_flow, out_sems.at[0])
    out_right.start()
    need(("wd", 0))
    down_taps(wd, b1, b2)
    need(("gtd", 0), ("xd", 0))
    down_part(0, {0: steps((0, RG, 1), (1, DC, 4)), last: steps((0, RG, 2))})
    down_end(0)
    need("cells0")
    first_part(cells_a)
    first_end(0)
    mine = near_rows.at[grp]
    near = [send(mine, mine, rsems, k - 1, (me, lax.rem(grp + k, 4))) for k in range(1, 4)]

    def far():
        part = far_rows.at[me]
        return [
            send(part, part, rsems, 2 + k, (lax.rem(me + k, 2 * HI), grp)) for k in range(1, 2 * HI)
        ]

    def far_start():
        wait_all(near)
        far_rows[me] = near_rows[0] + near_rows[1] + near_rows[2] + near_rows[3]
        start_all(far())

    start_all(near)
    steps((0, DA, 1), (0, DB, 1), (0, DC, 1), (0, RG, 3))()
    input_part(0, cells_a, {1: far_start})
    out_down = pltpu.make_async_copy(gdown, down_flow, out_sems.at[1])
    out_down.start()
    steps((0, DA, 2), (0, DB, 2))()
    for kind in KINDS:
        wait(1, kind, 4)
    steps((0, RG, 4), (0, DC, 2))()
    wait_all(far())
    total = far_rows[0]
    for k in range(1, 2 * HI):
        total = total + far_rows[k]
    obias[...] = total[2:4, :1120]
    ogain[...] = total[0:2, :1120] / gains[...]

    def factors(l):
        recip = col_to_row(kappa[:, l : l + 1]) / gains[l : l + 1, :]
        row = recip * recip * total[l : l + 1, :1120]
        return row, row_to_col(row[:, : SPANS[1][1]])

    def write_right(l, row):
        right = quarters(bufs[l, RG][4])
        or1[l] = right[:C, C2:480] - r1[l].astype(F32) * row[:, SPANS[2][0] : SPANS[2][1]]
        tail = right[C:]
        skip = jnp.concatenate([tail[:, :C], tail[:, C:C2], tail[:8, C2:480]], axis=0)
        os[l] = skip - vs[l].astype(F32) * row[:, SPANS[3][0] : SPANS[3][1]]
        or2[l] = right[:C, :C2] - r2[l].astype(F32) * row[:, SPANS[4][0] : SPANS[4][1]]

    def turned(l, kind):
        flat = quarters(bufs[l, kind][4]).T
        return jnp.concatenate([flat[C * p : C * (p + 1)] for p in range(3)], axis=1)

    def write_down(l, kind, col):
        if kind == DC:
            o1[l] = turned(l, kind) - v1[l].astype(F32) * col[:C]
        else:
            first = 0 if kind == DA else C
            part = slice(first, first + C)
            o2[l, part] = turned(l, kind) - v2[l, part].astype(F32) * col[C + first : C2 + first]

    row_1, col_1 = factors(1)
    row_0, col_0 = factors(0)
    steps((0, DA, 3), (0, DB, 3))()
    write_right(1, row_1)
    steps((0, DC, 3))()
    for kind in (DA, DB, DC):
        write_down(1, kind, col_1)
    wait(0, RG, 4)
    write_right(0, row_0)
    steps((0, DA, 4), (0, DB, 4), (0, DC, 4))()
    for kind in (DA, DB, DC):
        wait(0, kind, 4)
        write_down(0, kind, col_0)
    out_right.wait()
    out_down.wait()


def sum_shape(kind):
    return (2, 2, 2, HI, ROWS[kind], 128)


def run_backward_sums(down_cot, right_cot, kept, weights, mask, kappa, gains, v1, v2, r1, vs, r2):
    n = down_cot.shape[0]
    sds = jax.ShapeDtypeStruct
    vmem = pl.BlockSpec(memory_space=pltpu.VMEM)
    hbm = pl.BlockSpec(memory_space=pl.ANY)
    V = pltpu.VMEM
    wide = V((n, C2, PX), BF)
    flow = (n, C, PX)
    scratch = [V((n, 32, 32, C), BF)] * 2 + [V(flow, F32)] * 2 + [wide] * 8
    scratch += [V((8, 480, 256), BF), V((1280, 512), BF), V((C2, C), BF)]
    scratch += [V((2, C2, 480), BF), V((2, C2, 960), BF), V((C2, 640), BF), V((C2, 1280), BF)]
    scratch += [V((2, C2, 480), F32), V((2, C2, 960), F32), V((C2, 640), F32), V((C2, 1280), F32), V((C2, C), F32)]
    scratch += [V((LAYERS, 1120, 128), F32)]
    scratch += [V((1280, 1152), BF), V((480, 1152), BF), V((640, PX), BF), V((C, PX), BF), V((n, C, PX), BF)]
    scratch += [V(sum_shape(kind), BF) for l in range(LAYERS) for kind in KINDS]
    for l in range(LAYERS):
        for kind in KINDS:
            tail = (ROWS[kind], 128)
            scratch += [
                V((2, 2, HI) + tail, BF),
                V((2, HI) + tail, BF),
                V((HI,) + tail, BF),
                V((HI - 1,) + tail, BF),
                V((2, 2) + tail, BF),
            ]
    sem = pltpu.SemaphoreType.DMA
    scratch += [V((4, 8, 1152), F32), V((2 * HI, 8, 1152), F32), sem((72,)), sem((72,)), sem((10,)), sem((10,)), sem((24,)), sem((2,))]
    return pl.pallas_call(
        backward_kernel,
        in_specs=[hbm] * 11 + [vmem] * 8,
        out_specs=[hbm] * 2 + [vmem] * 7,
        out_shape=[sds(flow, F32)] * 2 + [sds(v.shape, F32) for v in (v1, v2, r1, vs, r2)] + [sds((LAYERS, 1120), F32)] * 2,
        scratch_shapes=scratch,
        compiler_params=pltpu.CompilerParams(
            vmem_limit_bytes=63 << 20, collective_id=1, has_side_effects=True
        ),
        name="backward_sums",
    )(down_cot, right_cot, *kept, *weights, mask, kappa, gains, v1, v2, r1, vs, r2)


def write_kernel(*refs):
    flows, small = refs[:4], refs[4:11]
    photos, results = refs[11:15], refs[15:]
    for v in range(8):
        store_bf16(photos[0].at[0], v, flows[0][0, :, at(v)])
        store_bf16(photos[1].at[0], v, flows[1][0, :, at(v)])
        store_f32(photos[2].at[0], v, flows[2][0, :, at(v)])
        store_f32(photos[3].at[0], v, flows[3][0, :, at(v)])

    @pl.when(pl.program_id(0) == 0)
    def _():
        for src, dst in zip(small, results):
            dst[...] = src[...]


def run_write(flows, small):
    n = flows[0].shape[0]
    sds = jax.ShapeDtypeStruct
    return pl.pallas_call(
        write_kernel,
        grid=(n,),
        in_specs=[image((1, C, PX))] * 4 + [once(a.shape) for a in small],
        out_specs=[image((1, 32, 32, C))] * 4 + [once(a.shape) for a in small],
        out_shape=[sds((n, 32, 32, C), f.dtype) for f in flows] + [sds(a.shape, a.dtype) for a in small],
        compiler_params=pltpu.CompilerParams(vmem_limit_bytes=63 << 20),
        name="write",
    )(*flows, *small)


def general_finish(lower, upper, whole_v, shards, gains):
    rows = lax.psum(jnp.stack([lower[4], upper[4]]), ("dp", "grp"))
    sums = []
    units = []
    inverse = []
    for m, (low, high) in enumerate(zip(unpack(*lower[:4]), unpack(*upper[:4]))):
        part = lax.psum_scatter(jnp.stack([low, high]), "dp", scatter_dimension=1, tiled=True)
        sums.append(lax.psum(part, "grp").astype(F32))
        vals = whole_v[m].astype(F32)
        inv = lax.rsqrt(jnp.sum(vals * vals, axis=1))
        inverse.append(inv)
        units.append(shards[m].astype(F32) * inv[:, None, :])
    inverse = jnp.concatenate(inverse, axis=1)
    dots = rows[:, 0] * inverse
    grads = [sums[m] - units[m] * dots[:, None, lo:hi] for m, (lo, hi) in enumerate(SPANS)]
    return (*grads, rows[:, 0] / gains, rows[:, 1])


def on_device(
    quick,
    down_in,
    right_in,
    pixel_mask,
    down_cot,
    right_cot,
    v_down1,
    v_down2,
    v_right1,
    v_skip,
    v_right2,
    gains,
    biases,
):
    shards = (v_down1, v_down2, v_right1, v_skip, v_right2)
    n = down_in.shape[0]
    if quick and n > 2:
        turned = (v_down1.swapaxes(1, 2), v_down2.swapaxes(1, 2), v_right1, v_skip, v_right2)
        down_last, right_last, *rest = run_forward_gather(down_in, right_in, *turned, gains, biases)
        kept, weights, kappa = rest[:6], rest[6:9], rest[9]
        down_g, right_g, *small = run_backward_sums(
            down_cot, right_cot, kept, weights, pixel_mask, kappa, gains, *turned
        )
        down_out, right_out, down_grad, right_grad, *grads = run_write(
            (down_last, right_last, down_g, right_g), small
        )
        grads[0] = grads[0].swapaxes(1, 2)
        grads[1] = grads[1].swapaxes(1, 2)
        return (down_out, right_out, down_grad, right_grad, *grads)
    whole_v = tuple(lax.all_gather(v, "dp", axis=1, tiled=True) for v in shards)
    weights = assemble(*whole_v)
    cols = jnp.concatenate([gains, biases], axis=0).T
    down_out, right_out, *kept, kappa = run_forward(down_in, right_in, *weights, cols)
    mask = pixel_mask.reshape(n, 4, 8, 32).transpose(0, 2, 1, 3).reshape(n, 1, 1024).astype(F32)
    down_g, right_g, cells_g, *upper = run_backward(1, down_cot, right_cot, None, mask, kept, kappa, *weights)
    down_grad, right_grad, *lower = run_backward(0, down_g, right_g, cells_g, mask, kept, kappa, *weights)
    grads = general_finish(lower, upper, whole_v, shards, gains)
    return (down_out, right_out, down_grad, right_grad, *grads)


def solution(mesh):
    photo = P(("dp", "grp"), None, None, None)
    rows = P(None, "dp", None)
    quick = mesh.shape["dp"] == 2 * HI and mesh.shape["grp"] == 4
    return jax.shard_map(
        functools.partial(on_device, quick),
        mesh=mesh,
        in_specs=(photo, photo, P(("dp", "grp"), None, None), photo, photo) + (rows,) * 5 + (P(), P()),
        out_specs=(photo,) * 4 + (rows,) * 5 + (P(), P()),
        check_vma=False,
    )
```

```python
import functools
import jax
import jax.numpy as jnp
from jax import lax
from jax.experimental import pallas as pl
from jax.experimental.pallas import tpu as pltpu
from jax.sharding import PartitionSpec as P

BF = jnp.bfloat16
F32 = jnp.float32
LAYERS = 2
HI = 4
MESH = pl.DeviceIdType.MESH
C = 160
C2 = 320
SPANS = ((0, 160), (160, 480), (480, 640), (640, 800), (800, 1120))


def nt(a, b):
    return lax.dot_general(a, b, (((1,), (1,)), ((), ())), preferred_element_type=F32)


def nn(a, b):
    return lax.dot_general(a, b, (((1,), (0,)), ((), ())), preferred_element_type=F32)


def eye(n):
    same = lax.broadcasted_iota(jnp.int32, (n, n), 0) == lax.broadcasted_iota(jnp.int32, (n, n), 1)
    return jnp.where(same, 1.0, 0.0).astype(BF)


def lane():
    return lax.broadcasted_iota(jnp.int32, (1, 128), 1)


def keep(cond, tile):
    return jnp.where(cond, tile, jnp.zeros((), tile.dtype))


def col_shift(tile, off):
    if off == 0:
        return tile
    col = lane() & 31
    if off == 1:
        return keep(col != 31, pltpu.roll(tile, 127, 1))
    return keep(col != 0, pltpu.roll(tile, 1, 1))


def row_before(tile):
    return keep(lane() >= 32, pltpu.roll(tile, 32, 1))


def row_after(tile):
    return keep(lane() < 96, pltpu.roll(tile, 96, 1))


def at(v):
    return slice(v * 128, (v + 1) * 128)


def put_down(ext, v, tile):
    n = tile.shape[0]
    for c in range(3):
        moved = col_shift(tile, c - 1)
        ext[c * n : (c + 1) * n, at(v + 1)] = moved
        if v == 7:
            ext[c * n : (c + 1) * n, at(0)] = row_before(moved)


def put_right(ext, v, tile):
    n = tile.shape[0]
    for c in range(2):
        moved = col_shift(tile, c - 1)
        ext[(2 + c) * n : (3 + c) * n, at(v)] = moved
        if v == 7:
            ext[c * n : (c + 1) * n, at(0)] = row_before(moved)
        else:
            ext[c * n : (c + 1) * n, at(v + 1)] = moved


def put_down_back(ext, v, tile):
    n = tile.shape[0]
    for c in range(3):
        moved = col_shift(tile, 1 - c)
        ext[c * n : (c + 1) * n, at(v)] = moved
        if v == 0:
            ext[c * n : (c + 1) * n, at(8)] = row_after(moved)


def put_right_back(ext, v, tile):
    n = tile.shape[0]
    for c in range(2):
        moved = col_shift(tile, 1 - c)
        ext[(2 + c) * n : (3 + c) * n, at(v)] = moved
        if v == 0:
            ext[c * n : (c + 1) * n, at(7)] = row_after(moved)
        else:
            ext[c * n : (c + 1) * n, at(v - 1)] = moved


def pair_elu(x):
    e = jnp.exp(-jnp.abs(x)) - 1.0
    up = x > 0
    return jnp.concatenate([jnp.where(up, x, e), jnp.where(up, e, -x)], axis=0).astype(BF)


def elu_back(grad, act):
    slope = jnp.minimum(act.astype(F32), 0.0) + 1.0
    both = grad * slope
    return both[:C] - both[C:]


def sigmoid(x):
    return 1.0 / (1.0 + jnp.exp(-x))


def load_cells(ref, v):
    rows = jnp.concatenate([ref[g * 8 + v] for g in range(4)], axis=0)
    return rows.T.astype(F32)


def store_bf16(ref, v, tile):
    out = tile.astype(BF).T
    for g in range(4):
        ref[g * 8 + v] = out[g * 32 : (g + 1) * 32]


def store_f32(ref, v, tile):
    out = tile.T
    for g in range(4):
        ref[g * 8 + v] = out[g * 32 : (g + 1) * 32]


def scale_of(total, gain):
    return gain * lax.rsqrt(total)


def square_sum(vals):
    vals = vals.astype(F32)
    return jnp.sum(vals * vals, axis=1, keepdims=True)


def block_square_sum(weight, lo, hi):
    total = None
    for k in range(8):
        vals = weight[k, lo:hi, :240].astype(F32)
        total = vals * vals if total is None else total + vals * vals
    return jnp.sum(total, axis=1, keepdims=True)


def down_product(weight, first, count, ext, j):
    acc = None
    for k in range(8):
        lo = j * 256 + 128 * (k // 4)
        part = nn(weight[k, first : first + count, :240], ext[240 * (k % 4) : 240 * (k % 4) + 240, lo : lo + 256])
        acc = part if acc is None else acc + part
    return acc


def fwd_kernel(
    down_in, right_in, wd, wr, wk, cols,
    down_out, right_out, cells, actd, actr, acth, gated, gater, kappa,
    right_t, skip_t, ext, ext4, dflow, rflow,
):
    @pl.when(pl.program_id(0) == 0)
    def _():
        for l in range(LAYERS):
            for k in range(4):
                rows = wr[l, k * C2 : (k + 1) * C2, :480]
                right_t[l, :, k * C2 : (k + 1) * C2] = nt(eye(480), rows).astype(BF)
            skip_t[l] = nt(eye(C), wk[l]).astype(BF)
            down_total = sum(square_sum(wd[l, k, :, :240]) for k in range(8))
            right_total = square_sum(right_t[l])
            totals = (down_total[C2:], down_total[:C2], right_total[C2:], square_sum(skip_t[l]), right_total[:C2])
            for total, (lo, hi) in zip(totals, SPANS):
                kappa[lo:hi, l : l + 1] = scale_of(total, cols[lo:hi, l : l + 1])

    for v in range(8):
        x = load_cells(down_in.at[0], v)
        dflow[:, at(v)] = x
        act = pair_elu(x)
        cells[0, 0, :, at(v)] = act
        put_down(ext, v, act)
        rflow[:, at(v)] = load_cells(right_in.at[0], v)
    for l in range(LAYERS):
        def scale(m):
            lo, hi = SPANS[m]
            return kappa[lo:hi, l : l + 1]

        def bias(m):
            lo, hi = SPANS[m]
            return cols[lo:hi, 2 + l : 3 + l]

        for j in range(4):
            acc = down_product(wd.at[l], C2, C, ext, j)
            for h in range(2):
                v = 2 * j + h
                actd[l, 0, :, at(v)] = pair_elu(acc[:, at(h)] * scale(0) + bias(0))
        for v in range(8):
            put_down(ext, v, actd[l, 0, :, at(v)])
            act = pair_elu(rflow[:, at(v)])
            actr[l, 0, :, at(v)] = act
            put_right(ext4, v, act)
        for j in range(4):
            acc = down_product(wd.at[l], 0, C2, ext, j)
            for h in range(2):
                v = 2 * j + h
                gate = acc[:, at(h)] * scale(1) + bias(1)
                t = gate[:C]
                s = sigmoid(gate[C:])
                gated[l, 0, :C, at(v)] = t.astype(BF)
                gated[l, 0, C:, at(v)] = s.astype(BF)
                new = dflow[:, at(v)] + t * s
                dflow[:, at(v)] = new
                cells[l + 1, 0, :, at(v)] = pair_elu(new)
        skip_bias = bias(2) + bias(3)
        for j in range(4):
            acc = nn(right_t[l, C2:], ext4[:, j * 256 : j * 256 + 256]) * scale(2)
            acc = acc + nn(skip_t[l], cells[l + 1, 0, :, j * 256 : j * 256 + 256]) * scale(3)
            for h in range(2):
                v = 2 * j + h
                acth[l, 0, :, at(v)] = pair_elu(acc[:, at(h)] + skip_bias)
        for v in range(8):
            put_right(ext4, v, acth[l, 0, :, at(v)])
            if l + 1 < LAYERS:
                put_down(ext, v, cells[l + 1, 0, :, at(v)])
        for j in range(4):
            acc = nn(right_t[l, :C2], ext4[:, j * 256 : j * 256 + 256])
            for h in range(2):
                v = 2 * j + h
                gate = acc[:, at(h)] * scale(4) + bias(4)
                t = gate[:C]
                s = sigmoid(gate[C:])
                gater[l, 0, :C, at(v)] = t.astype(BF)
                gater[l, 0, C:, at(v)] = s.astype(BF)
                rflow[:, at(v)] = rflow[:, at(v)] + t * s
    for v in range(8):
        store_bf16(down_out.at[0], v, dflow[:, at(v)])
        store_bf16(right_out.at[0], v, rflow[:, at(v)])


def gate_back(g, t, s):
    p = g * s
    q = p * t * (1.0 - s)
    return jnp.concatenate([p, q], axis=0)


def bwd_kernel(
    top, down_g, right_g, mask, *refs,
):
    refs = list(refs)
    cells_g = None if top else refs.pop(0)
    (
        low_cells, high_cells, actd, actr, acth, gated, gater, kappa, wd, wr, wk,
    ) = refs[:11]
    refs = refs[11:]
    if top:
        down_out, right_out, cells_out = refs[:3]
        refs = refs[3:]
    else:
        down_out, right_out = refs[:2]
        refs = refs[2:]
    (
        o_rg, o_da, o_db, o_dc, orows,
        b1, b2, br1, br2, g1, g2, gr1, gs, gr2, bsum, ext, ext1, ext4, ext41, dskip, gdown, gright,
    ) = refs
    layer = 1 if top else 0
    step = pl.program_id(0)

    @pl.when(step == 0)
    def _():
        down_taps(wd.at[0], b1, b2)
        right_taps(wr.at[0], br1, br2)
        for acc in (g1, g2, gr1, gs, gr2, bsum):
            acc[...] = jnp.zeros(acc.shape, F32)

    def scale(m):
        lo, hi = SPANS[m]
        return kappa[lo:hi, layer : layer + 1]

    def add_bias(m, total):
        lo, hi = SPANS[m]
        bsum[lo:hi, :] += total

    total = None
    for v in range(8):
        if top:
            m = mask[0, :, at(v)]
            gdown[:, at(v)] = load_cells(down_g.at[0], v) * m
            g = load_cells(right_g.at[0], v) * m
            gright[:, at(v)] = g
        else:
            g = right_g[0, :, at(v)]
        d = gate_back(g, gater[0, 0, :C, at(v)].astype(F32), gater[0, 0, C:, at(v)].astype(F32))
        total = d if total is None else total + d
        put_right_back(ext4, v, (d * scale(4)).astype(BF))
    add_bias(4, total)
    gr2[...] += nt(acth[0, 0], ext4[...])
    total = None
    for j in range(4):
        e = nn(br2[...], ext4[:, j * 256 : j * 256 + 256])
        for h in range(2):
            v = 2 * j + h
            d = elu_back(e[:, at(h)], acth[0, 0, :, at(v)])
            total = d if total is None else total + d
            put_right_back(ext41, v, (d * scale(2)).astype(BF))
            dskip[:, at(v)] = (d * scale(3)).astype(BF)
    add_bias(2, total)
    add_bias(3, total)
    gr1[...] += nt(actr[0, 0], ext41[...])
    gs[...] += nt(high_cells[0, 0], dskip[...])
    for j in range(4):
        e = nn(br1[...], ext41[:, j * 256 : j * 256 + 256])
        k = nn(wk[0], dskip[:, j * 256 : j * 256 + 256])
        for h in range(2):
            v = 2 * j + h
            old = gright[:, at(v)] if top else right_g[0, :, at(v)]
            new = old + elu_back(e[:, at(h)], actr[0, 0, :, at(v)])
            if top:
                right_out[0, :, at(v)] = new
            else:
                store_f32(right_out.at[0], v, new)
            gc = k[:, at(h)]
            if not top:
                gc = gc + cells_g[0, :, at(v)].astype(F32)
            old = gdown[:, at(v)] if top else down_g[0, :, at(v)]
            gdown[:, at(v)] = old + elu_back(gc, high_cells[0, 0, :, at(v)])
    total = None
    for v in range(8):
        g = gdown[:, at(v)]
        if top:
            down_out[0, :, at(v)] = g
        d = gate_back(g, gated[0, 0, :C, at(v)].astype(F32), gated[0, 0, C:, at(v)].astype(F32))
        total = d if total is None else total + d
        put_down_back(ext, v, (d * scale(1)).astype(BF))
    add_bias(1, total)
    for a in range(2):
        lo = 128 * (1 - a)
        g2[a] += nt(actd[0, 0], ext[:, lo : lo + 1024])
    total = None
    for j in range(4):
        e = nn(b2[1], ext[:, j * 256 : j * 256 + 256])
        e = e + nn(b2[0], ext[:, j * 256 + 128 : j * 256 + 384])
        for h in range(2):
            v = 2 * j + h
            d = elu_back(e[:, at(h)], actd[0, 0, :, at(v)])
            total = d if total is None else total + d
            put_down_back(ext1, v, (d * scale(0)).astype(BF))
    add_bias(0, total)
    for a in range(2):
        lo = 128 * (1 - a)
        g1[a] += nt(low_cells[0, 0], ext1[:, lo : lo + 1024])
    for j in range(4):
        e = nn(b1[1], ext1[:, j * 256 : j * 256 + 256])
        e = e + nn(b1[0], ext1[:, j * 256 + 128 : j * 256 + 384])
        if top:
            cells_out[0, :, j * 256 : j * 256 + 256] = e.astype(BF)
        else:
            for h in range(2):
                v = 2 * j + h
                last = gdown[:, at(v)] + elu_back(e[:, at(h)], low_cells[0, 0, :, at(v)])
                store_f32(down_out.at[0], v, last)

    @pl.when(step == pl.num_programs(0) - 1)
    def _():
        pack_right(o_rg, gr2, gr1, gs)
        pack_down(o_da, DA, g2, C2, 0)
        pack_down(o_db, DB, g2, C2, C)
        pack_down(o_dc, DC, g1, C, 0)
        orows[0:1, :] = jnp.concatenate(
            [
                dot_rows(b1[0], g1[0], C, 3) + dot_rows(b1[1], g1[1], C, 3),
                dot_rows(b2[0], g2[0], C2, 3) + dot_rows(b2[1], g2[1], C2, 3),
                dot_rows(br1[...], gr1[...], C, 4),
                dot_rows(wk[0], gs[...], C, 1),
                dot_rows(br2[...], gr2[...], C2, 4),
            ],
            axis=1,
        )
        orows[1:2, :] = jnp.sum(bsum[...].T, axis=0, keepdims=True)


def whole(shape, dtype=None):
    zeros = (0,) * len(shape)
    return pl.BlockSpec(shape, lambda i: zeros)


def once(shape):
    zeros = (0,) * len(shape)
    return pl.BlockSpec(shape, lambda i: zeros, pipeline_mode=pl.Buffered(1))


def image(shape):
    rest = (0,) * (len(shape) - 1)
    return pl.BlockSpec(shape, lambda i: (i,) + rest)


PX = 1024


def run_forward(down_in, right_in, wd, wr, wk, cols):
    n = down_in.shape[0]
    sds = jax.ShapeDtypeStruct
    kept = [(3, C2, PX)] + [(LAYERS, C2, PX)] * 5
    return pl.pallas_call(
        fwd_kernel,
        grid=(n,),
        in_specs=[image((1, 32, 32, C))] * 2 + [once(w.shape) for w in (wd, wr, wk)] + [once((1120, 4))],
        out_specs=[image((1, 32, 32, C))] * 2
        + [pl.BlockSpec((s[0], 1) + s[1:], lambda i: (0, i, 0, 0)) for s in kept]
        + [once((1120, 2))],
        out_shape=[sds((n, 32, 32, C), BF)] * 2
        + [sds((s[0], n) + s[1:], BF) for s in kept]
        + [sds((1120, 2), F32)],
        scratch_shapes=[
            pltpu.VMEM((LAYERS, 480, 1280), BF),
            pltpu.VMEM((LAYERS, C, C2), BF),
            pltpu.VMEM((960, 1152), BF),
            pltpu.VMEM((1280, PX), BF),
            pltpu.VMEM((C, PX), F32),
            pltpu.VMEM((C, PX), F32),
        ],
        compiler_params=pltpu.CompilerParams(vmem_limit_bytes=60 << 20),
        name="forward",
    )(down_in, right_in, wd, wr, wk, cols)


def run_backward(layer, down_g, right_g, cells_g, mask, kept, kappa, wd, wr, wk):
    n = down_g.shape[0]
    top = layer == 1
    sds = jax.ShapeDtypeStruct
    flow = image((1, C, PX))
    wide = image((1, C2, PX))

    def pick(which):
        return pl.BlockSpec((1, 1, C2, PX), lambda i: (which, i, 0, 0))

    def one_layer(shape):
        rest = (0,) * (len(shape) - 1)
        return pl.BlockSpec((1,) + shape[1:], lambda i: (layer,) + rest, pipeline_mode=pl.Buffered(1))

    cells = kept[0]
    ins = [down_g, right_g, mask] + ([] if top else [cells_g]) + [cells, cells] + list(kept[1:]) + [kappa, wd, wr, wk]
    photo = image((1, 32, 32, C))
    in_specs = (
        ([photo] * 2 if top else [flow] * 2)
        + [image((1, 1, PX))]
        + ([] if top else [wide])
        + [pick(layer), pick(layer + 1)]
        + [pick(layer)] * 5
        + [once((1120, 2))]
        + [one_layer(w.shape) for w in (wd, wr, wk)]
    )
    if top:
        out_specs = [flow, flow, wide]
        out_shape = [sds((n, C, PX), F32)] * 2 + [sds((n, C2, PX), BF)]
    else:
        out_specs = [photo] * 2
        out_shape = [sds((n, 32, 32, C), F32)] * 2
    return pl.pallas_call(
        functools.partial(bwd_kernel, top),
        grid=(n,),
        in_specs=in_specs,
        out_specs=out_specs + [once(sum_shape(kind)) for kind in KINDS] + [once((2, 1120))],
        out_shape=out_shape + [sds(sum_shape(kind), BF) for kind in KINDS] + [sds((2, 1120), F32)],
        scratch_shapes=[
            pltpu.VMEM((2, 320, 480), BF),
            pltpu.VMEM((2, 320, 960), BF),
            pltpu.VMEM((320, 640), BF),
            pltpu.VMEM((320, 1280), BF),
            pltpu.VMEM((2, 320, 480), F32),
            pltpu.VMEM((2, 320, 960), F32),
            pltpu.VMEM((320, 640), F32),
            pltpu.VMEM((320, 160), F32),
            pltpu.VMEM((320, 1280), F32),
            pltpu.VMEM((1120, 128), F32),
            pltpu.VMEM((960, 1152), BF),
            pltpu.VMEM((480, 1152), BF),
            pltpu.VMEM((1280, 1024), BF),
            pltpu.VMEM((640, 1024), BF),
            pltpu.VMEM((160, 1024), BF),
            pltpu.VMEM((C, PX), F32),
            pltpu.VMEM((C, PX), F32),
        ],
        compiler_params=pltpu.CompilerParams(vmem_limit_bytes=60 << 20),
        name="backward%d" % layer,
    )(*ins)


def assemble(v1, v2, r1, vs, r2):
    rows = jnp.concatenate([v2, v1], axis=2).reshape(LAYERS, 8, 240, 480)
    wd = jnp.pad(rows.swapaxes(2, 3), ((0, 0), (0, 0), (0, 0), (0, 16)))
    wr = jnp.pad(jnp.concatenate([r2, r1], axis=2), ((0, 0), (0, 0), (0, 32)))
    return wd, wr, vs


def unpack(*packed):
    blocks = []
    for kind, g in zip(KINDS, packed):
        order = (3, 1, 4, 0, 2, 5) if X_FIRST[kind] else (3, 2, 4, 0, 1, 5)
        blocks.append(g.transpose(order).reshape(8, ROWS[kind], 512))

    def down(block):
        return block[:, :, :480].reshape(8, 80, 3, C).swapaxes(1, 2).reshape(1920, C)

    right = blocks[0][:, :C].reshape(1280, 512)
    tail = blocks[0][:, C:, :480].reshape(8, 16, 3, C).swapaxes(1, 2).reshape(8, 48, C)
    skip = tail[:, :40].reshape(C2, C)
    down2 = jnp.concatenate([down(blocks[1]), down(blocks[2])], axis=1)
    return down(blocks[3]), down2, right[:, C2:480], skip, right[:, :C2]


def peers(hi_count):
    me = lax.axis_index("dp")
    grp = lax.axis_index("grp")
    hi, lo = me // 2, lax.rem(me, 2)
    y, core = grp // 2, lax.rem(grp, 2)
    return me, grp, hi, lo, y, core


def meet(me, grp, hi, lo, y, core, everyone):
    barrier = pltpu.get_barrier_semaphore()
    near = [((hi + k) % HI * 2 + lo, grp) for k in range(1, HI)]
    near += [(hi * 2 + 1 - lo, grp)]
    if everyone:
        near += [((hi + k) % HI * 2 + 1 - lo, grp) for k in range(1, HI)]
    near += [(me, (grp + k) % 4) for k in range(1, 4)]
    for device in near:
        pl.semaphore_signal(barrier, inc=1, device_id=device, device_id_type=MESH)
    pl.semaphore_wait(barrier, len(near))


def send(src, dst, sems, at_, device):
    return pltpu.make_async_remote_copy(
        src_ref=src,
        dst_ref=dst,
        send_sem=sems[0].at[at_],
        recv_sem=sems[1].at[at_],
        device_id=device,
        device_id_type=MESH,
    )


def start_all(copies):
    for copy in copies:
        copy.start()


def wait_all(copies):
    for copy in copies:
        copy.wait()


def add_into(dst, src):
    dst[...] = (dst[...].astype(F32) + src[...].astype(F32)).astype(BF)


def col_to_row(col):
    return jnp.broadcast_to(col, (col.shape[0], 128)).T[0:1, :]


def row_to_col(row):
    return jnp.broadcast_to(row, (128, row.shape[1])).T[:, 0:1]


def quarters(fin):
    return jnp.concatenate([fin[q // 2, q % 2].astype(F32) for q in range(4)], axis=1)


D1, D2A, D2B, RA, RB = 0, 1, 2, 3, 4
PIECE = {D1: (80, 256), D2A: (40, 256), D2B: (80, 256), RA: (88, 128), RB: (176, 128)}


def gather_copies(kind, stage, buf, sems, first, ids):
    me, grp, hi, lo, y, core = ids
    if kind in (D2A, RA):
        mine, line, plane = buf.at[core, y, lo, hi], buf.at[core, y, lo], buf.at[core, y]
    else:
        mine, line, plane = buf.at[core, lo, hi], buf.at[core, lo], None
    if stage == "z":
        return [
            send(mine, mine, sems, first + k - 1, (lax.rem(hi + k, HI) * 2 + lo, grp)) for k in range(1, HI)
        ]
    if stage == "x":
        return [send(line, line, sems, first + HI - 1, (hi * 2 + 1 - lo, grp))]
    if stage == "y":
        return [send(plane, plane, sems, first + HI, (me, (1 - y) * 2 + core))]
    part = buf.at[core]
    return [send(part, part, sems, first + HI + 1, (me, y * 2 + 1 - core))]


def forward_kernel(
    down_in, right_in, v1, v2, r1, vs, r2, gains, biases,
    down_out, right_out, cells_o, actd_o, actr_o, acth_o, gated_o, gater_o, wd_o, wr_o, wk_o, kappa,
    cells, actd, actr, acth, gated, gater, wd, wr, wk,
    b_d1, b_d2a, b_d2b, b_ra, b_rb, own_d, own_q, own_ra, own_rb, right_t, skip_t, ext, ext4, dflow, rflow, photo_d, photo_r, dlast, rlast, bias_col,
    send_sems, recv_sems, in_sems, out_sems,
):
    n = down_in.shape[0]
    ids = peers(HI)
    me, grp, hi, lo, y, core = ids
    sems = (send_sems, recv_sems)
    load_d = pltpu.make_async_copy(down_in, photo_d, in_sems.at[0])
    load_r = pltpu.make_async_copy(right_in, photo_r, in_sems.at[1])
    load_d.start()
    load_r.start()
    meet(*ids, False)
    bufs = {D1: b_d1, D2A: b_d2a, D2B: b_d2b, RA: b_ra, RB: b_rb}

    def copies(l, kind, stage):
        return gather_copies(kind, stage, bufs[kind].at[l], sems, (l * 5 + kind) * 6, ids)

    def start(l, kind, stage):
        start_all(copies(l, kind, stage))

    def wait(l, kind, stage):
        wait_all(copies(l, kind, stage))

    for l in range(LAYERS):
        own_d[l, :C2, :240] = v2[l]
        own_d[l, C2:, :240] = v1[l]
        own_d[l, :, 240:] = jnp.zeros((480, 16), BF)
        b_d1[l, core, lo, hi] = own_d[l, pl.ds(pl.multiple_of(C2 + core * 80, 16), 80), :]
        if l == 0:
            start(0, D1, "z")
        for q in range(4):
            own_q[l, q] = own_d[l, q * 40 : q * 40 + 40, :]
        b_d2a[l, core, y, lo, hi] = own_q[l, core * 2 + y]
        b_d2b[l, core, lo, hi] = own_d[l, pl.ds(pl.multiple_of(C + core * 80, 16), 80), :]
        skip = vs[l].astype(F32)
        third = jnp.concatenate([skip[32:], jnp.zeros((8, C), F32)], axis=0)
        tail = jnp.concatenate([skip[:16], skip[16:32], third], axis=1)
        right = jnp.concatenate([r2[l], r1[l]], axis=1).astype(F32)
        right = jnp.concatenate([right, tail], axis=0)
        right = jnp.concatenate([right, jnp.zeros((176, 32), F32)], axis=1).astype(BF)
        for q in range(4):
            own_ra[l, q] = right[(q % 2) * 88 : (q % 2) * 88 + 88, at(q // 2)]
        for c in range(2):
            own_rb[l, c] = right[:, at(2 + c)]
        b_ra[l, core, y, lo, hi] = own_ra[l, core * 2 + y]
        b_rb[l, core, lo, hi] = own_rb[l, core]

    def unpack_d1(l):
        for k in range(8):
            for c in range(2):
                wd[l, k, C2 + c * 80 : C2 + c * 80 + 80, :] = b_d1[l, c, k % 2, k // 2]

    def unpack_d2(l):
        for k in range(8):
            for q in range(4):
                wd[l, k, q * 40 : q * 40 + 40, :] = b_d2a[l, q // 2, q % 2, k % 2, k // 2]
            for c in range(2):
                wd[l, k, C + c * 80 : C + c * 80 + 80, :] = b_d2b[l, c, k % 2, k // 2]

    def unpack_rt(l):
        for k in range(8):
            tail = []
            for c in range(2):
                halves = [b_ra[l, c, h, k % 2, k // 2].astype(F32) for h in range(2)]
                tile = jnp.concatenate(halves, axis=0)
                wr[l, k * C : (k + 1) * C, at(c)] = tile[:C].astype(BF)
                tail.append(tile[C:])
            for c in range(2):
                tile = b_rb[l, c, k % 2, k // 2]
                wr[l, k * C : (k + 1) * C, at(2 + c)] = tile[:C]
                tail.append(tile[C:].astype(F32))
            tail = jnp.concatenate(tail, axis=1)
            skip = jnp.concatenate([tail[:, :C], tail[:, C:C2], tail[:8, C2:480]], axis=0)
            wk[l, k * 40 : k * 40 + 40, :] = skip.astype(BF)
        for k in range(4):
            rows = wr[l, k * C2 : (k + 1) * C2, :480]
            right_t[l, :, k * C2 : (k + 1) * C2] = nt(eye(480), rows).astype(BF)
        skip_t[l] = nt(eye(C), wk[l]).astype(BF)

    def set_scale(l, m, total):
        lo_, hi_ = SPANS[m]
        gain = row_to_col(gains[l : l + 1, lo_:hi_])
        kappa[lo_:hi_, l : l + 1] = scale_of(total, gain)

    def scale(l, m):
        lo_, hi_ = SPANS[m]
        return kappa[lo_:hi_, l : l + 1]

    def bias(l, m):
        lo_, hi_ = SPANS[m]
        return bias_col[lo_:hi_, l : l + 1]

    keep_out = []

    def save(src, dst):
        copy = pltpu.make_async_copy(src, dst, out_sems.at[len(keep_out)])
        copy.start()
        keep_out.append(copy)

    for l in range(LAYERS):
        bias_col[:, l : l + 1] = row_to_col(biases[l : l + 1, :])
    load_d.wait()
    load_r.wait()

    def begin(i, carry):
        for v in range(8):
            x = load_cells(photo_d.at[i], v)
            dflow[i, :, at(v)] = x
            cells[0, i, :, at(v)] = pair_elu(x)
            rflow[i, :, at(v)] = load_cells(photo_r.at[i], v)
        return carry

    wait(0, D1, "z")
    start(0, D1, "x")
    start(0, D2A, "z")
    start(0, D2B, "z")
    lax.fori_loop(0, n, begin, 0)
    save(cells.at[0], cells_o.at[0])
    wait(0, D2A, "z")
    start(0, D2A, "x")
    start(0, RA, "z")
    wait(0, D2B, "z")
    start(0, D2B, "x")
    start(0, RB, "z")
    wait(0, D1, "x")
    start(0, D1, "core")
    wait(0, D2A, "x")
    start(0, D2A, "y")
    wait(0, RA, "z")
    start(0, RA, "x")
    wait(0, D1, "core")

    def part_a(l, hooks):
        unpack_d1(l)
        set_scale(l, 0, block_square_sum(wd.at[l], C2, 480))

        def body(i, carry):
            for v in range(8):
                put_down(ext, v, cells[l, i, :, at(v)])
            for j in range(4):
                acc = down_product(wd.at[l], C2, C, ext, j)
                for h in range(2):
                    v = 2 * j + h
                    actd[l, i, :, at(v)] = pair_elu(acc[:, at(h)] * scale(l, 0) + bias(l, 0))
            for k, hook in hooks.items():
                pl.when(i == k)(hook)
            return carry

        lax.fori_loop(0, n, body, 0)
        save(actd.at[l], actd_o.at[l])

    def part_b(l, hooks):
        unpack_d2(l)
        set_scale(l, 1, block_square_sum(wd.at[l], 0, C2))
        save(wd.at[l], wd_o.at[l])

        def body(i, carry):
            for v in range(8):
                put_down(ext, v, actd[l, i, :, at(v)])
            for j in range(4):
                acc = down_product(wd.at[l], 0, C2, ext, j)
                for h in range(2):
                    v = 2 * j + h
                    gate = acc[:, at(h)] * scale(l, 1) + bias(l, 1)
                    t = gate[:C]
                    s = sigmoid(gate[C:])
                    gated[l, i, :C, at(v)] = t.astype(BF)
                    gated[l, i, C:, at(v)] = s.astype(BF)
                    new = dflow[i, :, at(v)] + t * s
                    dflow[i, :, at(v)] = new
                    cells[l + 1, i, :, at(v)] = pair_elu(new)
                    if l == LAYERS - 1:
                        dlast[i, :, at(v)] = new.astype(BF)
            for k, hook in hooks.items():
                pl.when(i == k)(hook)
            return carry

        lax.fori_loop(0, n, body, 0)
        save(gated.at[l], gated_o.at[l])
        save(cells.at[l + 1], cells_o.at[l + 1])
        if l == LAYERS - 1:
            save(dlast, down_out)

    def part_c(l, hooks):
        unpack_rt(l)
        total = square_sum(right_t[l])
        set_scale(l, 2, total[C2:])
        set_scale(l, 3, square_sum(skip_t[l]))
        set_scale(l, 4, total[:C2])
        save(wr.at[l], wr_o.at[l])
        save(wk.at[l], wk_o.at[l])
        first = len(keep_out)
        outs = [(actr.at[l], actr_o.at[l]), (acth.at[l], acth_o.at[l]), (gater.at[l], gater_o.at[l])]
        if l == LAYERS - 1:
            outs.append((rlast, right_out))

        def body(i, carry):
            for v in range(8):
                act = pair_elu(rflow[i, :, at(v)])
                actr[l, i, :, at(v)] = act
                put_right(ext4, v, act)
            skip_bias = bias(l, 2) + bias(l, 3)
            for j in range(4):
                acc = nn(right_t[l, C2:], ext4[:, j * 256 : j * 256 + 256]) * scale(l, 2)
                acc = acc + nn(skip_t[l], cells[l + 1, i, :, j * 256 : j * 256 + 256]) * scale(l, 3)
                for h in range(2):
                    v = 2 * j + h
                    acth[l, i, :, at(v)] = pair_elu(acc[:, at(h)] + skip_bias)
            for v in range(8):
                put_right(ext4, v, acth[l, i, :, at(v)])
            for j in range(4):
                acc = nn(right_t[l, :C2], ext4[:, j * 256 : j * 256 + 256])
                for h in range(2):
                    v = 2 * j + h
                    gate = acc[:, at(h)] * scale(l, 4) + bias(l, 4)
                    t = gate[:C]
                    s = sigmoid(gate[C:])
                    gater[l, i, :C, at(v)] = t.astype(BF)
                    gater[l, i, C:, at(v)] = s.astype(BF)
                    new = rflow[i, :, at(v)] + t * s
                    if l == LAYERS - 1:
                        rlast[i, :, at(v)] = new.astype(BF)
                    else:
                        rflow[i, :, at(v)] = new
            for k, (src, dst) in enumerate(outs):
                pltpu.make_async_copy(src.at[i], dst.at[i], out_sems.at[first + k]).start()
            for k, hook in hooks.items():
                pl.when(i == k)(hook)
            return carry

        lax.fori_loop(0, n, body, 0)
        for k, (src, dst) in enumerate(outs):
            keep_out.append(pltpu.make_async_copy(src, dst, out_sems.at[first + k]))

    last = n - 1

    def a0_mid():
        wait(0, D2B, "x")
        start(0, D2B, "core")

    def a0_last():
        wait(0, D2A, "y")
        start(0, D2A, "core")
        wait(0, RB, "z")
        start(0, RB, "x")
        start(1, D1, "z")
        start(1, D2A, "z")
        wait(0, RA, "x")
        start(0, RA, "y")

    def b0_mid():
        start(1, D2B, "z")
        wait(1, D1, "z")
        start(1, D1, "x")
        wait(1, D2A, "z")
        start(1, D2A, "x")

    def b0_last():
        wait(0, RA, "y")
        start(0, RA, "core")
        wait(0, RB, "x")
        start(0, RB, "core")
        start(1, RA, "z")
        wait(1, D2B, "z")
        start(1, D2B, "x")

    def c0_first():
        wait(1, D1, "x")
        start(1, D1, "core")
        wait(1, D2A, "x")
        start(1, D2A, "y")
        wait(1, RA, "z")
        start(1, RA, "x")
        start(1, RB, "z")

    def c0_mid():
        wait(1, D2B, "x")
        start(1, D2B, "core")

    def c0_last():
        wait(1, D2A, "y")
        start(1, D2A, "core")
        wait(1, RA, "x")
        start(1, RA, "y")
        wait(1, RB, "z")
        start(1, RB, "x")

    def b1_first():
        wait(1, RA, "y")
        start(1, RA, "core")
        wait(1, RB, "x")
        start(1, RB, "core")

    part_a(0, {1: a0_mid, last: a0_last})
    wait(0, D2A, "core")
    wait(0, D2B, "core")
    part_b(0, {1: b0_mid, last: b0_last})
    wait(0, RA, "core")
    wait(0, RB, "core")
    part_c(0, {0: c0_first, 1: c0_mid, last: c0_last})
    wait(1, D1, "core")
    part_a(1, {})
    wait(1, D2A, "core")
    wait(1, D2B, "core")
    part_b(1, {0: b1_first})
    wait(1, RA, "core")
    wait(1, RB, "core")
    part_c(1, {})
    for copy in keep_out:
        copy.wait()


def run_forward_gather(down_in, right_in, v1, v2, r1, vs, r2, gains, biases):
    n = down_in.shape[0]
    sds = jax.ShapeDtypeStruct
    vmem = pl.BlockSpec(memory_space=pltpu.VMEM)
    hbm = pl.BlockSpec(memory_space=pl.ANY)
    act = (LAYERS, n, C2, PX)
    kept = [(LAYERS + 1, n, C2, PX)] + [act] * 5
    weights = [(LAYERS, 8, 480, 256), (LAYERS, 1280, 512), (LAYERS, C2, C)]
    photo = (n, 32, 32, C)
    return pl.pallas_call(
        forward_kernel,
        in_specs=[hbm] * 2 + [vmem] * 7,
        out_specs=[hbm] * 11 + [vmem],
        out_shape=[sds((n, C, PX), BF)] * 2 + [sds(s, BF) for s in kept + weights] + [sds((1120, 2), F32)],
        scratch_shapes=[pltpu.VMEM(s, BF) for s in kept + weights]
        + [
            pltpu.VMEM((LAYERS, 2, 2, HI) + PIECE[D1], BF),
            pltpu.VMEM((LAYERS, 2, 2, 2, HI) + PIECE[D2A], BF),
            pltpu.VMEM((LAYERS, 2, 2, HI) + PIECE[D2B], BF),
            pltpu.VMEM((LAYERS, 2, 2, 2, HI) + PIECE[RA], BF),
            pltpu.VMEM((LAYERS, 2, 2, HI) + PIECE[RB], BF),
            pltpu.VMEM((LAYERS, 480, 256), BF),
            pltpu.VMEM((LAYERS, 4, 40, 256), BF),
            pltpu.VMEM((LAYERS, 4) + PIECE[RA], BF),
            pltpu.VMEM((LAYERS, 2) + PIECE[RB], BF),
            pltpu.VMEM((LAYERS, 480, 1280), BF),
            pltpu.VMEM((LAYERS, C, C2), BF),
            pltpu.VMEM((960, 1152), BF),
            pltpu.VMEM((1280, PX), BF),
            pltpu.VMEM((n, C, PX), F32),
            pltpu.VMEM((n, C, PX), F32),
            pltpu.VMEM(photo, BF),
            pltpu.VMEM(photo, BF),
            pltpu.VMEM((n, C, PX), BF),
            pltpu.VMEM((n, C, PX), BF),
            pltpu.VMEM((1120, LAYERS), F32),
            pltpu.SemaphoreType.DMA((60,)),
            pltpu.SemaphoreType.DMA((60,)),
            pltpu.SemaphoreType.DMA((2,)),
            pltpu.SemaphoreType.DMA((32,)),
        ],
        compiler_params=pltpu.CompilerParams(
            vmem_limit_bytes=62 << 20, collective_id=0, has_side_effects=True
        ),
        name="forward_gather",
    )(down_in, right_in, v1, v2, r1, vs, r2, gains, biases)


RG, DA, DB, DC = 0, 1, 2, 3
KINDS = (RG, DA, DB, DC)
ROWS = {RG: 176, DA: 80, DB: 80, DC: 80}
X_FIRST = {RG: True, DA: True, DB: False, DC: False}


def place(kind, k, q):
    core, y = divmod(q, 2)
    hi, lo = divmod(k, 2)
    return (core, lo, y, hi) if X_FIRST[kind] else (core, y, lo, hi)


def put_block(out, kind, k, row, tile):
    tile = jnp.concatenate([tile, jnp.zeros((tile.shape[0], 32), F32)], axis=1).astype(BF)
    for q in range(4):
        out[place(kind, k, q) + (slice(row, row + tile.shape[0]),)] = tile[:, at(q)]


def pack_down(out, kind, acc, width, first):
    for k in range(8):
        parts = []
        for p in range(3):
            tap, chan = divmod(240 * k + 80 * p, C2)
            a, c = divmod(tap, 3)
            lo = c * width + first
            parts.append(acc[a, chan : chan + 80, lo : lo + C])
        put_block(out, kind, k, 0, jnp.concatenate(parts, axis=1))


def pack_right(out, gr2, gr1, gs):
    for k in range(8):
        t, half = divmod(k, 2)
        row = slice(half * C, (half + 1) * C)
        part = jnp.concatenate([gr2[row, t * C2 : (t + 1) * C2], gr1[row, t * C : (t + 1) * C]], axis=1)
        put_block(out, RG, k, 0, part)
        skip = gs[40 * k : 40 * k + 40]
        third = jnp.concatenate([skip[32:], jnp.zeros((8, C), F32)], axis=0)
        put_block(out, RG, k, C, jnp.concatenate([skip[:16], skip[16:32], third], axis=1))


def dot_rows(weight, grad, width, count):
    row = jnp.sum(weight.astype(F32) * grad, axis=0, keepdims=True)
    return sum(row[:, k * width : (k + 1) * width] for k in range(count))


def right_taps(wr, br1, br2):
    for t in range(4):
        rows = wr[t * C2 : (t + 1) * C2, :480]
        br2[:, t * C2 : (t + 1) * C2] = rows[:, :C2]
        br1[:, t * C : (t + 1) * C] = rows[:, C2:]


def down_taps(wd, b1, b2):
    for k in range(8):
        rows = wd[k, :, :240].T
        for p in range(3):
            tap, chan = divmod(240 * k + 80 * p, C2)
            a, c = divmod(tap, 3)
            b2[a, chan : chan + 80, c * C2 : (c + 1) * C2] = rows[80 * p : 80 * p + 80, :C2]
            b1[a, chan : chan + 80, c * C : (c + 1) * C] = rows[80 * p : 80 * p + 80, C2:]


def sum_stage(kind, stage, sems, first, g, bufs, ids):
    me, grp, hi, lo, y, core = ids
    t1, t2, t3, t4, fin = bufs
    to_x = (hi * 2 + 1 - lo, grp)
    to_y = (me, (1 - y) * 2 + core)
    f, s, to_f, to_s = (lo, y, to_x, to_y) if X_FIRST[kind] else (y, lo, to_y, to_x)
    if stage == 0:
        return [send(g.at[1 - core], t1, sems, first, (me, y * 2 + 1 - core))]
    if stage == 1:
        return [send(t1.at[1 - f], t2, sems, first + 1, to_f)]
    if stage == 2:
        return [send(t2.at[1 - s], t3, sems, first + 2, to_s)]
    if stage == 3:
        return [
            send(t3.at[lax.rem(hi + k, HI)], t4.at[k - 1], sems, first + 2 + k, (lax.rem(hi + k, HI) * 2 + lo, grp))
            for k in range(1, HI)
        ]
    mine = fin.at[core, y]
    return [send(mine, mine, sems, first + 2 + HI + k - 1, (me, lax.rem(grp + k, 4))) for k in range(1, 4)]


def sum_adds(kind, stage, g, bufs, ids):
    me, grp, hi, lo, y, core = ids
    t1, t2, t3, t4, fin = bufs
    f, s = (lo, y) if X_FIRST[kind] else (y, lo)
    if stage == 1:
        add_into(t1, g.at[core])
    if stage == 2:
        add_into(t2, t1.at[f])
    if stage == 3:
        add_into(t3, t2.at[s])
    if stage == 4:
        total = t3[hi].astype(F32)
        for k in range(1, HI):
            total = total + t4[k - 1].astype(F32)
        fin[core, y] = total.astype(BF)


def backward_kernel(
    down_cot, right_cot, cells, actd, actr, acth, gated, gater, wd_in, wr_in, wk_in,
    mask, kappa, gains, v1, v2, r1, vs, r2,
    down_flow, right_flow, o1, o2, or1, os, or2, ogain, obias,
    *scratch,
):
    scratch = list(scratch)

    def take(count):
        out = scratch[:count]
        del scratch[:count]
        return out

    cot_d, cot_r, gdown, gright, gcells, cells_a, cells_b, xd, xr, xh, gtd, gtr, wd, wr, wk = take(15)
    b1, b2, br1, br2, g1, g2, gr1, gr2, gs, bsum = take(10)
    ext, ext1, ext41, dskip, dhd = take(5)
    packed = {(l, kind): take(1)[0] for l in range(LAYERS) for kind in KINDS}
    bufs = {(l, kind): take(5) for l in range(LAYERS) for kind in KINDS}
    near_rows, far_rows, send_sems, recv_sems, row_send, row_recv, in_sems, out_sems = take(8)
    n = gdown.shape[0]
    last = n - 1
    ids = peers(HI)
    me, grp, hi, lo, y, core = ids
    sems = (send_sems, recv_sems)
    rsems = (row_send, row_recv)
    loads = {}

    def load(name, src, dst):
        loads[name] = pltpu.make_async_copy(src, dst, in_sems.at[len(loads)])
        loads[name].start()

    def need(*names):
        for name in names:
            loads[name].wait()

    def load_right(l):
        load(("wr", l), wr_in.at[l], wr)
        load(("wk", l), wk_in.at[l], wk)
        load(("gtr", l), gater.at[l], gtr)
        load(("xh", l), acth.at[l], xh)
        load(("xr", l), actr.at[l], xr)

    load("cot_r", right_cot, cot_r)
    load("cot_d", down_cot, cot_d)
    load_right(1)
    load("cells2", cells.at[2], cells_a)
    load(("wd", 1), wd_in.at[1], wd)
    load(("gtd", 1), gated.at[1], gtd)
    load(("xd", 1), actd.at[1], xd)
    load("cells1", cells.at[1], cells_b)
    meet(*ids, True)

    def copies(l, kind, stage):
        return sum_stage(kind, stage, sems, (l * 4 + kind) * 9, packed[l, kind], bufs[l, kind], ids)

    def wait(l, kind, stage):
        wait_all(copies(l, kind, stage))

    def start(l, kind, stage):
        sum_adds(kind, stage, packed[l, kind], bufs[l, kind], ids)
        start_all(copies(l, kind, stage))

    def step(l, kind, stage):
        wait(l, kind, stage - 1)
        start(l, kind, stage)

    def steps(*moves):
        def hook():
            for move in moves:
                step(*move)

        return hook

    def run_hooks(i, hooks):
        for k, hook in hooks.items():
            pl.when(i == k)(hook)

    def begin(i, carry):
        for v in range(8):
            m = jnp.concatenate([mask[i, g * 8 + v : g * 8 + v + 1, :] for g in range(4)], axis=1).astype(F32)
            gdown[i, :, at(v)] = load_cells(cot_d.at[i], v) * m
            gright[i, :, at(v)] = load_cells(cot_r.at[i], v) * m
        return carry

    ext4 = ext.at[:, :PX]

    def clear(*accs):
        for acc in accs:
            acc[...] = jnp.zeros(acc.shape, F32)

    def right_part(l, high, hooks):
        def scale(m):
            return kappa[SPANS[m][0] : SPANS[m][1], l : l + 1]

        def body(i, carry):
            total = None
            for v in range(8):
                d = gate_back(
                    gright[i, :, at(v)], gtr[i, :C, at(v)].astype(F32), gtr[i, C:, at(v)].astype(F32)
                )
                total = d if total is None else total + d
                put_right_back(ext4, v, (d * scale(4)).astype(BF))
            bsum[l, SPANS[4][0] : SPANS[4][1], :] += total
            gr2[...] += nt(xh[i], ext4[...])
            total = None
            for j in range(4):
                e = nn(br2[...], ext4[:, j * 256 : j * 256 + 256])
                for h in range(2):
                    v = 2 * j + h
                    d = elu_back(e[:, at(h)], xh[i, :, at(v)])
                    total = d if total is None else total + d
                    put_right_back(ext41, v, (d * scale(2)).astype(BF))
                    dskip[:, at(v)] = (d * scale(3)).astype(BF)
            bsum[l, SPANS[2][0] : SPANS[2][1], :] += total
            bsum[l, SPANS[3][0] : SPANS[3][1], :] += total
            gr1[...] += nt(xr[i], ext41[...])
            gs[...] += nt(high[i], dskip[...])
            for j in range(4):
                e = nn(br1[...], ext41[:, j * 256 : j * 256 + 256])
                k = nn(wk[...], dskip[:, j * 256 : j * 256 + 256])
                for h in range(2):
                    v = 2 * j + h
                    gright[i, :, at(v)] += elu_back(e[:, at(h)], xr[i, :, at(v)])
                    gc = k[:, at(h)]
                    if l + 1 < LAYERS:
                        gc = gc + gcells[i, :, at(v)].astype(F32)
                    gdown[i, :, at(v)] += elu_back(gc, high[i, :, at(v)])
            run_hooks(i, hooks)
            return carry

        lax.fori_loop(0, n, body, 0)

    def down_part(l, hooks):
        def scale(m):
            return kappa[SPANS[m][0] : SPANS[m][1], l : l + 1]

        def body(i, carry):
            total = None
            for v in range(8):
                d = gate_back(
                    gdown[i, :, at(v)], gtd[i, :C, at(v)].astype(F32), gtd[i, C:, at(v)].astype(F32)
                )
                total = d if total is None else total + d
                put_down_back(ext, v, (d * scale(1)).astype(BF))
            bsum[l, SPANS[1][0] : SPANS[1][1], :] += total
            for a in range(2):
                first = 128 * (1 - a)
                g2[a] += nt(xd[i], ext[:960, first : first + PX])
            total = None
            for j in range(4):
                e = nn(b2[1], ext[:960, j * 256 : j * 256 + 256])
                e = e + nn(b2[0], ext[:960, j * 256 + 128 : j * 256 + 384])
                for h in range(2):
                    v = 2 * j + h
                    d = elu_back(e[:, at(h)], xd[i, :, at(v)])
                    total = d if total is None else total + d
                    dhd[i, :, at(v)] = (d * scale(0)).astype(BF)
            bsum[l, SPANS[0][0] : SPANS[0][1], :] += total
            run_hooks(i, hooks)
            return carry

        lax.fori_loop(0, n, body, 0)

    def first_part(low):
        def body(i, carry):
            for v in range(8):
                put_down_back(ext1, v, dhd[i, :, at(v)])
            for a in range(2):
                first = 128 * (1 - a)
                g1[a] += nt(low[i], ext1[:, first : first + PX])
            return carry

        lax.fori_loop(0, n, body, 0)

    def input_part(l, low, hooks):
        def body(i, carry):
            for v in range(8):
                put_down_back(ext1, v, dhd[i, :, at(v)])
            for j in range(4):
                e = nn(b1[1], ext1[:, j * 256 : j * 256 + 256])
                e = e + nn(b1[0], ext1[:, j * 256 + 128 : j * 256 + 384])
                if l > 0:
                    gcells[i, :, j * 256 : j * 256 + 256] = e.astype(BF)
                else:
                    for h in range(2):
                        v = 2 * j + h
                        gdown[i, :, at(v)] += elu_back(e[:, at(h)], low[i, :, at(v)])
            run_hooks(i, hooks)
            return carry

        lax.fori_loop(0, n, body, 0)

    def right_end(l):
        pack_right(packed[l, RG], gr2, gr1, gs)
        start(l, RG, 0)
        near_rows[grp, l : l + 1, SPANS[2][0] : SPANS[4][1]] = jnp.concatenate(
            [
                dot_rows(br1[...], gr1[...], C, 4),
                dot_rows(wk[...], gs[...], C, 1),
                dot_rows(br2[...], gr2[...], C2, 4),
            ],
            axis=1,
        )

    def down_end(l):
        pack_down(packed[l, DA], DA, g2, C2, 0)
        start(l, DA, 0)
        pack_down(packed[l, DB], DB, g2, C2, C)
        start(l, DB, 0)

    def first_end(l):
        pack_down(packed[l, DC], DC, g1, C, 0)
        start(l, DC, 0)
        near_rows[grp, l : l + 1, : SPANS[1][1]] = jnp.concatenate(
            [
                dot_rows(b1[0], g1[0], C, 3) + dot_rows(b1[1], g1[1], C, 3),
                dot_rows(b2[0], g2[0], C2, 3) + dot_rows(b2[1], g2[1], C2, 3),
            ],
            axis=1,
        )
        near_rows[grp, 2 + l : 3 + l, :1120] = jnp.sum(bsum[l].T, axis=0, keepdims=True)

    near_rows[grp] = jnp.zeros((8, 1152), F32)
    clear(bsum, gr1, gr2, gs, g1, g2)
    need("cot_r", "cot_d")
    lax.fori_loop(0, n, begin, 0)
    need(("wr", 1), ("wk", 1))
    right_taps(wr, br1, br2)
    need(("gtr", 1), ("xh", 1), ("xr", 1), "cells2")
    right_part(1, cells_a, {})
    right_end(1)
    load_right(0)
    load("cells0", cells.at[0], cells_a)
    need(("wd", 1))
    down_taps(wd, b1, b2)
    load(("wd", 0), wd_in.at[0], wd)
    need(("gtd", 1), ("xd", 1))
    down_part(1, {0: steps((1, RG, 1))})
    down_end(1)
    load(("gtd", 0), gated.at[0], gtd)
    load(("xd", 0), actd.at[0], xd)
    need("cells1")
    first_part(cells_b)
    first_end(1)
    steps((1, DA, 1), (1, DB, 1), (1, RG, 2))()
    input_part(1, cells_b, {last: steps((1, DC, 1))})
    clear(gr1, gr2, gs, g1, g2)
    need(("wr", 0), ("wk", 0))
    right_taps(wr, br1, br2)
    need(("gtr", 0), ("xh", 0), ("xr", 0))
    right_part(
        0,
        cells_b,
        {
            0: steps((1, DA, 2), (1, DB, 2), (1, RG, 3), (1, DC, 2)),
            1: steps((1, DA, 3), (1, DB, 3), (1, RG, 4)),
            last: steps((1, DC, 3), (1, DA, 4), (1, DB, 4)),
        },
    )
    right_end(0)
    out_right = pltpu.make_async_copy(gright, right_flow, out_sems.at[0])
    out_right.start()
    need(("wd", 0))
    down_taps(wd, b1, b2)
    need(("gtd", 0), ("xd", 0))
    down_part(0, {0: steps((0, RG, 1), (1, DC, 4)), last: steps((0, RG, 2))})
    down_end(0)
    need("cells0")
    first_part(cells_a)
    first_end(0)
    mine = near_rows.at[grp]
    near = [send(mine, mine, rsems, k - 1, (me, lax.rem(grp + k, 4))) for k in range(1, 4)]

    def far():
        part = far_rows.at[me]
        return [
            send(part, part, rsems, 2 + k, (lax.rem(me + k, 2 * HI), grp)) for k in range(1, 2 * HI)
        ]

    def far_start():
        wait_all(near)
        far_rows[me] = near_rows[0] + near_rows[1] + near_rows[2] + near_rows[3]
        start_all(far())

    start_all(near)
    steps((0, DA, 1), (0, DB, 1), (0, RG, 3), (0, DC, 1))()
    input_part(0, cells_a, {1: far_start})
    out_down = pltpu.make_async_copy(gdown, down_flow, out_sems.at[1])
    out_down.start()
    steps((0, DA, 2), (0, DB, 2))()
    for kind in KINDS:
        wait(1, kind, 4)
    steps((0, RG, 4), (0, DC, 2))()
    wait_all(far())
    total = far_rows[0]
    for k in range(1, 2 * HI):
        total = total + far_rows[k]
    obias[...] = total[2:4, :1120]
    ogain[...] = total[0:2, :1120] / gains[...]

    def factors(l):
        recip = col_to_row(kappa[:, l : l + 1]) / gains[l : l + 1, :]
        row = recip * recip * total[l : l + 1, :1120]
        return row, row_to_col(row[:, : SPANS[1][1]])

    def write_right(l, row):
        right = quarters(bufs[l, RG][4])
        or1[l] = right[:C, C2:480] - r1[l].astype(F32) * row[:, SPANS[2][0] : SPANS[2][1]]
        tail = right[C:]
        skip = jnp.concatenate([tail[:, :C], tail[:, C:C2], tail[:8, C2:480]], axis=0)
        os[l] = skip - vs[l].astype(F32) * row[:, SPANS[3][0] : SPANS[3][1]]
        or2[l] = right[:C, :C2] - r2[l].astype(F32) * row[:, SPANS[4][0] : SPANS[4][1]]

    def turned(l, kind):
        flat = quarters(bufs[l, kind][4]).T
        return jnp.concatenate([flat[C * p : C * (p + 1)] for p in range(3)], axis=1)

    def write_down(l, kind, col):
        if kind == DC:
            o1[l] = turned(l, kind) - v1[l].astype(F32) * col[:C]
        else:
            first = 0 if kind == DA else C
            part = slice(first, first + C)
            o2[l, part] = turned(l, kind) - v2[l, part].astype(F32) * col[C + first : C2 + first]

    row_1, col_1 = factors(1)
    row_0, col_0 = factors(0)
    steps((0, DA, 3), (0, DB, 3))()
    write_right(1, row_1)
    steps((0, DC, 3))()
    for kind in (DA, DB, DC):
        write_down(1, kind, col_1)
    wait(0, RG, 4)
    write_right(0, row_0)
    steps((0, DA, 4), (0, DB, 4), (0, DC, 4))()
    for kind in (DA, DB, DC):
        wait(0, kind, 4)
        write_down(0, kind, col_0)
    out_right.wait()
    out_down.wait()


def sum_shape(kind):
    return (2, 2, 2, HI, ROWS[kind], 128)


def run_backward_sums(down_cot, right_cot, kept, weights, mask, kappa, gains, v1, v2, r1, vs, r2):
    n = down_cot.shape[0]
    sds = jax.ShapeDtypeStruct
    vmem = pl.BlockSpec(memory_space=pltpu.VMEM)
    hbm = pl.BlockSpec(memory_space=pl.ANY)
    V = pltpu.VMEM
    wide = V((n, C2, PX), BF)
    flow = (n, C, PX)
    scratch = [V((n, 32, 32, C), BF)] * 2 + [V(flow, F32)] * 2 + [wide] * 8
    scratch += [V((8, 480, 256), BF), V((1280, 512), BF), V((C2, C), BF)]
    scratch += [V((2, C2, 480), BF), V((2, C2, 960), BF), V((C2, 640), BF), V((C2, 1280), BF)]
    scratch += [V((2, C2, 480), F32), V((2, C2, 960), F32), V((C2, 640), F32), V((C2, 1280), F32), V((C2, C), F32)]
    scratch += [V((LAYERS, 1120, 128), F32)]
    scratch += [V((1280, 1152), BF), V((480, 1152), BF), V((640, PX), BF), V((C, PX), BF), V((n, C, PX), BF)]
    scratch += [V(sum_shape(kind), BF) for l in range(LAYERS) for kind in KINDS]
    for l in range(LAYERS):
        for kind in KINDS:
            tail = (ROWS[kind], 128)
            scratch += [
                V((2, 2, HI) + tail, BF),
                V((2, HI) + tail, BF),
                V((HI,) + tail, BF),
                V((HI - 1,) + tail, BF),
                V((2, 2) + tail, BF),
            ]
    sem = pltpu.SemaphoreType.DMA
    scratch += [V((4, 8, 1152), F32), V((2 * HI, 8, 1152), F32), sem((72,)), sem((72,)), sem((10,)), sem((10,)), sem((24,)), sem((2,))]
    return pl.pallas_call(
        backward_kernel,
        in_specs=[hbm] * 11 + [vmem] * 8,
        out_specs=[hbm] * 2 + [vmem] * 7,
        out_shape=[sds(flow, F32)] * 2 + [sds(v.shape, F32) for v in (v1, v2, r1, vs, r2)] + [sds((LAYERS, 1120), F32)] * 2,
        scratch_shapes=scratch,
        compiler_params=pltpu.CompilerParams(
            vmem_limit_bytes=63 << 20, collective_id=1, has_side_effects=True
        ),
        name="backward_sums",
    )(down_cot, right_cot, *kept, *weights, mask, kappa, gains, v1, v2, r1, vs, r2)


def write_kernel(*refs):
    flows, small = refs[:4], refs[4:11]
    photos, results = refs[11:15], refs[15:]
    for flow, photo in zip(flows, photos):
        for v in range(4):
            tile = flow[0, :, at(v)].T
            for g in range(4):
                photo[0, g, v] = tile[g * 32 : (g + 1) * 32]

    @pl.when((pl.program_id(0) == 0) & (pl.program_id(1) == 0))
    def _():
        for src, dst in zip(small, results):
            dst[...] = src[...]


def run_write(flows, small):
    n = flows[0].shape[0]
    sds = jax.ShapeDtypeStruct

    def fixed(a):
        zeros = (0,) * a.ndim
        return pl.BlockSpec(a.shape, lambda i, h: zeros, pipeline_mode=pl.Buffered(1))

    out = pl.pallas_call(
        write_kernel,
        grid=(n, 2),
        in_specs=[pl.BlockSpec((1, C, PX // 2), lambda i, h: (i, 0, h))] * 4 + [fixed(a) for a in small],
        out_specs=[pl.BlockSpec((1, 4, 4, 32, C), lambda i, h: (i, 0, h, 0, 0))] * 4 + [fixed(a) for a in small],
        out_shape=[sds((n, 4, 8, 32, C), f.dtype) for f in flows] + [sds(a.shape, a.dtype) for a in small],
        compiler_params=pltpu.CompilerParams(vmem_limit_bytes=63 << 20),
        name="write",
    )(*flows, *small)
    return [a.reshape(n, 32, 32, C) for a in out[:4]] + list(out[4:])


def general_finish(lower, upper, whole_v, shards, gains):
    rows = lax.psum(jnp.stack([lower[4], upper[4]]), ("dp", "grp"))
    sums = []
    units = []
    inverse = []
    for m, (low, high) in enumerate(zip(unpack(*lower[:4]), unpack(*upper[:4]))):
        part = lax.psum_scatter(jnp.stack([low, high]), "dp", scatter_dimension=1, tiled=True)
        sums.append(lax.psum(part, "grp").astype(F32))
        vals = whole_v[m].astype(F32)
        inv = lax.rsqrt(jnp.sum(vals * vals, axis=1))
        inverse.append(inv)
        units.append(shards[m].astype(F32) * inv[:, None, :])
    inverse = jnp.concatenate(inverse, axis=1)
    dots = rows[:, 0] * inverse
    grads = [sums[m] - units[m] * dots[:, None, lo:hi] for m, (lo, hi) in enumerate(SPANS)]
    return (*grads, rows[:, 0] / gains, rows[:, 1])


def on_device(
    quick,
    down_in,
    right_in,
    pixel_mask,
    down_cot,
    right_cot,
    v_down1,
    v_down2,
    v_right1,
    v_skip,
    v_right2,
    gains,
    biases,
):
    shards = (v_down1, v_down2, v_right1, v_skip, v_right2)
    n = down_in.shape[0]
    if quick and n > 2:
        turned = (v_down1.swapaxes(1, 2), v_down2.swapaxes(1, 2), v_right1, v_skip, v_right2)
        down_last, right_last, *rest = run_forward_gather(down_in, right_in, *turned, gains, biases)
        kept, weights, kappa = rest[:6], rest[6:9], rest[9]
        down_g, right_g, *small = run_backward_sums(
            down_cot, right_cot, kept, weights, pixel_mask, kappa, gains, *turned
        )
        down_out, right_out, down_grad, right_grad, *grads = run_write(
            (down_last, right_last, down_g, right_g), small
        )
        grads[0] = grads[0].swapaxes(1, 2)
        grads[1] = grads[1].swapaxes(1, 2)
        return (down_out, right_out, down_grad, right_grad, *grads)
    whole_v = tuple(lax.all_gather(v, "dp", axis=1, tiled=True) for v in shards)
    weights = assemble(*whole_v)
    cols = jnp.concatenate([gains, biases], axis=0).T
    down_out, right_out, *kept, kappa = run_forward(down_in, right_in, *weights, cols)
    mask = pixel_mask.reshape(n, 4, 8, 32).transpose(0, 2, 1, 3).reshape(n, 1, 1024).astype(F32)
    down_g, right_g, cells_g, *upper = run_backward(1, down_cot, right_cot, None, mask, kept, kappa, *weights)
    down_grad, right_grad, *lower = run_backward(0, down_g, right_g, cells_g, mask, kept, kappa, *weights)
    grads = general_finish(lower, upper, whole_v, shards, gains)
    return (down_out, right_out, down_grad, right_grad, *grads)


def solution(mesh):
    photo = P(("dp", "grp"), None, None, None)
    rows = P(None, "dp", None)
    quick = mesh.shape["dp"] == 2 * HI and mesh.shape["grp"] == 4
    return jax.shard_map(
        functools.partial(on_device, quick),
        mesh=mesh,
        in_specs=(photo, photo, P(("dp", "grp"), None, None), photo, photo) + (rows,) * 5 + (P(), P()),
        out_specs=(photo,) * 4 + (rows,) * 5 + (P(), P()),
        check_vma=False,
    )
```

```python
import functools
import jax
import jax.numpy as jnp
from jax import lax
from jax.experimental import pallas as pl
from jax.experimental.pallas import tpu as pltpu
from jax.sharding import PartitionSpec as P

BF = jnp.bfloat16
F32 = jnp.float32
LAYERS = 2
HI = 4
MESH = pl.DeviceIdType.MESH
C = 160
C2 = 320
SPANS = ((0, 160), (160, 480), (480, 640), (640, 800), (800, 1120))


def nt(a, b):
    return lax.dot_general(a, b, (((1,), (1,)), ((), ())), preferred_element_type=F32)


def nn(a, b):
    return lax.dot_general(a, b, (((1,), (0,)), ((), ())), preferred_element_type=F32)


def eye(n):
    same = lax.broadcasted_iota(jnp.int32, (n, n), 0) == lax.broadcasted_iota(jnp.int32, (n, n), 1)
    return jnp.where(same, 1.0, 0.0).astype(BF)


def lane():
    return lax.broadcasted_iota(jnp.int32, (1, 128), 1)


def keep(cond, tile):
    return jnp.where(cond, tile, jnp.zeros((), tile.dtype))


def col_shift(tile, off):
    if off == 0:
        return tile
    col = lane() & 31
    if off == 1:
        return keep(col != 31, pltpu.roll(tile, 127, 1))
    return keep(col != 0, pltpu.roll(tile, 1, 1))


def row_before(tile):
    return keep(lane() >= 32, pltpu.roll(tile, 32, 1))


def row_after(tile):
    return keep(lane() < 96, pltpu.roll(tile, 96, 1))


def at(v):
    return slice(v * 128, (v + 1) * 128)


def put_down(ext, v, tile):
    n = tile.shape[0]
    for c in range(3):
        moved = col_shift(tile, c - 1)
        ext[c * n : (c + 1) * n, at(v + 1)] = moved
        if v == 7:
            ext[c * n : (c + 1) * n, at(0)] = row_before(moved)


def put_right(ext, v, tile):
    n = tile.shape[0]
    for c in range(2):
        moved = col_shift(tile, c - 1)
        ext[(2 + c) * n : (3 + c) * n, at(v)] = moved
        if v == 7:
            ext[c * n : (c + 1) * n, at(0)] = row_before(moved)
        else:
            ext[c * n : (c + 1) * n, at(v + 1)] = moved


def put_down_back(ext, v, tile):
    n = tile.shape[0]
    for c in range(3):
        moved = col_shift(tile, 1 - c)
        ext[c * n : (c + 1) * n, at(v)] = moved
        if v == 0:
            ext[c * n : (c + 1) * n, at(8)] = row_after(moved)


def put_right_back(ext, v, tile):
    n = tile.shape[0]
    for c in range(2):
        moved = col_shift(tile, 1 - c)
        ext[(2 + c) * n : (3 + c) * n, at(v)] = moved
        if v == 0:
            ext[c * n : (c + 1) * n, at(7)] = row_after(moved)
        else:
            ext[c * n : (c + 1) * n, at(v - 1)] = moved


def pair_elu(x):
    e = jnp.exp(-jnp.abs(x)) - 1.0
    up = x > 0
    return jnp.concatenate([jnp.where(up, x, e), jnp.where(up, e, -x)], axis=0).astype(BF)


def elu_back(grad, act):
    slope = jnp.minimum(act.astype(F32), 0.0) + 1.0
    both = grad * slope
    return both[:C] - both[C:]


def sigmoid(x):
    return 1.0 / (1.0 + jnp.exp(-x))


def load_cells(ref, v):
    rows = jnp.concatenate([ref[g * 8 + v] for g in range(4)], axis=0)
    return rows.T.astype(F32)


def store_bf16(ref, v, tile):
    out = tile.astype(BF).T
    for g in range(4):
        ref[g * 8 + v] = out[g * 32 : (g + 1) * 32]


def store_f32(ref, v, tile):
    out = tile.T
    for g in range(4):
        ref[g * 8 + v] = out[g * 32 : (g + 1) * 32]


def scale_of(total, gain):
    return gain * lax.rsqrt(total)


def square_sum(vals):
    vals = vals.astype(F32)
    return jnp.sum(vals * vals, axis=1, keepdims=True)


def block_square_sum(weight, lo, hi):
    total = None
    for k in range(8):
        vals = weight[k, lo:hi, :240].astype(F32)
        total = vals * vals if total is None else total + vals * vals
    return jnp.sum(total, axis=1, keepdims=True)


def down_product(weight, first, count, ext, j):
    acc = None
    for k in range(8):
        lo = j * 256 + 128 * (k // 4)
        part = nn(weight[k, first : first + count, :240], ext[240 * (k % 4) : 240 * (k % 4) + 240, lo : lo + 256])
        acc = part if acc is None else acc + part
    return acc


def fwd_kernel(
    down_in, right_in, wd, wr, wk, cols,
    down_out, right_out, cells, actd, actr, acth, gated, gater, kappa,
    right_t, skip_t, ext, ext4, dflow, rflow,
):
    @pl.when(pl.program_id(0) == 0)
    def _():
        for l in range(LAYERS):
            for k in range(4):
                rows = wr[l, k * C2 : (k + 1) * C2, :480]
                right_t[l, :, k * C2 : (k + 1) * C2] = nt(eye(480), rows).astype(BF)
            skip_t[l] = nt(eye(C), wk[l]).astype(BF)
            down_total = sum(square_sum(wd[l, k, :, :240]) for k in range(8))
            right_total = square_sum(right_t[l])
            totals = (down_total[C2:], down_total[:C2], right_total[C2:], square_sum(skip_t[l]), right_total[:C2])
            for total, (lo, hi) in zip(totals, SPANS):
                kappa[lo:hi, l : l + 1] = scale_of(total, cols[lo:hi, l : l + 1])

    for v in range(8):
        x = load_cells(down_in.at[0], v)
        dflow[:, at(v)] = x
        act = pair_elu(x)
        cells[0, 0, :, at(v)] = act
        put_down(ext, v, act)
        rflow[:, at(v)] = load_cells(right_in.at[0], v)
    for l in range(LAYERS):
        def scale(m):
            lo, hi = SPANS[m]
            return kappa[lo:hi, l : l + 1]

        def bias(m):
            lo, hi = SPANS[m]
            return cols[lo:hi, 2 + l : 3 + l]

        for j in range(4):
            acc = down_product(wd.at[l], C2, C, ext, j)
            for h in range(2):
                v = 2 * j + h
                actd[l, 0, :, at(v)] = pair_elu(acc[:, at(h)] * scale(0) + bias(0))
        for v in range(8):
            put_down(ext, v, actd[l, 0, :, at(v)])
            act = pair_elu(rflow[:, at(v)])
            actr[l, 0, :, at(v)] = act
            put_right(ext4, v, act)
        for j in range(4):
            acc = down_product(wd.at[l], 0, C2, ext, j)
            for h in range(2):
                v = 2 * j + h
                gate = acc[:, at(h)] * scale(1) + bias(1)
                t = gate[:C]
                s = sigmoid(gate[C:])
                gated[l, 0, :C, at(v)] = t.astype(BF)
                gated[l, 0, C:, at(v)] = s.astype(BF)
                new = dflow[:, at(v)] + t * s
                dflow[:, at(v)] = new
                cells[l + 1, 0, :, at(v)] = pair_elu(new)
        skip_bias = bias(2) + bias(3)
        for j in range(4):
            acc = nn(right_t[l, C2:], ext4[:, j * 256 : j * 256 + 256]) * scale(2)
            acc = acc + nn(skip_t[l], cells[l + 1, 0, :, j * 256 : j * 256 + 256]) * scale(3)
            for h in range(2):
                v = 2 * j + h
                acth[l, 0, :, at(v)] = pair_elu(acc[:, at(h)] + skip_bias)
        for v in range(8):
            put_right(ext4, v, acth[l, 0, :, at(v)])
            if l + 1 < LAYERS:
                put_down(ext, v, cells[l + 1, 0, :, at(v)])
        for j in range(4):
            acc = nn(right_t[l, :C2], ext4[:, j * 256 : j * 256 + 256])
            for h in range(2):
                v = 2 * j + h
                gate = acc[:, at(h)] * scale(4) + bias(4)
                t = gate[:C]
                s = sigmoid(gate[C:])
                gater[l, 0, :C, at(v)] = t.astype(BF)
                gater[l, 0, C:, at(v)] = s.astype(BF)
                rflow[:, at(v)] = rflow[:, at(v)] + t * s
    for v in range(8):
        store_bf16(down_out.at[0], v, dflow[:, at(v)])
        store_bf16(right_out.at[0], v, rflow[:, at(v)])


def gate_back(g, t, s):
    p = g * s
    q = p * t * (1.0 - s)
    return jnp.concatenate([p, q], axis=0)


def bwd_kernel(
    top, down_g, right_g, mask, *refs,
):
    refs = list(refs)
    cells_g = None if top else refs.pop(0)
    (
        low_cells, high_cells, actd, actr, acth, gated, gater, kappa, wd, wr, wk,
    ) = refs[:11]
    refs = refs[11:]
    if top:
        down_out, right_out, cells_out = refs[:3]
        refs = refs[3:]
    else:
        down_out, right_out = refs[:2]
        refs = refs[2:]
    (
        o_rg, o_da, o_db, o_dc, orows,
        b1, b2, br1, br2, g1, g2, gr1, gs, gr2, bsum, ext, ext1, ext4, ext41, dskip, gdown, gright,
    ) = refs
    layer = 1 if top else 0
    step = pl.program_id(0)

    @pl.when(step == 0)
    def _():
        down_taps(wd.at[0], b1, b2)
        right_taps(wr.at[0], br1, br2)
        for acc in (g1, g2, gr1, gs, gr2, bsum):
            acc[...] = jnp.zeros(acc.shape, F32)

    def scale(m):
        lo, hi = SPANS[m]
        return kappa[lo:hi, layer : layer + 1]

    def add_bias(m, total):
        lo, hi = SPANS[m]
        bsum[lo:hi, :] += total

    total = None
    for v in range(8):
        if top:
            m = mask[0, :, at(v)]
            gdown[:, at(v)] = load_cells(down_g.at[0], v) * m
            g = load_cells(right_g.at[0], v) * m
            gright[:, at(v)] = g
        else:
            g = right_g[0, :, at(v)]
        d = gate_back(g, gater[0, 0, :C, at(v)].astype(F32), gater[0, 0, C:, at(v)].astype(F32))
        total = d if total is None else total + d
        put_right_back(ext4, v, (d * scale(4)).astype(BF))
    add_bias(4, total)
    gr2[...] += nt(acth[0, 0], ext4[...])
    total = None
    for j in range(4):
        e = nn(br2[...], ext4[:, j * 256 : j * 256 + 256])
        for h in range(2):
            v = 2 * j + h
            d = elu_back(e[:, at(h)], acth[0, 0, :, at(v)])
            total = d if total is None else total + d
            put_right_back(ext41, v, (d * scale(2)).astype(BF))
            dskip[:, at(v)] = (d * scale(3)).astype(BF)
    add_bias(2, total)
    add_bias(3, total)
    gr1[...] += nt(actr[0, 0], ext41[...])
    gs[...] += nt(high_cells[0, 0], dskip[...])
    for j in range(4):
        e = nn(br1[...], ext41[:, j * 256 : j * 256 + 256])
        k = nn(wk[0], dskip[:, j * 256 : j * 256 + 256])
        for h in range(2):
            v = 2 * j + h
            old = gright[:, at(v)] if top else right_g[0, :, at(v)]
            new = old + elu_back(e[:, at(h)], actr[0, 0, :, at(v)])
            if top:
                right_out[0, :, at(v)] = new
            else:
                store_f32(right_out.at[0], v, new)
            gc = k[:, at(h)]
            if not top:
                gc = gc + cells_g[0, :, at(v)].astype(F32)
            old = gdown[:, at(v)] if top else down_g[0, :, at(v)]
            gdown[:, at(v)] = old + elu_back(gc, high_cells[0, 0, :, at(v)])
    total = None
    for v in range(8):
        g = gdown[:, at(v)]
        if top:
            down_out[0, :, at(v)] = g
        d = gate_back(g, gated[0, 0, :C, at(v)].astype(F32), gated[0, 0, C:, at(v)].astype(F32))
        total = d if total is None else total + d
        put_down_back(ext, v, (d * scale(1)).astype(BF))
    add_bias(1, total)
    for a in range(2):
        lo = 128 * (1 - a)
        g2[a] += nt(actd[0, 0], ext[:, lo : lo + 1024])
    total = None
    for j in range(4):
        e = nn(b2[1], ext[:, j * 256 : j * 256 + 256])
        e = e + nn(b2[0], ext[:, j * 256 + 128 : j * 256 + 384])
        for h in range(2):
            v = 2 * j + h
            d = elu_back(e[:, at(h)], actd[0, 0, :, at(v)])
            total = d if total is None else total + d
            put_down_back(ext1, v, (d * scale(0)).astype(BF))
    add_bias(0, total)
    for a in range(2):
        lo = 128 * (1 - a)
        g1[a] += nt(low_cells[0, 0], ext1[:, lo : lo + 1024])
    for j in range(4):
        e = nn(b1[1], ext1[:, j * 256 : j * 256 + 256])
        e = e + nn(b1[0], ext1[:, j * 256 + 128 : j * 256 + 384])
        if top:
            cells_out[0, :, j * 256 : j * 256 + 256] = e.astype(BF)
        else:
            for h in range(2):
                v = 2 * j + h
                last = gdown[:, at(v)] + elu_back(e[:, at(h)], low_cells[0, 0, :, at(v)])
                store_f32(down_out.at[0], v, last)

    @pl.when(step == pl.num_programs(0) - 1)
    def _():
        pack_right(o_rg, gr2, gr1, gs)
        pack_down(o_da, DA, g2, C2, 0)
        pack_down(o_db, DB, g2, C2, C)
        pack_down(o_dc, DC, g1, C, 0)
        orows[0:1, :] = jnp.concatenate(
            [
                dot_rows(b1[0], g1[0], C, 3) + dot_rows(b1[1], g1[1], C, 3),
                dot_rows(b2[0], g2[0], C2, 3) + dot_rows(b2[1], g2[1], C2, 3),
                dot_rows(br1[...], gr1[...], C, 4),
                dot_rows(wk[0], gs[...], C, 1),
                dot_rows(br2[...], gr2[...], C2, 4),
            ],
            axis=1,
        )
        orows[1:2, :] = jnp.sum(bsum[...].T, axis=0, keepdims=True)


def whole(shape, dtype=None):
    zeros = (0,) * len(shape)
    return pl.BlockSpec(shape, lambda i: zeros)


def once(shape):
    zeros = (0,) * len(shape)
    return pl.BlockSpec(shape, lambda i: zeros, pipeline_mode=pl.Buffered(1))


def image(shape):
    rest = (0,) * (len(shape) - 1)
    return pl.BlockSpec(shape, lambda i: (i,) + rest)


PX = 1024


def run_forward(down_in, right_in, wd, wr, wk, cols):
    n = down_in.shape[0]
    sds = jax.ShapeDtypeStruct
    kept = [(3, C2, PX)] + [(LAYERS, C2, PX)] * 5
    return pl.pallas_call(
        fwd_kernel,
        grid=(n,),
        in_specs=[image((1, 32, 32, C))] * 2 + [once(w.shape) for w in (wd, wr, wk)] + [once((1120, 4))],
        out_specs=[image((1, 32, 32, C))] * 2
        + [pl.BlockSpec((s[0], 1) + s[1:], lambda i: (0, i, 0, 0)) for s in kept]
        + [once((1120, 2))],
        out_shape=[sds((n, 32, 32, C), BF)] * 2
        + [sds((s[0], n) + s[1:], BF) for s in kept]
        + [sds((1120, 2), F32)],
        scratch_shapes=[
            pltpu.VMEM((LAYERS, 480, 1280), BF),
            pltpu.VMEM((LAYERS, C, C2), BF),
            pltpu.VMEM((960, 1152), BF),
            pltpu.VMEM((1280, PX), BF),
            pltpu.VMEM((C, PX), F32),
            pltpu.VMEM((C, PX), F32),
        ],
        compiler_params=pltpu.CompilerParams(vmem_limit_bytes=60 << 20),
        name="forward",
    )(down_in, right_in, wd, wr, wk, cols)


def run_backward(layer, down_g, right_g, cells_g, mask, kept, kappa, wd, wr, wk):
    n = down_g.shape[0]
    top = layer == 1
    sds = jax.ShapeDtypeStruct
    flow = image((1, C, PX))
    wide = image((1, C2, PX))

    def pick(which):
        return pl.BlockSpec((1, 1, C2, PX), lambda i: (which, i, 0, 0))

    def one_layer(shape):
        rest = (0,) * (len(shape) - 1)
        return pl.BlockSpec((1,) + shape[1:], lambda i: (layer,) + rest, pipeline_mode=pl.Buffered(1))

    cells = kept[0]
    ins = [down_g, right_g, mask] + ([] if top else [cells_g]) + [cells, cells] + list(kept[1:]) + [kappa, wd, wr, wk]
    photo = image((1, 32, 32, C))
    in_specs = (
        ([photo] * 2 if top else [flow] * 2)
        + [image((1, 1, PX))]
        + ([] if top else [wide])
        + [pick(layer), pick(layer + 1)]
        + [pick(layer)] * 5
        + [once((1120, 2))]
        + [one_layer(w.shape) for w in (wd, wr, wk)]
    )
    if top:
        out_specs = [flow, flow, wide]
        out_shape = [sds((n, C, PX), F32)] * 2 + [sds((n, C2, PX), BF)]
    else:
        out_specs = [photo] * 2
        out_shape = [sds((n, 32, 32, C), F32)] * 2
    return pl.pallas_call(
        functools.partial(bwd_kernel, top),
        grid=(n,),
        in_specs=in_specs,
        out_specs=out_specs + [once(sum_shape(kind)) for kind in KINDS] + [once((2, 1120))],
        out_shape=out_shape + [sds(sum_shape(kind), BF) for kind in KINDS] + [sds((2, 1120), F32)],
        scratch_shapes=[
            pltpu.VMEM((2, 320, 480), BF),
            pltpu.VMEM((2, 320, 960), BF),
            pltpu.VMEM((320, 640), BF),
            pltpu.VMEM((320, 1280), BF),
            pltpu.VMEM((2, 320, 480), F32),
            pltpu.VMEM((2, 320, 960), F32),
            pltpu.VMEM((320, 640), F32),
            pltpu.VMEM((320, 160), F32),
            pltpu.VMEM((320, 1280), F32),
            pltpu.VMEM((1120, 128), F32),
            pltpu.VMEM((960, 1152), BF),
            pltpu.VMEM((480, 1152), BF),
            pltpu.VMEM((1280, 1024), BF),
            pltpu.VMEM((640, 1024), BF),
            pltpu.VMEM((160, 1024), BF),
            pltpu.VMEM((C, PX), F32),
            pltpu.VMEM((C, PX), F32),
        ],
        compiler_params=pltpu.CompilerParams(vmem_limit_bytes=60 << 20),
        name="backward%d" % layer,
    )(*ins)


def assemble(v1, v2, r1, vs, r2):
    rows = jnp.concatenate([v2, v1], axis=2).reshape(LAYERS, 8, 240, 480)
    wd = jnp.pad(rows.swapaxes(2, 3), ((0, 0), (0, 0), (0, 0), (0, 16)))
    wr = jnp.pad(jnp.concatenate([r2, r1], axis=2), ((0, 0), (0, 0), (0, 32)))
    return wd, wr, vs


def unpack(*packed):
    blocks = []
    for kind, g in zip(KINDS, packed):
        order = (3, 1, 4, 0, 2, 5) if X_FIRST[kind] else (3, 2, 4, 0, 1, 5)
        blocks.append(g.transpose(order).reshape(8, ROWS[kind], 512))

    def down(block):
        return block[:, :, :480].reshape(8, 80, 3, C).swapaxes(1, 2).reshape(1920, C)

    right = blocks[0][:, :C].reshape(1280, 512)
    tail = blocks[0][:, C:, :480].reshape(8, 16, 3, C).swapaxes(1, 2).reshape(8, 48, C)
    skip = tail[:, :40].reshape(C2, C)
    down2 = jnp.concatenate([down(blocks[1]), down(blocks[2])], axis=1)
    return down(blocks[3]), down2, right[:, C2:480], skip, right[:, :C2]


def peers(hi_count):
    me = lax.axis_index("dp")
    grp = lax.axis_index("grp")
    hi, lo = me // 2, lax.rem(me, 2)
    y, core = grp // 2, lax.rem(grp, 2)
    return me, grp, hi, lo, y, core


def meet(me, grp, hi, lo, y, core, everyone):
    barrier = pltpu.get_barrier_semaphore()
    near = [((hi + k) % HI * 2 + lo, grp) for k in range(1, HI)]
    near += [(hi * 2 + 1 - lo, grp)]
    if everyone:
        near += [((hi + k) % HI * 2 + 1 - lo, grp) for k in range(1, HI)]
    near += [(me, (grp + k) % 4) for k in range(1, 4)]
    for device in near:
        pl.semaphore_signal(barrier, inc=1, device_id=device, device_id_type=MESH)
    pl.semaphore_wait(barrier, len(near))


def send(src, dst, sems, at_, device):
    return pltpu.make_async_remote_copy(
        src_ref=src,
        dst_ref=dst,
        send_sem=sems[0].at[at_],
        recv_sem=sems[1].at[at_],
        device_id=device,
        device_id_type=MESH,
    )


def start_all(copies):
    for copy in copies:
        copy.start()


def wait_all(copies):
    for copy in copies:
        copy.wait()


def add_into(dst, src):
    dst[...] = (dst[...].astype(F32) + src[...].astype(F32)).astype(BF)


def col_to_row(col):
    return jnp.broadcast_to(col, (col.shape[0], 128)).T[0:1, :]


def row_to_col(row):
    return jnp.broadcast_to(row, (128, row.shape[1])).T[:, 0:1]


def quarters(fin):
    return jnp.concatenate([fin[q // 2, q % 2].astype(F32) for q in range(4)], axis=1)


D1, D2A, D2B, RA, RB = 0, 1, 2, 3, 4
PIECE = {D1: (80, 256), D2A: (40, 256), D2B: (80, 256), RA: (88, 128), RB: (176, 128)}


def gather_copies(kind, stage, buf, sems, first, ids):
    me, grp, hi, lo, y, core = ids
    if kind in (D2A, RA):
        mine, line, plane = buf.at[core, y, lo, hi], buf.at[core, y, lo], buf.at[core, y]
    else:
        mine, line, plane = buf.at[core, lo, hi], buf.at[core, lo], None
    if stage == "z":
        return [
            send(mine, mine, sems, first + k - 1, (lax.rem(hi + k, HI) * 2 + lo, grp)) for k in range(1, HI)
        ]
    if stage == "x":
        return [send(line, line, sems, first + HI - 1, (hi * 2 + 1 - lo, grp))]
    if stage == "y":
        return [send(plane, plane, sems, first + HI, (me, (1 - y) * 2 + core))]
    part = buf.at[core]
    return [send(part, part, sems, first + HI + 1, (me, y * 2 + 1 - core))]


def forward_kernel(
    down_in, right_in, v1, v2, r1, vs, r2, gains, biases,
    down_out, right_out, cells_o, actd_o, actr_o, acth_o, gated_o, gater_o, wd_o, wr_o, wk_o, kappa,
    cells, actd, actr, acth, gated, gater, wd, wr, wk,
    b_d1, b_d2a, b_d2b, b_ra, b_rb, own_d, own_q, own_ra, own_rb, right_t, skip_t, ext, ext4, dflow, rflow, photo_d, photo_r, dlast, rlast, bias_col,
    send_sems, recv_sems, in_sems, out_sems,
):
    n = down_in.shape[0]
    ids = peers(HI)
    me, grp, hi, lo, y, core = ids
    sems = (send_sems, recv_sems)
    load_d = pltpu.make_async_copy(down_in, photo_d, in_sems.at[0])
    load_r = pltpu.make_async_copy(right_in, photo_r, in_sems.at[1])
    load_d.start()
    load_r.start()
    meet(*ids, False)
    bufs = {D1: b_d1, D2A: b_d2a, D2B: b_d2b, RA: b_ra, RB: b_rb}

    def copies(l, kind, stage):
        return gather_copies(kind, stage, bufs[kind].at[l], sems, (l * 5 + kind) * 6, ids)

    def start(l, kind, stage):
        start_all(copies(l, kind, stage))

    def wait(l, kind, stage):
        wait_all(copies(l, kind, stage))

    for l in range(LAYERS):
        own_d[l, :C2, :240] = v2[l]
        own_d[l, C2:, :240] = v1[l]
        own_d[l, :, 240:] = jnp.zeros((480, 16), BF)
        b_d1[l, core, lo, hi] = own_d[l, pl.ds(pl.multiple_of(C2 + core * 80, 16), 80), :]
        if l == 0:
            start(0, D1, "z")
        for q in range(4):
            own_q[l, q] = own_d[l, q * 40 : q * 40 + 40, :]
        b_d2a[l, core, y, lo, hi] = own_q[l, core * 2 + y]
        b_d2b[l, core, lo, hi] = own_d[l, pl.ds(pl.multiple_of(C + core * 80, 16), 80), :]
        skip = vs[l].astype(F32)
        third = jnp.concatenate([skip[32:], jnp.zeros((8, C), F32)], axis=0)
        tail = jnp.concatenate([skip[:16], skip[16:32], third], axis=1)
        right = jnp.concatenate([r2[l], r1[l]], axis=1).astype(F32)
        right = jnp.concatenate([right, tail], axis=0)
        right = jnp.concatenate([right, jnp.zeros((176, 32), F32)], axis=1).astype(BF)
        for q in range(4):
            own_ra[l, q] = right[(q % 2) * 88 : (q % 2) * 88 + 88, at(q // 2)]
        for c in range(2):
            own_rb[l, c] = right[:, at(2 + c)]
        b_ra[l, core, y, lo, hi] = own_ra[l, core * 2 + y]
        b_rb[l, core, lo, hi] = own_rb[l, core]

    def unpack_d1(l):
        for k in range(8):
            for c in range(2):
                wd[l, k, C2 + c * 80 : C2 + c * 80 + 80, :] = b_d1[l, c, k % 2, k // 2]

    def unpack_d2(l):
        for k in range(8):
            for q in range(4):
                wd[l, k, q * 40 : q * 40 + 40, :] = b_d2a[l, q // 2, q % 2, k % 2, k // 2]
            for c in range(2):
                wd[l, k, C + c * 80 : C + c * 80 + 80, :] = b_d2b[l, c, k % 2, k // 2]

    def unpack_rt(l):
        for k in range(8):
            tail = []
            for c in range(2):
                halves = [b_ra[l, c, h, k % 2, k // 2].astype(F32) for h in range(2)]
                tile = jnp.concatenate(halves, axis=0)
                wr[l, k * C : (k + 1) * C, at(c)] = tile[:C].astype(BF)
                tail.append(tile[C:])
            for c in range(2):
                tile = b_rb[l, c, k % 2, k // 2]
                wr[l, k * C : (k + 1) * C, at(2 + c)] = tile[:C]
                tail.append(tile[C:].astype(F32))
            tail = jnp.concatenate(tail, axis=1)
            skip = jnp.concatenate([tail[:, :C], tail[:, C:C2], tail[:8, C2:480]], axis=0)
            wk[l, k * 40 : k * 40 + 40, :] = skip.astype(BF)
        for k in range(4):
            rows = wr[l, k * C2 : (k + 1) * C2, :480]
            right_t[l, :, k * C2 : (k + 1) * C2] = nt(eye(480), rows).astype(BF)
        skip_t[l] = nt(eye(C), wk[l]).astype(BF)

    def set_scale(l, m, total):
        lo_, hi_ = SPANS[m]
        gain = row_to_col(gains[l : l + 1, lo_:hi_])
        kappa[lo_:hi_, l : l + 1] = scale_of(total, gain)

    def scale(l, m):
        lo_, hi_ = SPANS[m]
        return kappa[lo_:hi_, l : l + 1]

    def bias(l, m):
        lo_, hi_ = SPANS[m]
        return bias_col[lo_:hi_, l : l + 1]

    keep_out = []

    def save(src, dst):
        copy = pltpu.make_async_copy(src, dst, out_sems.at[len(keep_out)])
        copy.start()
        keep_out.append(copy)

    for l in range(LAYERS):
        bias_col[:, l : l + 1] = row_to_col(biases[l : l + 1, :])
    load_d.wait()
    load_r.wait()

    def begin(i, carry):
        for v in range(8):
            x = load_cells(photo_d.at[i], v)
            dflow[i, :, at(v)] = x
            cells[0, i, :, at(v)] = pair_elu(x)
            rflow[i, :, at(v)] = load_cells(photo_r.at[i], v)
        return carry

    wait(0, D1, "z")
    start(0, D1, "x")
    start(0, D2A, "z")
    start(0, D2B, "z")
    lax.fori_loop(0, n, begin, 0)
    save(cells.at[0], cells_o.at[0])
    wait(0, D2A, "z")
    start(0, D2A, "x")
    start(0, RA, "z")
    wait(0, D2B, "z")
    start(0, D2B, "x")
    start(0, RB, "z")
    wait(0, D1, "x")
    start(0, D1, "core")
    wait(0, D2A, "x")
    start(0, D2A, "y")
    wait(0, RA, "z")
    start(0, RA, "x")
    wait(0, D1, "core")

    def part_a(l, hooks):
        unpack_d1(l)
        set_scale(l, 0, block_square_sum(wd.at[l], C2, 480))

        def body(i, carry):
            for v in range(8):
                put_down(ext, v, cells[l, i, :, at(v)])
            for j in range(4):
                acc = down_product(wd.at[l], C2, C, ext, j)
                for h in range(2):
                    v = 2 * j + h
                    actd[l, i, :, at(v)] = pair_elu(acc[:, at(h)] * scale(l, 0) + bias(l, 0))
            for k, hook in hooks.items():
                pl.when(i == k)(hook)
            return carry

        lax.fori_loop(0, n, body, 0)
        save(actd.at[l], actd_o.at[l])

    def part_b(l, hooks):
        unpack_d2(l)
        set_scale(l, 1, block_square_sum(wd.at[l], 0, C2))
        save(wd.at[l], wd_o.at[l])

        def body(i, carry):
            for v in range(8):
                put_down(ext, v, actd[l, i, :, at(v)])
            for j in range(4):
                acc = down_product(wd.at[l], 0, C2, ext, j)
                for h in range(2):
                    v = 2 * j + h
                    gate = acc[:, at(h)] * scale(l, 1) + bias(l, 1)
                    t = gate[:C]
                    s = sigmoid(gate[C:])
                    gated[l, i, :C, at(v)] = t.astype(BF)
                    gated[l, i, C:, at(v)] = s.astype(BF)
                    new = dflow[i, :, at(v)] + t * s
                    dflow[i, :, at(v)] = new
                    cells[l + 1, i, :, at(v)] = pair_elu(new)
                    if l == LAYERS - 1:
                        dlast[i, :, at(v)] = new.astype(BF)
            for k, hook in hooks.items():
                pl.when(i == k)(hook)
            return carry

        lax.fori_loop(0, n, body, 0)
        save(gated.at[l], gated_o.at[l])
        save(cells.at[l + 1], cells_o.at[l + 1])
        if l == LAYERS - 1:
            save(dlast, down_out)

    def part_c(l, hooks):
        unpack_rt(l)
        total = square_sum(right_t[l])
        set_scale(l, 2, total[C2:])
        set_scale(l, 3, square_sum(skip_t[l]))
        set_scale(l, 4, total[:C2])
        save(wr.at[l], wr_o.at[l])
        save(wk.at[l], wk_o.at[l])
        first = len(keep_out)
        outs = [(actr.at[l], actr_o.at[l]), (acth.at[l], acth_o.at[l]), (gater.at[l], gater_o.at[l])]
        if l == LAYERS - 1:
            outs.append((rlast, right_out))

        def body(i, carry):
            for v in range(8):
                act = pair_elu(rflow[i, :, at(v)])
                actr[l, i, :, at(v)] = act
                put_right(ext4, v, act)
            skip_bias = bias(l, 2) + bias(l, 3)
            for j in range(4):
                acc = nn(right_t[l, C2:], ext4[:, j * 256 : j * 256 + 256]) * scale(l, 2)
                acc = acc + nn(skip_t[l], cells[l + 1, i, :, j * 256 : j * 256 + 256]) * scale(l, 3)
                for h in range(2):
                    v = 2 * j + h
                    acth[l, i, :, at(v)] = pair_elu(acc[:, at(h)] + skip_bias)
            for v in range(8):
                put_right(ext4, v, acth[l, i, :, at(v)])
            for j in range(4):
                acc = nn(right_t[l, :C2], ext4[:, j * 256 : j * 256 + 256])
                for h in range(2):
                    v = 2 * j + h
                    gate = acc[:, at(h)] * scale(l, 4) + bias(l, 4)
                    t = gate[:C]
                    s = sigmoid(gate[C:])
                    gater[l, i, :C, at(v)] = t.astype(BF)
                    gater[l, i, C:, at(v)] = s.astype(BF)
                    new = rflow[i, :, at(v)] + t * s
                    if l == LAYERS - 1:
                        rlast[i, :, at(v)] = new.astype(BF)
                    else:
                        rflow[i, :, at(v)] = new
            for k, (src, dst) in enumerate(outs):
                pltpu.make_async_copy(src.at[i], dst.at[i], out_sems.at[first + k]).start()
            for k, hook in hooks.items():
                pl.when(i == k)(hook)
            return carry

        lax.fori_loop(0, n, body, 0)
        for k, (src, dst) in enumerate(outs):
            keep_out.append(pltpu.make_async_copy(src, dst, out_sems.at[first + k]))

    last = n - 1

    def a0_mid():
        wait(0, D2B, "x")
        start(0, D2B, "core")

    def a0_last():
        wait(0, D2A, "y")
        start(0, D2A, "core")
        wait(0, RB, "z")
        start(0, RB, "x")
        start(1, D1, "z")
        start(1, D2A, "z")
        wait(0, RA, "x")
        start(0, RA, "y")

    def b0_mid():
        start(1, D2B, "z")
        wait(1, D1, "z")
        start(1, D1, "x")
        wait(1, D2A, "z")
        start(1, D2A, "x")

    def b0_last():
        wait(0, RA, "y")
        start(0, RA, "core")
        wait(0, RB, "x")
        start(0, RB, "core")
        start(1, RA, "z")
        wait(1, D2B, "z")
        start(1, D2B, "x")

    def c0_first():
        wait(1, D1, "x")
        start(1, D1, "core")
        wait(1, D2A, "x")
        start(1, D2A, "y")
        wait(1, RA, "z")
        start(1, RA, "x")
        start(1, RB, "z")

    def c0_mid():
        wait(1, D2B, "x")
        start(1, D2B, "core")

    def c0_last():
        wait(1, D2A, "y")
        start(1, D2A, "core")
        wait(1, RA, "x")
        start(1, RA, "y")
        wait(1, RB, "z")
        start(1, RB, "x")

    def b1_first():
        wait(1, RA, "y")
        start(1, RA, "core")
        wait(1, RB, "x")
        start(1, RB, "core")

    part_a(0, {1: a0_mid, last: a0_last})
    wait(0, D2A, "core")
    wait(0, D2B, "core")
    part_b(0, {1: b0_mid, last: b0_last})
    wait(0, RA, "core")
    wait(0, RB, "core")
    part_c(0, {0: c0_first, 1: c0_mid, last: c0_last})
    wait(1, D1, "core")
    part_a(1, {})
    wait(1, D2A, "core")
    wait(1, D2B, "core")
    part_b(1, {0: b1_first})
    wait(1, RA, "core")
    wait(1, RB, "core")
    part_c(1, {})
    for copy in keep_out:
        copy.wait()


def run_forward_gather(down_in, right_in, v1, v2, r1, vs, r2, gains, biases):
    n = down_in.shape[0]
    sds = jax.ShapeDtypeStruct
    vmem = pl.BlockSpec(memory_space=pltpu.VMEM)
    hbm = pl.BlockSpec(memory_space=pl.ANY)
    act = (LAYERS, n, C2, PX)
    kept = [(LAYERS + 1, n, C2, PX)] + [act] * 5
    weights = [(LAYERS, 8, 480, 256), (LAYERS, 1280, 512), (LAYERS, C2, C)]
    photo = (n, 32, 32, C)
    return pl.pallas_call(
        forward_kernel,
        in_specs=[hbm] * 2 + [vmem] * 7,
        out_specs=[hbm] * 11 + [vmem],
        out_shape=[sds((n, C, PX), BF)] * 2 + [sds(s, BF) for s in kept + weights] + [sds((1120, 2), F32)],
        scratch_shapes=[pltpu.VMEM(s, BF) for s in kept + weights]
        + [
            pltpu.VMEM((LAYERS, 2, 2, HI) + PIECE[D1], BF),
            pltpu.VMEM((LAYERS, 2, 2, 2, HI) + PIECE[D2A], BF),
            pltpu.VMEM((LAYERS, 2, 2, HI) + PIECE[D2B], BF),
            pltpu.VMEM((LAYERS, 2, 2, 2, HI) + PIECE[RA], BF),
            pltpu.VMEM((LAYERS, 2, 2, HI) + PIECE[RB], BF),
            pltpu.VMEM((LAYERS, 480, 256), BF),
            pltpu.VMEM((LAYERS, 4, 40, 256), BF),
            pltpu.VMEM((LAYERS, 4) + PIECE[RA], BF),
            pltpu.VMEM((LAYERS, 2) + PIECE[RB], BF),
            pltpu.VMEM((LAYERS, 480, 1280), BF),
            pltpu.VMEM((LAYERS, C, C2), BF),
            pltpu.VMEM((960, 1152), BF),
            pltpu.VMEM((1280, PX), BF),
            pltpu.VMEM((n, C, PX), F32),
            pltpu.VMEM((n, C, PX), F32),
            pltpu.VMEM(photo, BF),
            pltpu.VMEM(photo, BF),
            pltpu.VMEM((n, C, PX), BF),
            pltpu.VMEM((n, C, PX), BF),
            pltpu.VMEM((1120, LAYERS), F32),
            pltpu.SemaphoreType.DMA((60,)),
            pltpu.SemaphoreType.DMA((60,)),
            pltpu.SemaphoreType.DMA((2,)),
            pltpu.SemaphoreType.DMA((32,)),
        ],
        compiler_params=pltpu.CompilerParams(
            vmem_limit_bytes=62 << 20, collective_id=0, has_side_effects=True
        ),
        name="forward_gather",
    )(down_in, right_in, v1, v2, r1, vs, r2, gains, biases)


RG, DA, DB, DC = 0, 1, 2, 3
KINDS = (RG, DA, DB, DC)
ROWS = {RG: 176, DA: 80, DB: 80, DC: 80}
X_FIRST = {RG: True, DA: True, DB: False, DC: False}


def place(kind, k, q):
    core, y = divmod(q, 2)
    hi, lo = divmod(k, 2)
    return (core, lo, y, hi) if X_FIRST[kind] else (core, y, lo, hi)


def put_block(out, kind, k, row, tile):
    tile = jnp.concatenate([tile, jnp.zeros((tile.shape[0], 32), F32)], axis=1).astype(BF)
    for q in range(4):
        out[place(kind, k, q) + (slice(row, row + tile.shape[0]),)] = tile[:, at(q)]


def pack_down(out, kind, acc, width, first):
    for k in range(8):
        parts = []
        for p in range(3):
            tap, chan = divmod(240 * k + 80 * p, C2)
            a, c = divmod(tap, 3)
            lo = c * width + first
            parts.append(acc[a, chan : chan + 80, lo : lo + C])
        put_block(out, kind, k, 0, jnp.concatenate(parts, axis=1))


def pack_right(out, gr2, gr1, gs):
    for k in range(8):
        t, half = divmod(k, 2)
        row = slice(half * C, (half + 1) * C)
        part = jnp.concatenate([gr2[row, t * C2 : (t + 1) * C2], gr1[row, t * C : (t + 1) * C]], axis=1)
        put_block(out, RG, k, 0, part)
        skip = gs[40 * k : 40 * k + 40]
        third = jnp.concatenate([skip[32:], jnp.zeros((8, C), F32)], axis=0)
        put_block(out, RG, k, C, jnp.concatenate([skip[:16], skip[16:32], third], axis=1))


def dot_rows(weight, grad, width, count):
    row = jnp.sum(weight.astype(F32) * grad, axis=0, keepdims=True)
    return sum(row[:, k * width : (k + 1) * width] for k in range(count))


def right_taps(wr, br1, br2):
    for t in range(4):
        rows = wr[t * C2 : (t + 1) * C2, :480]
        br2[:, t * C2 : (t + 1) * C2] = rows[:, :C2]
        br1[:, t * C : (t + 1) * C] = rows[:, C2:]


def down_taps(wd, b1, b2):
    for k in range(8):
        rows = wd[k, :, :240].T
        for p in range(3):
            tap, chan = divmod(240 * k + 80 * p, C2)
            a, c = divmod(tap, 3)
            b2[a, chan : chan + 80, c * C2 : (c + 1) * C2] = rows[80 * p : 80 * p + 80, :C2]
            b1[a, chan : chan + 80, c * C : (c + 1) * C] = rows[80 * p : 80 * p + 80, C2:]


def sum_stage(kind, stage, sems, first, g, bufs, ids):
    me, grp, hi, lo, y, core = ids
    t1, t2, t3, t4, fin = bufs
    to_x = (hi * 2 + 1 - lo, grp)
    to_y = (me, (1 - y) * 2 + core)
    f, s, to_f, to_s = (lo, y, to_x, to_y) if X_FIRST[kind] else (y, lo, to_y, to_x)
    if stage == 0:
        return [send(g.at[1 - core], t1, sems, first, (me, y * 2 + 1 - core))]
    if stage == 1:
        return [send(t1.at[1 - f], t2, sems, first + 1, to_f)]
    if stage == 2:
        return [send(t2.at[1 - s], t3, sems, first + 2, to_s)]
    if stage == 3:
        return [
            send(t3.at[lax.rem(hi + k, HI)], t4.at[k - 1], sems, first + 2 + k, (lax.rem(hi + k, HI) * 2 + lo, grp))
            for k in range(1, HI)
        ]
    mine = fin.at[core, y]
    return [send(mine, mine, sems, first + 2 + HI + k - 1, (me, lax.rem(grp + k, 4))) for k in range(1, 4)]


def sum_adds(kind, stage, g, bufs, ids):
    me, grp, hi, lo, y, core = ids
    t1, t2, t3, t4, fin = bufs
    f, s = (lo, y) if X_FIRST[kind] else (y, lo)
    if stage == 1:
        add_into(t1, g.at[core])
    if stage == 2:
        add_into(t2, t1.at[f])
    if stage == 3:
        add_into(t3, t2.at[s])
    if stage == 4:
        total = t3[hi].astype(F32)
        for k in range(1, HI):
            total = total + t4[k - 1].astype(F32)
        fin[core, y] = total.astype(BF)


def backward_kernel(
    down_cot, right_cot, down_last, right_last, cells, actd, actr, acth, gated, gater, wd_in, wr_in, wk_in,
    mask, kappa, gains, v1, v2, r1, vs, r2,
    down_out, right_out, down_grad, right_grad, o1, o2, or1, os, or2, ogain, obias,
    *scratch,
):
    scratch = list(scratch)

    def take(count):
        out = scratch[:count]
        del scratch[:count]
        return out

    cot_d, cot_r, gdown, gright, gcells, cells_a, cells_b, xd, xr, xh, gtd, gtr, wd, wr, wk = take(15)
    b1, b2, br1, br2, g1, g2, gr1, gr2, gs, bsum = take(10)
    ext, ext1, dhd, photo = take(4)
    packed = {(l, kind): take(1)[0] for l in range(LAYERS) for kind in KINDS}
    bufs = {(l, kind): take(5) for l in range(LAYERS) for kind in KINDS}
    near_rows, far_rows, send_sems, recv_sems, row_send, row_recv, in_sems, out_sems = take(8)
    n = gdown.shape[0]
    last = n - 1
    ids = peers(HI)
    me, grp, hi, lo, y, core = ids
    sems = (send_sems, recv_sems)
    rsems = (row_send, row_recv)
    loads = {}

    def load(name, src, dst):
        loads[name] = pltpu.make_async_copy(src, dst, in_sems.at[len(loads)])
        loads[name].start()

    def need(*names):
        for name in names:
            loads[name].wait()

    def load_right(l):
        load(("wr", l), wr_in.at[l], wr)
        load(("wk", l), wk_in.at[l], wk)
        load(("gtr", l), gater.at[l], gtr)
        load(("xh", l), acth.at[l], xh)
        load(("xr", l), actr.at[l], xr)

    load("cot_r", right_cot, cot_r)
    load("cot_d", down_cot, cot_d)
    load_right(1)
    load("cells2", cells.at[2], cells_a)
    load(("wd", 1), wd_in.at[1], wd)
    load(("gtd", 1), gated.at[1], gtd)
    load(("xd", 1), actd.at[1], xd)
    load("cells1", cells.at[1], cells_b)
    meet(*ids, True)

    def copies(l, kind, stage):
        return sum_stage(kind, stage, sems, (l * 4 + kind) * 9, packed[l, kind], bufs[l, kind], ids)

    def wait(l, kind, stage):
        wait_all(copies(l, kind, stage))

    def start(l, kind, stage):
        sum_adds(kind, stage, packed[l, kind], bufs[l, kind], ids)
        start_all(copies(l, kind, stage))

    def step(l, kind, stage):
        wait(l, kind, stage - 1)
        start(l, kind, stage)

    def steps(*moves):
        def hook():
            for move in moves:
                step(*move)

        return hook

    def run_hooks(i, hooks):
        for k, hook in hooks.items():
            pl.when(i == k)(hook)

    def begin(i, carry):
        for v in range(8):
            m = jnp.concatenate([mask[i, g * 8 + v : g * 8 + v + 1, :] for g in range(4)], axis=1).astype(F32)
            gdown[i, :, at(v)] = load_cells(cot_d.at[i], v) * m
            gright[i, :, at(v)] = load_cells(cot_r.at[i], v) * m
        return carry

    ext4 = ext.at[:, :PX]
    ext41 = ext1.at[:, :PX]
    dskip = dhd.at[0]

    def clear(*accs):
        for acc in accs:
            acc[...] = jnp.zeros(acc.shape, F32)

    def right_part(l, high, hooks):
        def scale(m):
            return kappa[SPANS[m][0] : SPANS[m][1], l : l + 1]

        def body(i, carry):
            total = None
            for v in range(8):
                d = gate_back(
                    gright[i, :, at(v)], gtr[i, :C, at(v)].astype(F32), gtr[i, C:, at(v)].astype(F32)
                )
                total = d if total is None else total + d
                put_right_back(ext4, v, (d * scale(4)).astype(BF))
            bsum[l, SPANS[4][0] : SPANS[4][1], :] += total
            gr2[...] += nt(xh[i], ext4[...])
            total = None
            for j in range(4):
                e = nn(br2[...], ext4[:, j * 256 : j * 256 + 256])
                for h in range(2):
                    v = 2 * j + h
                    d = elu_back(e[:, at(h)], xh[i, :, at(v)])
                    total = d if total is None else total + d
                    put_right_back(ext41, v, (d * scale(2)).astype(BF))
                    dskip[:, at(v)] = (d * scale(3)).astype(BF)
            bsum[l, SPANS[2][0] : SPANS[2][1], :] += total
            bsum[l, SPANS[3][0] : SPANS[3][1], :] += total
            gr1[...] += nt(xr[i], ext41[...])
            gs[...] += nt(high[i], dskip[...])
            for j in range(4):
                e = nn(br1[...], ext41[:, j * 256 : j * 256 + 256])
                k = nn(wk[...], dskip[:, j * 256 : j * 256 + 256])
                for h in range(2):
                    v = 2 * j + h
                    gright[i, :, at(v)] += elu_back(e[:, at(h)], xr[i, :, at(v)])
                    gc = k[:, at(h)]
                    if l + 1 < LAYERS:
                        gc = gc + gcells[i, :, at(v)].astype(F32)
                    gdown[i, :, at(v)] += elu_back(gc, high[i, :, at(v)])
            run_hooks(i, hooks)
            return carry

        lax.fori_loop(0, n, body, 0)

    def down_part(l, hooks):
        def scale(m):
            return kappa[SPANS[m][0] : SPANS[m][1], l : l + 1]

        def body(i, carry):
            total = None
            for v in range(8):
                d = gate_back(
                    gdown[i, :, at(v)], gtd[i, :C, at(v)].astype(F32), gtd[i, C:, at(v)].astype(F32)
                )
                total = d if total is None else total + d
                put_down_back(ext, v, (d * scale(1)).astype(BF))
            bsum[l, SPANS[1][0] : SPANS[1][1], :] += total
            for a in range(2):
                first = 128 * (1 - a)
                g2[a] += nt(xd[i], ext[:960, first : first + PX])
            total = None
            for j in range(4):
                e = nn(b2[1], ext[:960, j * 256 : j * 256 + 256])
                e = e + nn(b2[0], ext[:960, j * 256 + 128 : j * 256 + 384])
                for h in range(2):
                    v = 2 * j + h
                    d = elu_back(e[:, at(h)], xd[i, :, at(v)])
                    total = d if total is None else total + d
                    dhd[i, :, at(v)] = (d * scale(0)).astype(BF)
            bsum[l, SPANS[0][0] : SPANS[0][1], :] += total
            run_hooks(i, hooks)
            return carry

        lax.fori_loop(0, n, body, 0)

    def first_part(low):
        def body(i, carry):
            for v in range(8):
                put_down_back(ext1, v, dhd[i, :, at(v)])
            for a in range(2):
                first = 128 * (1 - a)
                g1[a] += nt(low[i], ext1[:480, first : first + PX])
            return carry

        lax.fori_loop(0, n, body, 0)

    def input_part(l, low, hooks):
        def body(i, carry):
            for v in range(8):
                put_down_back(ext1, v, dhd[i, :, at(v)])
            for j in range(4):
                e = nn(b1[1], ext1[:480, j * 256 : j * 256 + 256])
                e = e + nn(b1[0], ext1[:480, j * 256 + 128 : j * 256 + 384])
                if l > 0:
                    gcells[i, :, j * 256 : j * 256 + 256] = e.astype(BF)
                else:
                    for h in range(2):
                        v = 2 * j + h
                        gdown[i, :, at(v)] += elu_back(e[:, at(h)], low[i, :, at(v)])
            run_hooks(i, hooks)
            return carry

        lax.fori_loop(0, n, body, 0)

    def right_end(l):
        pack_right(packed[l, RG], gr2, gr1, gs)
        start(l, RG, 0)
        near_rows[grp, l : l + 1, SPANS[2][0] : SPANS[4][1]] = jnp.concatenate(
            [
                dot_rows(br1[...], gr1[...], C, 4),
                dot_rows(wk[...], gs[...], C, 1),
                dot_rows(br2[...], gr2[...], C2, 4),
            ],
            axis=1,
        )

    def down_end(l):
        pack_down(packed[l, DA], DA, g2, C2, 0)
        start(l, DA, 0)
        pack_down(packed[l, DB], DB, g2, C2, C)
        start(l, DB, 0)

    def first_end(l):
        pack_down(packed[l, DC], DC, g1, C, 0)
        start(l, DC, 0)
        near_rows[grp, l : l + 1, : SPANS[1][1]] = jnp.concatenate(
            [
                dot_rows(b1[0], g1[0], C, 3) + dot_rows(b1[1], g1[1], C, 3),
                dot_rows(b2[0], g2[0], C2, 3) + dot_rows(b2[1], g2[1], C2, 3),
            ],
            axis=1,
        )
        near_rows[grp, 2 + l : 3 + l, :1120] = jnp.sum(bsum[l].T, axis=0, keepdims=True)

    near_rows[grp] = jnp.zeros((8, 1152), F32)
    clear(bsum, gr1, gr2, gs, g1, g2)
    need("cot_r", "cot_d")
    lax.fori_loop(0, n, begin, 0)
    need(("wr", 1), ("wk", 1))
    right_taps(wr, br1, br2)
    need(("gtr", 1), ("xh", 1), ("xr", 1), "cells2")
    right_part(1, cells_a, {})
    right_end(1)
    load_right(0)
    load("cells0", cells.at[0], cells_a)
    need(("wd", 1))
    down_taps(wd, b1, b2)
    load(("wd", 0), wd_in.at[0], wd)
    need(("gtd", 1), ("xd", 1))
    down_part(1, {0: steps((1, RG, 1))})
    down_end(1)
    load(("gtd", 0), gated.at[0], gtd)
    load(("xd", 0), actd.at[0], xd)
    need("cells1")
    first_part(cells_b)
    first_end(1)
    steps((1, DA, 1), (1, DB, 1), (1, RG, 2))()
    input_part(1, cells_b, {last: steps((1, DC, 1))})
    clear(gr1, gr2, gs, g1, g2)
    need(("wr", 0), ("wk", 0))
    right_taps(wr, br1, br2)
    need(("gtr", 0), ("xh", 0), ("xr", 0))
    right_part(
        0,
        cells_b,
        {
            0: steps((1, DA, 2), (1, DB, 2), (1, RG, 3), (1, DC, 2)),
            1: steps((1, DA, 3), (1, DB, 3), (1, RG, 4)),
            last: steps((1, DC, 3), (1, DA, 4), (1, DB, 4)),
        },
    )
    right_end(0)
    load("down_last", down_last, xr.at[:, pl.ds(0, C)])
    load("right_last", right_last, xr.at[:, pl.ds(C, C)])
    need(("wd", 0))
    down_taps(wd, b1, b2)
    need(("gtd", 0), ("xd", 0))
    down_part(0, {0: steps((0, RG, 1), (1, DC, 4)), last: steps((0, RG, 2))})
    down_end(0)
    need("cells0")
    first_part(cells_a)
    first_end(0)
    mine = near_rows.at[grp]
    near = [send(mine, mine, rsems, k - 1, (me, lax.rem(grp + k, 4))) for k in range(1, 4)]

    def far():
        part = far_rows.at[me]
        return [
            send(part, part, rsems, 2 + k, (lax.rem(me + k, 2 * HI), grp)) for k in range(1, 2 * HI)
        ]

    def far_start():
        wait_all(near)
        far_rows[me] = near_rows[0] + near_rows[1] + near_rows[2] + near_rows[3]
        start_all(far())

    start_all(near)
    steps((0, DA, 1), (0, DB, 1), (0, RG, 3), (0, DC, 1))()
    input_part(0, cells_a, {1: far_start})
    steps((0, DA, 2), (0, DB, 2))()
    leaving = []
    count = [0]

    def leave(src, dst):
        copy = pltpu.make_async_copy(src, dst, out_sems.at[count[0]])
        count[0] += 1
        copy.start()
        leaving.append(copy)

    slots = [None]

    def turn(flow, dst):
        for i in range(n):
            if slots[0] is not None:
                slots[0].wait()
            for v in range(8):
                store_f32(photo.at[0], v, flow[i, :, at(v)])
            leave(photo.at[0], dst.at[i])
            slots[0] = leaving.pop()

    def turn_last(i, carry):
        for v in range(8):
            store_bf16(cot_d.at[i], v, xr[i, :C, at(v)])
            store_bf16(cot_r.at[i], v, xr[i, C:, at(v)])
        return carry

    turn(gdown, down_grad)
    for kind in KINDS:
        wait(1, kind, 4)
    steps((0, RG, 4), (0, DC, 2))()
    need("down_last", "right_last")
    lax.fori_loop(0, n, turn_last, 0)
    leave(cot_d, down_out)
    leave(cot_r, right_out)
    wait_all(far())
    total = far_rows[0]
    for k in range(1, 2 * HI):
        total = total + far_rows[k]
    obias[...] = total[2:4, :1120]
    ogain[...] = total[0:2, :1120] / gains[...]

    def factors(l):
        recip = col_to_row(kappa[:, l : l + 1]) / gains[l : l + 1, :]
        row = recip * recip * total[l : l + 1, :1120]
        return row, row_to_col(row[:, : SPANS[1][1]])

    def write_right(l, row):
        right = quarters(bufs[l, RG][4])
        or1[l] = right[:C, C2:480] - r1[l].astype(F32) * row[:, SPANS[2][0] : SPANS[2][1]]
        tail = right[C:]
        skip = jnp.concatenate([tail[:, :C], tail[:, C:C2], tail[:8, C2:480]], axis=0)
        os[l] = skip - vs[l].astype(F32) * row[:, SPANS[3][0] : SPANS[3][1]]
        or2[l] = right[:C, :C2] - r2[l].astype(F32) * row[:, SPANS[4][0] : SPANS[4][1]]

    def turned(l, kind):
        flat = quarters(bufs[l, kind][4]).T
        return jnp.concatenate([flat[C * p : C * (p + 1)] for p in range(3)], axis=1)

    def write_down(l, kind, col):
        if kind == DC:
            o1[l] = turned(l, kind) - v1[l].astype(F32) * col[:C]
        else:
            first = 0 if kind == DA else C
            part = slice(first, first + C)
            o2[l, part] = turned(l, kind) - v2[l, part].astype(F32) * col[C + first : C2 + first]

    row_1, col_1 = factors(1)
    row_0, col_0 = factors(0)
    steps((0, DA, 3), (0, DB, 3))()
    turn(gright, right_grad)
    steps((0, DC, 3))()
    write_right(1, row_1)
    for kind in (DA, DB, DC):
        write_down(1, kind, col_1)
    wait(0, RG, 4)
    write_right(0, row_0)
    steps((0, DA, 4), (0, DB, 4), (0, DC, 4))()
    for kind in (DA, DB, DC):
        wait(0, kind, 4)
        write_down(0, kind, col_0)
    for copy in leaving + slots:
        copy.wait()


def sum_shape(kind):
    return (2, 2, 2, HI, ROWS[kind], 128)


def run_backward_sums(down_cot, right_cot, down_last, right_last, kept, weights, mask, kappa, gains, v1, v2, r1, vs, r2):
    n = down_cot.shape[0]
    sds = jax.ShapeDtypeStruct
    vmem = pl.BlockSpec(memory_space=pltpu.VMEM)
    hbm = pl.BlockSpec(memory_space=pl.ANY)
    V = pltpu.VMEM
    wide = V((n, C2, PX), BF)
    flow = (n, C, PX)
    scratch = [V((n, 32, 32, C), BF)] * 2 + [V(flow, F32)] * 2 + [wide] * 8
    scratch += [V((8, 480, 256), BF), V((1280, 512), BF), V((C2, C), BF)]
    scratch += [V((2, C2, 480), BF), V((2, C2, 960), BF), V((C2, 640), BF), V((C2, 1280), BF)]
    scratch += [V((2, C2, 480), F32), V((2, C2, 960), F32), V((C2, 640), F32), V((C2, 1280), F32), V((C2, C), F32)]
    scratch += [V((LAYERS, 1120, 128), F32)]
    scratch += [V((1280, 1152), BF), V((640, 1152), BF), V((n, C, PX), BF), V((1, 32, 32, C), F32)]
    scratch += [V(sum_shape(kind), BF) for l in range(LAYERS) for kind in KINDS]
    for l in range(LAYERS):
        for kind in KINDS:
            tail = (ROWS[kind], 128)
            scratch += [
                V((2, 2, HI) + tail, BF),
                V((2, HI) + tail, BF),
                V((HI,) + tail, BF),
                V((HI - 1,) + tail, BF),
                V((2, 2) + tail, BF),
            ]
    sem = pltpu.SemaphoreType.DMA
    scratch += [V((4, 8, 1152), F32), V((2 * HI, 8, 1152), F32), sem((72,)), sem((72,)), sem((10,)), sem((10,)), sem((24,)), sem((2 + 2 * n,))]
    photo = (n, 32, 32, C)
    return pl.pallas_call(
        backward_kernel,
        in_specs=[hbm] * 13 + [vmem] * 8,
        out_specs=[hbm] * 4 + [vmem] * 7,
        out_shape=[sds(photo, BF)] * 2 + [sds(photo, F32)] * 2 + [sds(v.shape, F32) for v in (v1, v2, r1, vs, r2)] + [sds((LAYERS, 1120), F32)] * 2,
        scratch_shapes=scratch,
        compiler_params=pltpu.CompilerParams(
            vmem_limit_bytes=63 << 20, collective_id=1, has_side_effects=True
        ),
        name="backward_sums",
    )(down_cot, right_cot, down_last, right_last, *kept, *weights, mask, kappa, gains, v1, v2, r1, vs, r2)


def write_kernel(*refs):
    half = (len(refs) - 1) // 2
    sems = refs[-1]
    copies = []
    for src, dst in zip(refs[:half], refs[half : 2 * half]):
        for i in range(src.shape[0]):
            copies.append(pltpu.make_async_copy(src.at[i], dst.at[i], sems.at[len(copies)]))
    start_all(copies)
    wait_all(copies)


def run_write(results):
    hbm = pl.BlockSpec(memory_space=pl.ANY)
    count = sum(a.shape[0] for a in results)
    return pl.pallas_call(
        write_kernel,
        in_specs=[hbm] * len(results),
        out_specs=[hbm] * len(results),
        out_shape=[jax.ShapeDtypeStruct(a.shape, a.dtype) for a in results],
        scratch_shapes=[pltpu.SemaphoreType.DMA((count,))],
        compiler_params=pltpu.CompilerParams(vmem_limit_bytes=63 << 20),
        name="write",
    )(*results)


def general_finish(lower, upper, whole_v, shards, gains):
    rows = lax.psum(jnp.stack([lower[4], upper[4]]), ("dp", "grp"))
    sums = []
    units = []
    inverse = []
    for m, (low, high) in enumerate(zip(unpack(*lower[:4]), unpack(*upper[:4]))):
        part = lax.psum_scatter(jnp.stack([low, high]), "dp", scatter_dimension=1, tiled=True)
        sums.append(lax.psum(part, "grp").astype(F32))
        vals = whole_v[m].astype(F32)
        inv = lax.rsqrt(jnp.sum(vals * vals, axis=1))
        inverse.append(inv)
        units.append(shards[m].astype(F32) * inv[:, None, :])
    inverse = jnp.concatenate(inverse, axis=1)
    dots = rows[:, 0] * inverse
    grads = [sums[m] - units[m] * dots[:, None, lo:hi] for m, (lo, hi) in enumerate(SPANS)]
    return (*grads, rows[:, 0] / gains, rows[:, 1])


def on_device(
    quick,
    down_in,
    right_in,
    pixel_mask,
    down_cot,
    right_cot,
    v_down1,
    v_down2,
    v_right1,
    v_skip,
    v_right2,
    gains,
    biases,
):
    shards = (v_down1, v_down2, v_right1, v_skip, v_right2)
    n = down_in.shape[0]
    if quick and n > 2:
        turned = (v_down1.swapaxes(1, 2), v_down2.swapaxes(1, 2), v_right1, v_skip, v_right2)
        down_last, right_last, *rest = run_forward_gather(down_in, right_in, *turned, gains, biases)
        kept, weights, kappa = rest[:6], rest[6:9], rest[9]
        results = run_backward_sums(
            down_cot, right_cot, down_last, right_last, kept, weights, pixel_mask, kappa, gains, *turned
        )
        gain, bias = results[9:]
        down_out, right_out, down_grad, right_grad, *grads = run_write(results[:9])
        grads += [gain, bias]
        grads[0] = grads[0].swapaxes(1, 2)
        grads[1] = grads[1].swapaxes(1, 2)
        return (down_out, right_out, down_grad, right_grad, *grads)
    whole_v = tuple(lax.all_gather(v, "dp", axis=1, tiled=True) for v in shards)
    weights = assemble(*whole_v)
    cols = jnp.concatenate([gains, biases], axis=0).T
    down_out, right_out, *kept, kappa = run_forward(down_in, right_in, *weights, cols)
    mask = pixel_mask.reshape(n, 4, 8, 32).transpose(0, 2, 1, 3).reshape(n, 1, 1024).astype(F32)
    down_g, right_g, cells_g, *upper = run_backward(1, down_cot, right_cot, None, mask, kept, kappa, *weights)
    down_grad, right_grad, *lower = run_backward(0, down_g, right_g, cells_g, mask, kept, kappa, *weights)
    grads = general_finish(lower, upper, whole_v, shards, gains)
    return (down_out, right_out, down_grad, right_grad, *grads)


def solution(mesh):
    photo = P(("dp", "grp"), None, None, None)
    rows = P(None, "dp", None)
    quick = mesh.shape["dp"] == 2 * HI and mesh.shape["grp"] == 4
    return jax.shard_map(
        functools.partial(on_device, quick),
        mesh=mesh,
        in_specs=(photo, photo, P(("dp", "grp"), None, None), photo, photo) + (rows,) * 5 + (P(), P()),
        out_specs=(photo,) * 4 + (rows,) * 5 + (P(), P()),
        check_vma=False,
    )
```
